32 devices in a mesh: box: 4 (over y, core), gz: 8 (over z, x).
Axes of the slice: x: 2, y: 2, z: 4, core: 2. Of those that a mesh axis runs over, the one named last changes fastest.
Arguments:
- coarse_mismatch: float32 [64, 512, 512], P('gz', 'box'), may hold values from -4 to 4, as said below
- fine_div: float32 [64, 128, 256], P('box', 'gz'), may hold values from -12 to 12
- reflux: float32 [64, 128, 128], P('box', 'gz'), may hold values from -12 to 12
- box_list: int32 [64, 3], replicated, may hold values from 0 to 500, as said below
- cf_mask: int32 [64, 4], replicated, may hold values 0 or 1
Outputs:
- sync_phi: float32 [64, 512, 512], P('gz', 'box')
The draws below stay inside these ranges and needn't reach their ends.
Inputs may be any that keep to these rules, and one draw needn't show every extreme that they name: `coarse_mismatch`: the base level's divergence mismatch. `box_list`: column 0 is the owning box group; columns 1 and 2 are 4 more than multiples of 16, with column 1 below 128 and column 2 below 512; patches of one owner never share a position. The 16 patches of one box group (rows of one aligned block) have at most 4 with one owner, and some owner has exactly 4 in every block.
All inputs are finite; a program needn't handle non-finite values.
Results may differ from the reference program's by a relative error of at most 0.0003.
Values sent between devices are 32-bit elements; how exact they have to be, the bound alone decides.
No kernel may reach another device: no remote copies, remote signals or barrier semaphores. Data moves between devices by JAX's collectives and lax.ppermute only.
A program may use at most 320 MiB of HBM per device.

```python
import jax
import jax.numpy as jnp
from jax import lax

CX = 128
NY = 512
PATCH_DEV = 16
LEVELS = 4
CSWEEPS = 16
CAP = 4
NX = 512
NZ = 64
PATCHES = 64
N_BOX = 4


def draw_coarse_mismatch(key, part):
    inner = jax.random.fold_in(key, 3)
    values = jnp.clip(jax.random.normal(inner, (NZ, NX, NY), jnp.float32), -4.0, 4.0)
    return values.astype(jnp.float32)


def draw_box_list(key, part):
    key_hot, key_offset, key_shuffle, key_tiles = jax.random.split(jax.random.fold_in(key, 7), 4)
    hot_owner = jax.random.randint(key_hot, (), 0, N_BOX)
    others = max(N_BOX - 1, 1)
    offsets = jax.random.randint(key_offset, (N_BOX, 1), 0, others)
    offsets = offsets.at[0, 0].set((N_BOX - 1 - hot_owner) % others)
    position = jnp.arange(PATCH_DEV, dtype=jnp.int32)[None, :]
    spread = (hot_owner + 1 + (offsets + position - CAP) % others) % N_BOX
    assigned = jnp.where(position < CAP, hot_owner, spread)
    shuffle = jax.vmap(lambda inner: jax.random.permutation(inner, PATCH_DEV))(jax.random.split(key_shuffle, N_BOX))
    owners = jnp.take_along_axis(assigned, shuffle, axis=1)
    same_owner = owners[:, :, None] == owners[:, None, :]
    earlier = jnp.arange(PATCH_DEV)[:, None] < jnp.arange(PATCH_DEV)[None, :]
    rank_of = jnp.sum((same_owner & earlier[None]).astype(jnp.int32), axis=1)
    slot_index = jnp.arange(N_BOX, dtype=jnp.int32)[:, None] * CAP + rank_of
    tile_count = CX // 16 * (NY // 16)
    tile_perm = jax.vmap(lambda inner: jax.random.permutation(inner, tile_count))(jax.random.split(key_tiles, N_BOX))
    tile_perm = (tile_perm - tile_perm[:, :1] + tile_count - 1) % tile_count
    tile_index = tile_perm[owners, slot_index]
    x_start = 16 * (tile_index // (NY // 16)) + 4
    y_start = 16 * (tile_index % (NY // 16)) + 4
    return jnp.stack([owners, x_start, y_start], axis=-1).reshape(N_BOX * PATCH_DEV, 3).astype(jnp.int32)


def with_ends(values, key, smallest, top_value):
    longest = values.shape.index(max(values.shape))
    spots = []
    for shift in (0, 1):
        where = [jax.random.randint(jax.random.fold_in(key, axis), (), 0, length) for axis, length in enumerate(values.shape)]
        where[longest] = (where[longest] + shift) % values.shape[longest]
        spots.append(tuple(where))
    return values.at[spots[0]].set(smallest).at[spots[1]].set(top_value)


def levels(stream_key, shape, cuts, smallest, largest):
    level, own = 1.0, jax.random.fold_in(stream_key, 6)
    for axis_at, blocks in cuts:
        heights = jnp.exp(jax.random.uniform(jax.random.fold_in(own, axis_at), (blocks,), jnp.float32, smallest / len(cuts), largest / len(cuts)))
        level = level * jnp.repeat(heights, shape[axis_at] // blocks).reshape([-1 if axis == axis_at else 1 for axis in range(len(shape))])
    return level


def scatter_about(stream_key, extent, width, limit, shards=(), kind=jnp.bfloat16):
    result = jax.random.normal(stream_key, extent, jnp.float32) * width
    if len(shards) > 0:
        result = levels(stream_key, extent, shards, -0.22, 0.18) * result
    return jnp.clip(result, min=-limit, max=limit).astype(kind)


def setup_inputs(seed: int = 0) -> dict:
    key_of = jax.random.split(jax.random.key(seed), 6)
    coarse_mismatch = draw_coarse_mismatch(jax.random.fold_in(key_of[5], 71), 0)
    fine_div = scatter_about(key_of[1], (PATCHES, 2 * NZ, 256), 2.0, 12.0, ((0, 4), (1, 8)), jnp.float32)
    reflux = scatter_about(key_of[2], (PATCHES, 2 * NZ, 128), 2.0, 12.0, ((0, 4), (1, 8)), jnp.float32)
    box_list = draw_box_list(jax.random.fold_in(key_of[5], 71), 0)
    cf_mask = with_ends((jax.random.randint(key_of[4], (PATCHES, 4), 0, 4) < 3).astype(jnp.int32), jax.random.fold_in(key_of[4], 1), 0, 1)
    return dict(coarse_mismatch=coarse_mismatch, fine_div=fine_div, reflux=reflux, box_list=box_list, cf_mask=cf_mask)


OMEGA = 0.8


def neighbor_sum(field):
    padded = jnp.pad(field, 1)
    total = padded[2:, 1:-1, 1:-1] + padded[:-2, 1:-1, 1:-1]
    total = total + padded[1:-1, 2:, 1:-1] + padded[1:-1, :-2, 1:-1]
    return total + padded[1:-1, 1:-1, 2:] + padded[1:-1, 1:-1, :-2]


def jacobi_sweep(field, scaled, around):
    return field + OMEGA * (scaled - (6.0 * field - around)) / 6.0


def restrict(field):
    z_cells, x_cells, y_cells = field.shape
    return field.reshape(z_cells // 2, 2, x_cells // 2, 2, y_cells // 2, 2).sum(axis=(1, 3, 5)) * 0.125


def prolong(field):
    return jnp.repeat(jnp.repeat(jnp.repeat(field, 2, axis=0), 2, axis=1), 2, axis=2)


def vcycle(source, grid_level):
    scaling = float(4 ** grid_level)
    scaled = source * scaling
    field = OMEGA * scaled / 6.0
    if grid_level == LEVELS - 1:
        return lax.fori_loop(0, CSWEEPS - 1, lambda step_index, field_now: jacobi_sweep(field_now, scaled, neighbor_sum(field_now)), field)
    field = jacobi_sweep(field, scaled, neighbor_sum(field))
    residue = source - (6.0 * field - neighbor_sum(field)) / scaling
    field = field + prolong(vcycle(restrict(residue), grid_level + 1))
    field = jacobi_sweep(field, scaled, neighbor_sum(field))
    return jacobi_sweep(field, scaled, neighbor_sum(field))


def average_fine(fine):
    patch_count, fine_z, _ = fine.shape
    return fine.reshape(patch_count, fine_z // 2, 2, 8, 2, 8, 2).sum(axis=(2, 4, 6)) * 0.125


def average_flux(fluxes):
    patch_count, fine_z, _ = fluxes.shape
    return fluxes.reshape(patch_count, fine_z // 2, 2, 2, 4, 8, 2).sum(axis=(2, 3, 6)) * 0.125


def reference(coarse_mismatch, fine_div, reflux, box_list, cf_mask):
    averaged = average_fine(fine_div)
    face_flux = average_flux(reflux) * cf_mask.astype(jnp.float32)[:, None, :, None]
    zero_index = jnp.zeros((), jnp.int32)

    def place(patch, field):
        x_start = (box_list[patch, 0] * CX + box_list[patch, 1]).astype(jnp.int32)
        y_start = box_list[patch, 2].astype(jnp.int32)
        block = lax.dynamic_index_in_dim(averaged, patch, 0, keepdims=False)
        flux_here = lax.dynamic_index_in_dim(face_flux, patch, 0, keepdims=False)
        field = lax.dynamic_update_slice(field, block, (zero_index, x_start, y_start))
        sides = ((flux_here[:, 0, :][:, None, :], x_start - 1, y_start),
                 (flux_here[:, 1, :][:, None, :], x_start + 8, y_start),
                 (flux_here[:, 2, :][:, :, None], x_start, y_start - 1),
                 (flux_here[:, 3, :][:, :, None], x_start, y_start + 8))
        for values, row_start, column in sides:
            corner = (zero_index, row_start.astype(jnp.int32), column.astype(jnp.int32))
            current = lax.dynamic_slice(field, corner, values.shape)
            field = lax.dynamic_update_slice(field, current + values, corner)
        return field

    right_side = lax.fori_loop(0, PATCHES, place, coarse_mismatch)
    return vcycle(right_side, 0)
```

```python
import functools

import jax
import jax.numpy as jnp
from jax import lax
from jax.experimental import pallas as pl
from jax.experimental.pallas import tpu as pltpu
from jax.sharding import PartitionSpec as P

CSWEEPS = 16
OMEGA = 0.8
C = OMEGA / 6.0
HX = 32
HU = 8
LANES = 128
F32 = jnp.float32
BF16 = jnp.bfloat16
I32 = jnp.int32

VM = pl.BlockSpec(memory_space=pltpu.VMEM)
SM = pl.BlockSpec(memory_space=pltpu.SMEM)
ANY = pl.BlockSpec(memory_space=pl.ANY)
PARAMS = pltpu.CompilerParams(vmem_limit_bytes=56 << 20)


def iota(shape, dim):
    return lax.broadcasted_iota(I32, shape, dim)


def as_matrix(condition):
    return condition.astype(F32).astype(BF16)


def pair_matrix(length):
    shape = (length, length // 2)
    return as_matrix((iota(shape, 0) >> 1) == iota(shape, 1))


def copy_matrix(length):
    shape = (length, 2 * length)
    return as_matrix(iota(shape, 0) == (iota(shape, 1) >> 1))


def select_dot(values, matrix):
    high = values.astype(BF16)
    low = (values - high.astype(F32)).astype(BF16)
    return jnp.dot(high, matrix, preferred_element_type=F32) + jnp.dot(
        low, matrix, preferred_element_type=F32
    )


def each(count, body, unroll=1):
    def step(index, carry):
        body(index)
        return carry

    lax.fori_loop(0, count, step, 0, unroll=unroll)


def beside_lanes(blocks):
    lane = iota(blocks[0].shape, 1)
    right = [pltpu.roll(block, 1, 1) for block in blocks]
    left = [pltpu.roll(block, LANES - 1, 1) for block in blocks]
    sums = []
    for b in range(len(blocks)):
        before = right[b - 1] if b > 0 else 0.0
        after = left[b + 1] if b + 1 < len(blocks) else 0.0
        sums.append(
            jnp.where(lane == 0, before, right[b]) + jnp.where(lane == LANES - 1, after, left[b])
        )
    return sums


def around(field, plane, row, rows):
    count = field.shape[1]

    def at(p, first):
        return [field[p, b, first : first + rows, :] for b in range(count)]

    middle = at(plane, row + 8)
    parts = zip(
        at(plane, row + 7), at(plane, row + 9), beside_lanes(middle), at(plane - 1, row + 8), at(plane + 1, row + 8)
    )
    return middle, [(a + b) + (c + (d + e)) for a, b, c, d, e in parts]


class Edges:
    def __init__(self, boxes, slabs):
        self.box, self.slab = lax.axis_index("box"), lax.axis_index("gz")
        self.boxes, self.slabs = boxes, slabs

    def planes(self, plane, count):
        outside = ((plane < 0) & (self.slab == 0)) | ((plane >= count) & (self.slab == self.slabs - 1))
        return jnp.where(outside, 0.0, 1.0).astype(F32)

    def low(self):
        return jnp.where(self.box == 0, 0.0, 1.0).astype(F32)

    def high(self):
        return jnp.where(self.box == self.boxes - 1, 0.0, 1.0).astype(F32)


def chunks_of(rows, halo, chunk, cut=0):
    out = [] if cut else [(0, halo, -1)]
    inner = (halo, rows - halo)
    for first in range(inner[0], inner[1], chunk):
        out.append((first, min(chunk, inner[1] - first), 0))
    return out if cut else out + [(rows - halo, halo, 1)]


def scale_of(side, edges, plane_scale):
    if side == 0:
        return plane_scale
    row_scale = edges.low() if side < 0 else edges.high()
    return row_scale if plane_scale is None else row_scale * plane_scale


def relax(new, noff, planes, source, soff, rows, halo, edges, count, old=None, ooff=0, extra=None, chunk=16, shift=8, cut=0):
    def body(index):
        plane_scale = None if count is None else edges.planes(index + planes[0], count)
        for first, size, side in chunks_of(rows, halo, chunk, cut):
            scale = scale_of(side, edges, plane_scale)
            if old is None:
                middle, near = around(source, index + (planes[0] + soff), first, size)
                values = [(1.2 * C) * m + (C * C) * n for m, n in zip(middle, near)]
                if extra is not None:
                    values = [v + extra(index, b, first, size) for b, v in enumerate(values)]
            else:
                middle, near = around(old, index + (planes[0] + ooff), first, size)
                at = index + (planes[0] + soff)
                values = [
                    (1.0 - OMEGA) * m + C * (source[at, b, first + 8 : first + 8 + size, :] + n)
                    for b, (m, n) in enumerate(zip(middle, near))
                ]
            for b, value in enumerate(values):
                if scale is not None:
                    value = value * scale
                new[index + (planes[0] + noff), b, first + shift : first + shift + size, :] = value

    each(planes[1] - planes[0], body)


def restrict(source, soff, v, voff, pairs, rows, store, chunk=16):
    count = v.shape[1]
    width = min(2, count)
    half = rows // 2

    def body(index):
        low_v, low_s = 2 * index + (2 * pairs[0] + voff), 2 * index + (2 * pairs[0] + soff)
        matrix = pair_matrix(width * LANES)
        for first in range(0, half, chunk):
            size = min(chunk, half - first)

            def at(field, plane, b, offset):
                return field[plane, b, pl.ds(8 + 2 * first + offset, size, stride=2), :]

            whole = [
                (at(v, low_v, b, 0) + at(v, low_v, b, 1)) + (at(v, low_v + 1, b, 0) + at(v, low_v + 1, b, 1))
                for b in range(count)
            ]
            near = beside_lanes(whole)
            sums = []
            for b in range(count):
                total = near[b] - 4.0 * whole[b]
                total = total + (at(source, low_s, b, 0) + at(source, low_s, b, 1))
                total = total + (at(source, low_s + 1, b, 0) + at(source, low_s + 1, b, 1))
                total = total + (at(v, low_v - 1, b, 0) + at(v, low_v - 1, b, 1))
                total = total + (at(v, low_v + 2, b, 0) + at(v, low_v + 2, b, 1))
                total = total + (at(v, low_v, b, -1) + at(v, low_v + 1, b, -1))
                total = total + (at(v, low_v, b, 2) + at(v, low_v + 1, b, 2))
                sums.append(total)
            for group in range(count // width):
                piece = sums[width * group]
                if width == 2:
                    piece = jnp.concatenate([piece, sums[2 * group + 1]], axis=1)
                store(index, group, first, size, 0.5 * select_dot(piece, matrix))

    each(pairs[1] - pairs[0], body)


def zero(ref, planes):
    for plane in planes:
        ref[plane] = jnp.zeros(ref.shape[1:], F32)


def zero_rims(ref, planes=None):
    rows = ref.shape[2]
    for plane in range(ref.shape[0]) if planes is None else planes:
        for b in range(ref.shape[1]):
            ref[plane, b, 0:8, :] = jnp.zeros((8, LANES), F32)
            ref[plane, b, rows - 8 : rows, :] = jnp.zeros((8, LANES), F32)


def block_copies(wide, tiled, planes, first, rows, sem, back=False):
    copies = []
    for b in range(tiled.shape[1]):
        pair = (
            wide.at[:, :, pl.ds(LANES * b, LANES)],
            tiled.at[pl.ds(planes[0], planes[1]), b, pl.ds(first, rows), :],
        )
        copies.append(pltpu.make_async_copy(*(pair[::-1] if back else pair), sem))
    return copies


def pack_kernel(mask, fine, flux, out, fine_s, flux_s, sem):
    patches, fine_z = fine.shape[0], fine.shape[1]
    n0 = fine_z // 2
    blocks = fine_s.shape[0]
    copies = [
        pltpu.make_async_copy(fine.at[:, :, pl.ds(LANES * b, LANES)], fine_s.at[b], sem.at[b])
        for b in range(blocks)
    ]
    copies.append(pltpu.make_async_copy(flux, flux_s, sem.at[blocks]))
    for copy in copies:
        copy.start()
    base = lax.axis_index("box") * patches
    side = (iota((n0, LANES), 1) >> 4) & 3
    source, target = iota((LANES, LANES), 0), iota((LANES, LANES), 1)
    s, i = (source >> 4) & 3, (source & 15) >> 1
    goal = jnp.where(
        s == 0, i + 91, jnp.where(s == 1, i + 1, jnp.where(s == 2, 80 - 10 * i, 89 - 10 * i))
    )
    matrices = [as_matrix(goal == target)]
    for b in range(blocks):
        place = source + LANES * b
        goal = 10 * (8 - (place >> 5)) + ((place & 15) >> 1) + 1
        matrices.append(as_matrix(goal == target))
    for copy in copies:
        copy.wait()
    masked, fine_rows = [], [[] for _ in range(blocks)]
    for patch in range(patches):
        m = [mask[s, base + patch].astype(F32) for s in range(4)]
        factor = jnp.where(side == 0, m[0], jnp.where(side == 1, m[1], jnp.where(side == 2, m[2], m[3])))
        masked.append(
            (flux_s[patch, pl.ds(0, n0, stride=2), :] + flux_s[patch, pl.ds(1, n0, stride=2), :]) * factor
        )
        for b in range(blocks):
            fine_rows[b].append(
                fine_s[b, patch, pl.ds(0, n0, stride=2), :] + fine_s[b, patch, pl.ds(1, n0, stride=2), :]
            )
    total = select_dot(jnp.concatenate(masked, axis=0), matrices[0])
    for b in range(blocks):
        total = total + select_dot(jnp.concatenate(fine_rows[b], axis=0), matrices[b + 1])
    out[...] = 0.125 * total


def down_kernel(
    boxes, slabs, n0, x0,
    box_list, coarse, x_low, x_high, packed,
    f_own, z_top, z_bot, c1, c2, up, down,
    fb, vb, g1, v1, sem, out_sem,
):
    edges = Edges(boxes, slabs)
    rows0, rows1, rows2 = x0 + 2 * HX, x0 // 2 + HX, x0 // 4 + HX // 2
    n1, n2 = n0 // 2, n0 // 4
    copies = (
        block_copies(x_low, fb, (2, n0), 8, HX, sem.at[0])
        + block_copies(coarse, fb, (2, n0), 8 + HX, x0, sem.at[1])
        + block_copies(x_high, fb, (2, n0), 8 + HX + x0, HX, sem.at[2])
    )
    for copy in copies:
        copy.start()
    zero(fb, (0, 1, n0 + 2, n0 + 3))
    zero_rims(fb, range(2, n0 + 2))
    zero(vb, (0, 1, n0 + 4, n0 + 5))
    zero_rims(vb, range(2, n0 + 4))
    zero(g1, (0, 1, 2, n1 + 5, n1 + 6, n1 + 7))
    zero_rims(g1, range(3, n1 + 5))
    zero(v1, (0, 1, 2, n1 + 7, n1 + 8, n1 + 9))
    zero_rims(v1, range(3, n1 + 7))
    for copy in copies:
        copy.wait()

    lane = iota((16, LANES), 1)
    tile_row = iota((16, LANES), 0)
    ring_row = (tile_row >= 3) & (tile_row < 13)
    core_row = (tile_row >= 4) & (tile_row < 12)

    def place(patch):
        start = (box_list[0, patch] - edges.box) * x0 + box_list[1, patch] - 4 + HX

        @pl.when((start >= 0) & (start < rows0))
        def _():
            row = pl.multiple_of(start + 8, 8)
            column = box_list[2, patch] - 4
            block, offset = column >> 7, column & 127
            across = lane - offset
            ring = ring_row & (across >= 3) & (across < 13)
            core = core_row & (across >= 4) & (across < 12)
            for z in range(n0):
                values = jnp.broadcast_to(packed[pl.ds(patch * n0 + z, 1), :], (8, LANES))
                values = pltpu.roll(values, 0, 1, stride=10, stride_axis=0)
                tile = jnp.concatenate(
                    [
                        pltpu.roll(values, (offset + 11) & 127, 1),
                        pltpu.roll(values, (offset + 91) & 127, 1),
                    ],
                    axis=0,
                )
                now = fb[2 + z, block, pl.ds(row, 16), :]
                fb[2 + z, block, pl.ds(row, 16), :] = jnp.where(core, 0.0, now) + jnp.where(ring, tile, 0.0)

    each(box_list.shape[1], place)

    inner = pl.ds(8 + HX - HU, x0 + 2 * HU)
    outs = [
        pltpu.make_async_copy(fb.at[pl.ds(2, n0), :, inner, :], f_own, out_sem.at[0]),
        pltpu.make_async_copy(fb.at[pl.ds(n0 - 1, 3), :, inner, :], z_top, out_sem.at[1]),
        pltpu.make_async_copy(fb.at[pl.ds(2, 3), :, inner, :], z_bot, out_sem.at[2]),
    ]
    for copy in outs:
        copy.start()

    relax(vb, 3, (-1, n0 + 1), fb, 2, rows0, HX, edges, n0)

    h1 = HX // 2

    def store1(index, group, first, size, value):
        scale = edges.planes(index - 1, n1)
        if first < h1:
            scale = scale * edges.low()
        if first >= rows1 - h1:
            scale = scale * edges.high()
        g1[index + 3, group, 8 + first : 8 + first + size, :] = value * scale

    restrict(fb, 2, vb, 3, (-1, n1 + 1), rows0, store1)
    for plane in range(n1 + 2):
        for b in range(g1.shape[1]):
            c1[plane, b] = g1[plane + 3, b, 8 + h1 - HU : 8 + rows1 - h1 + HU, :]

    relax(v1, 5, (-2, n1 + 2), g1, 4, rows1, h1, edges, n1)

    h2 = HX // 4

    def store2(index, group, first, size, value):
        if first < h2:
            value = value * edges.low()
        if first >= rows2 - h2:
            value = value * edges.high()
        c2[index, group, first : first + size, :] = value

    restrict(g1, 4, v1, 5, (-2, n2 + 2), rows1, store2, chunk=8)

    r1 = c1.shape[2]
    for target, fine_plane, coarse_first in ((up, n1 + 1, n2 + 2), (down, 0, 0)):
        target[0:rows2] = c2[coarse_first, 0]
        target[rows2 : 2 * rows2] = c2[coarse_first + 1, 0]
        for b in range(c1.shape[1]):
            first = 2 * rows2 + b * r1
            target[first : first + r1] = c1[fine_plane, b]
    for copy in outs:
        copy.wait()


def join_kernel(c1, c2, below, above, s1, copies):
    n1, n2 = s1.shape[0], c2.shape[0] - 4
    rows2, r1 = c2.shape[2], c1.shape[2]
    for plane in range(n2):
        value = c2[2 + plane, 0]
        if plane < 2:
            value = value + below[plane * rows2 : (plane + 1) * rows2]
        if plane >= n2 - 2:
            first = (plane - (n2 - 2)) * rows2
            value = value + above[first : first + rows2]
        for slab in range(copies.shape[0]):
            copies[slab, plane * rows2 : (plane + 1) * rows2] = value
    for plane in range(n1):
        s1[plane] = c1[1 + plane]
    for b in range(s1.shape[1]):
        first = 2 * rows2 + b * r1
        s1[0, b] = s1[0, b] + below[first : first + r1]
        s1[n1 - 1, b] = s1[n1 - 1, b] + above[first : first + r1]


def third_kernel(boxes, slabs, s2, s3, fb, vb):
    edges = Edges(boxes, slabs)
    planes, rows = s2.shape[0], s2.shape[1]
    zero(fb, (0, planes + 1))
    zero(vb, (0, planes + 1))
    zero_rims(fb, range(1, planes + 1))
    zero_rims(vb, range(1, planes + 1))
    for plane in range(planes):
        fb[plane + 1, 0, 8 : 8 + rows, :] = s2[plane]
    relax(vb, 1, (0, planes), fb, 1, rows, HX // 4, edges, None, chunk=32)
    quarter = planes // 4
    h3 = HX // 8
    own = rows // 2 - 2 * h3
    lanes = LANES // 2

    for part in range(2):

        def store(index, group, first, size, value, part=part):
            s3[index, :, lanes * part : lanes * (part + 1)] = value[h3 : h3 + own]

        restrict(
            fb, 1, vb, 1, (quarter * part, quarter * (part + 1)), rows, store, chunk=rows // 2
        )


def coarse_kernel(
    boxes, slabs,
    s3, s2, s1, s1_below, s1_above,
    e1,
    sc, va3, vb3, e3p, f2, v2a, v2b, e2p, f1, v1a, v1b,
):
    edges = Edges(boxes, slabs)
    slab = edges.slab
    half, rows3 = sc.shape[0], sc.shape[2] - 16
    own3 = s3.shape[2]
    zero_rims(va3)
    zero_rims(vb3)
    for box in range(boxes):
        for plane in range(half):
            value = s3[box, plane]
            sc[plane, 0, 8 + box * own3 : 8 + (box + 1) * own3, :] = value
            va3[plane, 0, 8 + box * own3 : 8 + (box + 1) * own3, :] = C * value

    def coarsest(old, new):
        chunk = 16
        lane = iota((chunk, LANES), 1)
        for row in range(0, rows3, chunk):
            inner = slice(row + 8, row + 8 + chunk)
            for plane in range(half):
                middle = old[plane, 0, inner, :]
                before = jnp.where((lane & 63) == 0, 0.0, pltpu.roll(middle, 1, 1))
                after = jnp.where((lane & 63) == 63, 0.0, pltpu.roll(middle, LANES - 1, 1))
                if plane > 0:
                    lower = old[plane - 1, 0, inner, :]
                else:
                    lower = jnp.where(lane < 64, 0.0, pltpu.roll(old[half - 1, 0, inner, :], 64, 1))
                if plane < half - 1:
                    upper = old[plane + 1, 0, inner, :]
                else:
                    upper = jnp.where(lane < 64, pltpu.roll(old[0, 0, inner, :], 64, 1), 0.0)
                beside = old[plane, 0, row + 7 : row + 7 + chunk, :] + old[plane, 0, row + 9 : row + 9 + chunk, :]
                near = beside + ((before + after) + (lower + upper))
                new[plane, 0, inner, :] = (1.0 - OMEGA) * middle + C * (sc[plane, 0, inner, :] + near)

    def double(index):
        coarsest(va3, vb3)
        coarsest(vb3, va3)

    each((CSWEEPS - 1) // 2, double)
    coarsest(va3, vb3)

    n2, rows2 = s2.shape[0] // slabs, s2.shape[1]
    n3 = n2 // 2
    shape = (LANES, LANES)
    copy_low = (iota(shape, 0) == (iota(shape, 1) >> 1)).astype(F32)
    copy_high = (iota(shape, 0) == (iota(shape, 1) >> 1) + 64).astype(F32)
    total3 = 2 * half
    h3 = HX // 8
    window = pl.multiple_of(edges.box * own3, 8)
    for k in range(-2, n3 + 2):
        plane = slab * n3 + k
        inside = (plane >= 0) & (plane < total3)
        safe = jnp.clip(plane, 0, total3 - 1)
        upper = safe >= half
        matrix = jnp.where(upper, copy_high, copy_low) * jnp.where(inside, 1.0, 0.0)
        value = vb3[jnp.where(upper, safe - half, safe), 0, pl.ds(window, own3 + 16), :]
        value = select_dot(value, matrix.astype(BF16))[8 - h3 : 8 + own3 + h3]
        e3p[k + 2, pl.ds(0, own3 + 2 * h3, stride=2), :] = value
        e3p[k + 2, pl.ds(1, own3 + 2 * h3, stride=2), :] = value

    zero_rims(f2)
    zero_rims(v2a)
    zero_rims(v2b)
    planes2 = s2.shape[0]
    for p in range(-5, n2 + 5):
        plane = slab * n2 + p
        inside = jnp.where((plane >= 0) & (plane < planes2), 1.0, 0.0)
        f2[p + 5, 0, 8 : 8 + rows2, :] = s2[jnp.clip(plane, 0, planes2 - 1)] * inside

    def extra2(index, b, first, size):
        return e3p[index >> 1, first : first + size, :]

    h2 = HX // 4
    relax(v2a, 5, (-4, n2 + 4), f2, 5, rows2, h2, edges, n2, extra=extra2, chunk=32)
    relax(v2b, 5, (-3, n2 + 3), f2, 5, rows2, h2, edges, n2, old=v2a, ooff=5, chunk=32)
    relax(v2a, 5, (-2, n2 + 2), f2, 5, rows2, h2, edges, n2, old=v2b, ooff=5, chunk=32)

    n1, rows1 = s1.shape[0], s1.shape[2]
    cut = h2 - HU // 2
    matrix2 = copy_matrix(LANES)
    for k in range(-2, n2 + 2):
        value = select_dot(v2a[k + 5, 0, 8 + cut : 8 + rows2 - cut, :], matrix2)
        for b in range(2):
            part = value[:, LANES * b : LANES * (b + 1)]
            e2p[k + 2, b, pl.ds(0, rows2 - 2 * cut, stride=2), :] = part
            e2p[k + 2, b, pl.ds(1, rows2 - 2 * cut, stride=2), :] = part
    zero_rims(f1)
    zero_rims(v1a)
    zero_rims(v1b)
    for b in range(f1.shape[1]):
        for p in range(4):
            f1[p, b, 8 : 8 + rows1, :] = s1_below[n1 - 4 + p, b]
            f1[4 + n1 + p, b, 8 : 8 + rows1, :] = s1_above[p, b]
        for p in range(n1):
            f1[4 + p, b, 8 : 8 + rows1, :] = s1[p, b]

    def extra1(index, b, first, size):
        return e2p[(index + 1) >> 1, b, first : first + size, :]

    relax(v1a, 4, (-3, n1 + 3), f1, 4, rows1, HU, edges, n1, extra=extra1)
    relax(v1b, 4, (-2, n1 + 2), f1, 4, rows1, HU, edges, n1, old=v1a, ooff=4)
    relax(e1, 1, (-1, n1 + 1), f1, 4, rows1, HU, edges, n1, old=v1b, ooff=4, shift=0)


def finish_kernel(
    boxes, slabs, n0, x0,
    e1, f_own, z_below, z_above,
    out,
    fb, va, vb, ep, ob, sem, out_sem,
):
    edges = Edges(boxes, slabs)
    rows = x0 + 2 * HU
    copies = [
        pltpu.make_async_copy(z_below, fb.at[pl.ds(0, 3), :, pl.ds(8, rows), :], sem.at[0]),
        pltpu.make_async_copy(f_own, fb.at[pl.ds(3, n0), :, pl.ds(8, rows), :], sem.at[1]),
        pltpu.make_async_copy(z_above, fb.at[pl.ds(3 + n0, 3), :, pl.ds(8, rows), :], sem.at[2]),
    ]
    for copy in copies:
        copy.start()
    zero_rims(fb)
    zero_rims(va)
    zero_rims(vb)
    matrix = copy_matrix(LANES)
    cut = HU // 2
    r1 = e1.shape[2]
    size1 = r1 - 2 * cut

    def prolong(k):
        for group in range(e1.shape[1]):
            value = select_dot(e1[k, group, cut : r1 - cut, :], matrix)
            for b in range(2):
                part = value[:, LANES * b : LANES * (b + 1)]
                ep[k, 2 * group + b, pl.ds(0, size1, stride=2), :] = part
                ep[k, 2 * group + b, pl.ds(1, size1, stride=2), :] = part

    each(e1.shape[0], prolong)
    for copy in copies:
        copy.wait()

    def extra(index, b, first, size):
        return ep[index >> 1, b, first : first + size, :]

    relax(va, 3, (-2, n0 + 2), fb, 3, rows, HU, edges, n0, extra=extra)
    relax(vb, 3, (-1, n0 + 1), fb, 3, rows, HU, edges, n0, old=va, ooff=3)

    def last(z):
        view = ob.at[pl.ds(z, 1)]
        relax(view, 0, (0, 1), fb.at[pl.ds(z + 3, 1)], 0, rows, HU, edges, None, old=vb.at[pl.ds(z + 2, 3)], ooff=1, shift=-HU, cut=1)
        for copy in block_copies(out.at[pl.ds(z, 1)], ob, (z, 1), 0, x0, out_sem, back=True):
            copy.start()

    each(n0, last)
    for copy in block_copies(out, ob, (0, n0), 0, x0, out_sem, back=True):
        copy.wait()


def shape_of(*dims):
    return jax.ShapeDtypeStruct(dims, F32)


def scratch(*dims):
    return pltpu.VMEM(dims, F32)


def cost(flops, moved):
    return pl.CostEstimate(flops=flops, bytes_accessed=moved, transcendentals=0)


def shift_by(array, axis, step):
    size = lax.axis_size(axis)
    pairs = [(i, i + step) for i in range(size) if 0 <= i + step < size]
    return lax.ppermute(array, axis, pairs)


def per_device(coarse, fine_div, reflux, box_list, cf_mask):
    boxes, slabs = lax.axis_size("box"), lax.axis_size("gz")
    n0, x0, y0 = coarse.shape
    n1, n2 = n0 // 2, n0 // 4
    b0, b1 = y0 // LANES, y0 // LANES // 2
    patches, fine_z, fine_lanes = fine_div.shape
    rows0, rows1, rows2 = x0 + 2 * HX, x0 // 2 + HX, x0 // 4 + HX // 2
    up_rows0, up_rows1 = x0 + 2 * HU, x0 // 2 + 2 * HU
    dma = pltpu.SemaphoreType.DMA

    x_low = shift_by(coarse[:, x0 - HX :], "box", 1)
    x_high = shift_by(coarse[:, :HX], "box", -1)

    fine_blocks = fine_lanes // LANES
    packed = pl.pallas_call(
        pack_kernel,
        name="pack",
        out_shape=shape_of(patches * n0, LANES),
        in_specs=[SM, ANY, ANY],
        out_specs=VM,
        scratch_shapes=[
            scratch(fine_blocks, patches, fine_z, LANES),
            scratch(patches, fine_z, LANES),
            dma((fine_blocks + 1,)),
        ],
        compiler_params=PARAMS,
        cost_estimate=cost(10**7, 10**6),
    )(cf_mask.T, fine_div, reflux)
    packed = lax.all_gather(packed, "box", axis=0, tiled=True)

    message = 2 * rows2 + b1 * up_rows1
    f_own, z_top, z_bot, c1, c2, up, down = pl.pallas_call(
        functools.partial(down_kernel, boxes, slabs, n0, x0),
        name="down",
        out_shape=(
            shape_of(n0, b0, up_rows0, LANES),
            shape_of(3, b0, up_rows0, LANES),
            shape_of(3, b0, up_rows0, LANES),
            shape_of(n1 + 2, b1, up_rows1, LANES),
            shape_of(n2 + 4, 1, rows2, LANES),
            shape_of(message, LANES),
            shape_of(message, LANES),
        ),
        in_specs=[SM, ANY, ANY, ANY, VM],
        out_specs=(ANY,) * 3 + (VM,) * 4,
        scratch_shapes=[
            scratch(n0 + 4, b0, rows0 + 16, LANES),
            scratch(n0 + 6, b0, rows0 + 16, LANES),
            scratch(n1 + 8, b1, rows1 + 16, LANES),
            scratch(n1 + 10, b1, rows1 + 16, LANES),
            dma((3,)),
            dma((3,)),
        ],
        compiler_params=PARAMS,
        cost_estimate=cost(3 * 10**7, 10**7),
    )(box_list.T, coarse, x_low, x_high, packed)

    from_below = shift_by(up, "gz", 1)
    from_above = shift_by(down, "gz", -1)
    s1, copies = pl.pallas_call(
        join_kernel,
        name="join",
        out_shape=(shape_of(n1, b1, up_rows1, LANES), shape_of(slabs, n2 * rows2, LANES)),
        in_specs=[VM] * 4,
        out_specs=(VM, VM),
        compiler_params=PARAMS,
        cost_estimate=cost(10**6, 10**6),
    )(c1, c2, from_below, from_above)
    s2 = lax.all_to_all(copies, "gz", split_axis=0, concat_axis=0, tiled=True)
    s2 = s2.reshape(slabs * n2, rows2, LANES)
    s1_below = shift_by(s1, "gz", 1)
    s1_above = shift_by(s1, "gz", -1)
    z_below = shift_by(z_top, "gz", 1)
    z_above = shift_by(z_bot, "gz", -1)

    planes2, half = slabs * n2, slabs * n2 // 4
    own3 = x0 // 8
    s3 = pl.pallas_call(
        functools.partial(third_kernel, boxes, slabs),
        name="third",
        out_shape=shape_of(half, own3, LANES),
        in_specs=[VM],
        out_specs=VM,
        scratch_shapes=[scratch(planes2 + 2, 1, rows2 + 16, LANES)] * 2,
        compiler_params=PARAMS,
        cost_estimate=cost(10**6, 10**6),
    )(s2)
    s3 = lax.all_gather(s3, "box", axis=0)
    rows3 = boxes * own3
    e1 = pl.pallas_call(
        functools.partial(coarse_kernel, boxes, slabs),
        name="coarse",
        out_shape=shape_of(n1 + 2, b1, up_rows1, LANES),
        in_specs=[VM] * 5,
        out_specs=VM,
        scratch_shapes=[scratch(half, 1, rows3 + 16, LANES)] * 3
        + [scratch(n2 // 2 + 4, rows2, LANES)]
        + [scratch(n2 + 10, 1, rows2 + 16, LANES)] * 3
        + [scratch(n2 + 4, 2, up_rows1, LANES)]
        + [scratch(n1 + 8, b1, up_rows1 + 16, LANES)] * 3,
        compiler_params=PARAMS,
        cost_estimate=cost(10**7, 4 * 10**6),
    )(s3, s2, s1, s1_below, s1_above)

    return pl.pallas_call(
        functools.partial(finish_kernel, boxes, slabs, n0, x0),
        name="finish",
        out_shape=shape_of(n0, x0, y0),
        in_specs=[VM, ANY, ANY, ANY],
        out_specs=ANY,
        scratch_shapes=[scratch(n0 + 6, b0, up_rows0 + 16, LANES)] * 3
        + [
            scratch(n1 + 2, b0, up_rows0, LANES),
            scratch(n0, b0, x0, LANES),
            dma((3,)),
            dma(()),
        ],
        compiler_params=PARAMS,
        cost_estimate=cost(3 * 10**7, 10**7),
    )(e1, f_own, z_below, z_above)


def solution(mesh):
    return jax.shard_map(
        per_device,
        mesh=mesh,
        in_specs=(P("gz", "box", None), P("box", "gz", None), P("box", "gz", None), P(), P()),
        out_specs=P("gz", "box", None),
        check_vma=False,
    )
```

```python
import functools

import jax
import jax.numpy as jnp
from jax import lax
from jax.experimental import pallas as pl
from jax.experimental.pallas import tpu as pltpu
from jax.sharding import PartitionSpec as P


CSWEEPS = 16
OMEGA = 0.8
C = OMEGA / 6.0
HX = 32
HU = 8
LANES = 128
F32 = jnp.float32
BF16 = jnp.bfloat16
I32 = jnp.int32

VM = pl.BlockSpec(memory_space=pltpu.VMEM)
SM = pl.BlockSpec(memory_space=pltpu.SMEM)
ANY = pl.BlockSpec(memory_space=pl.ANY)
PARAMS = pltpu.CompilerParams(vmem_limit_bytes=56 << 20)


def iota(shape, dim):
    return lax.broadcasted_iota(I32, shape, dim)


def as_matrix(condition):
    return condition.astype(F32).astype(BF16)


def pair_matrix(length):
    shape = (length, length // 2)
    return as_matrix((iota(shape, 0) >> 1) == iota(shape, 1))


def copy_matrix(length):
    shape = (length, 2 * length)
    return as_matrix(iota(shape, 0) == (iota(shape, 1) >> 1))


def select_dot(values, matrix):
    high = values.astype(BF16)
    low = (values - high.astype(F32)).astype(BF16)
    return jnp.dot(high, matrix, preferred_element_type=F32) + jnp.dot(
        low, matrix, preferred_element_type=F32
    )


def each(count, body, unroll=1):
    def step(index, carry):
        body(index)
        return carry

    lax.fori_loop(0, count, step, 0, unroll=unroll)


def beside_lanes(blocks):
    lane = iota(blocks[0].shape, 1)
    right = [pltpu.roll(block, 1, 1) for block in blocks]
    left = [pltpu.roll(block, LANES - 1, 1) for block in blocks]
    sums = []
    for b in range(len(blocks)):
        before = right[b - 1] if b > 0 else 0.0
        after = left[b + 1] if b + 1 < len(blocks) else 0.0
        sums.append(
            jnp.where(lane == 0, before, right[b]) + jnp.where(lane == LANES - 1, after, left[b])
        )
    return sums


def around(field, plane, row, rows):
    count = field.shape[1]

    def at(p, first):
        return [field[p, b, first : first + rows, :] for b in range(count)]

    middle = at(plane, row + 8)
    parts = zip(
        at(plane, row + 7), at(plane, row + 9), beside_lanes(middle), at(plane - 1, row + 8), at(plane + 1, row + 8)
    )
    return middle, [(a + b) + (c + (d + e)) for a, b, c, d, e in parts]


class Edges:
    def __init__(self, boxes, slabs):
        self.box, self.slab = lax.axis_index("box"), lax.axis_index("gz")
        self.boxes, self.slabs = boxes, slabs

    def planes(self, plane, count):
        outside = ((plane < 0) & (self.slab == 0)) | ((plane >= count) & (self.slab == self.slabs - 1))
        return jnp.where(outside, 0.0, 1.0).astype(F32)

    def low(self):
        return jnp.where(self.box == 0, 0.0, 1.0).astype(F32)

    def high(self):
        return jnp.where(self.box == self.boxes - 1, 0.0, 1.0).astype(F32)


def chunks_of(rows, halo, chunk, cut=0):
    out = [] if cut else [(0, halo, -1)]
    inner = (halo, rows - halo)
    for first in range(inner[0], inner[1], chunk):
        out.append((first, min(chunk, inner[1] - first), 0))
    return out if cut else out + [(rows - halo, halo, 1)]


def scale_of(side, edges, plane_scale):
    if side == 0:
        return plane_scale
    row_scale = edges.low() if side < 0 else edges.high()
    return row_scale if plane_scale is None else row_scale * plane_scale


def relax(new, noff, planes, source, soff, rows, halo, edges, count, old=None, ooff=0, extra=None, chunk=16, shift=8, cut=0):
    def body(index):
        plane_scale = None if count is None else edges.planes(index + planes[0], count)
        for first, size, side in chunks_of(rows, halo, chunk, cut):
            scale = scale_of(side, edges, plane_scale)
            if old is None:
                middle, near = around(source, index + (planes[0] + soff), first, size)
                values = [(1.2 * C) * m + (C * C) * n for m, n in zip(middle, near)]
                if extra is not None:
                    values = [v + extra(index, b, first, size) for b, v in enumerate(values)]
            else:
                middle, near = around(old, index + (planes[0] + ooff), first, size)
                at = index + (planes[0] + soff)
                values = [
                    (1.0 - OMEGA) * m + C * (source[at, b, first + 8 : first + 8 + size, :] + n)
                    for b, (m, n) in enumerate(zip(middle, near))
                ]
            for b, value in enumerate(values):
                if scale is not None:
                    value = value * scale
                new[index + (planes[0] + noff), b, first + shift : first + shift + size, :] = value

    each(planes[1] - planes[0], body)


def restrict(source, soff, v, voff, pairs, rows, store, chunk=16):
    count = v.shape[1]
    width = min(2, count)
    half = rows // 2

    def body(index):
        low_v, low_s = 2 * index + (2 * pairs[0] + voff), 2 * index + (2 * pairs[0] + soff)
        matrix = pair_matrix(width * LANES)
        for first in range(0, half, chunk):
            size = min(chunk, half - first)

            def at(field, plane, b, offset):
                return field[plane, b, pl.ds(8 + 2 * first + offset, size, stride=2), :]

            whole = [
                (at(v, low_v, b, 0) + at(v, low_v, b, 1)) + (at(v, low_v + 1, b, 0) + at(v, low_v + 1, b, 1))
                for b in range(count)
            ]
            near = beside_lanes(whole)
            sums = []
            for b in range(count):
                total = near[b] - 4.0 * whole[b]
                total = total + (at(source, low_s, b, 0) + at(source, low_s, b, 1))
                total = total + (at(source, low_s + 1, b, 0) + at(source, low_s + 1, b, 1))
                total = total + (at(v, low_v - 1, b, 0) + at(v, low_v - 1, b, 1))
                total = total + (at(v, low_v + 2, b, 0) + at(v, low_v + 2, b, 1))
                total = total + (at(v, low_v, b, -1) + at(v, low_v + 1, b, -1))
                total = total + (at(v, low_v, b, 2) + at(v, low_v + 1, b, 2))
                sums.append(total)
            for group in range(count // width):
                piece = sums[width * group]
                if width == 2:
                    piece = jnp.concatenate([piece, sums[2 * group + 1]], axis=1)
                store(index, group, first, size, 0.5 * select_dot(piece, matrix))

    each(pairs[1] - pairs[0], body)


def zero(ref, planes):
    for plane in planes:
        ref[plane] = jnp.zeros(ref.shape[1:], F32)


def zero_rims(ref, planes=None):
    rows = ref.shape[2]
    for plane in range(ref.shape[0]) if planes is None else planes:
        for b in range(ref.shape[1]):
            ref[plane, b, 0:8, :] = jnp.zeros((8, LANES), F32)
            ref[plane, b, rows - 8 : rows, :] = jnp.zeros((8, LANES), F32)


def block_copies(wide, tiled, planes, first, rows, sem, back=False):
    copies = []
    for b in range(tiled.shape[1]):
        pair = (
            wide.at[:, :, pl.ds(LANES * b, LANES)],
            tiled.at[pl.ds(planes[0], planes[1]), b, pl.ds(first, rows), :],
        )
        copies.append(pltpu.make_async_copy(*(pair[::-1] if back else pair), sem))
    return copies


def pack_kernel(mask, fine, flux, out, fine_s, flux_s, sem):
    patches, fine_z = fine.shape[0], fine.shape[1]
    n0 = fine_z // 2
    blocks = fine_s.shape[0]
    copies = [
        pltpu.make_async_copy(fine.at[:, :, pl.ds(LANES * b, LANES)], fine_s.at[b], sem.at[b])
        for b in range(blocks)
    ]
    copies.append(pltpu.make_async_copy(flux, flux_s, sem.at[blocks]))
    for copy in copies:
        copy.start()
    base = lax.axis_index("box") * patches
    side = (iota((n0, LANES), 1) >> 4) & 3
    source, target = iota((LANES, LANES), 0), iota((LANES, LANES), 1)
    s, i = (source >> 4) & 3, (source & 15) >> 1
    goal = jnp.where(
        s == 0, i + 91, jnp.where(s == 1, i + 1, jnp.where(s == 2, 80 - 10 * i, 89 - 10 * i))
    )
    matrices = [as_matrix(goal == target)]
    for b in range(blocks):
        place = source + LANES * b
        goal = 10 * (8 - (place >> 5)) + ((place & 15) >> 1) + 1
        matrices.append(as_matrix(goal == target))
    for copy in copies:
        copy.wait()
    masked, fine_rows = [], [[] for _ in range(blocks)]
    for patch in range(patches):
        m = [mask[s, base + patch].astype(F32) for s in range(4)]
        factor = jnp.where(side == 0, m[0], jnp.where(side == 1, m[1], jnp.where(side == 2, m[2], m[3])))
        masked.append(
            (flux_s[patch, pl.ds(0, n0, stride=2), :] + flux_s[patch, pl.ds(1, n0, stride=2), :]) * factor
        )
        for b in range(blocks):
            fine_rows[b].append(
                fine_s[b, patch, pl.ds(0, n0, stride=2), :] + fine_s[b, patch, pl.ds(1, n0, stride=2), :]
            )
    total = select_dot(jnp.concatenate(masked, axis=0), matrices[0])
    for b in range(blocks):
        total = total + select_dot(jnp.concatenate(fine_rows[b], axis=0), matrices[b + 1])
    out[...] = 0.125 * total


class Tiles:
    def __init__(self):
        self.lane = iota((16, LANES), 1)
        row = iota((16, LANES), 0)
        self.ring_row = (row >= 3) & (row < 13)
        self.core_row = (row >= 4) & (row < 12)

    def put(self, field, row, column, pairs):
        row = pl.multiple_of(row, 8)
        block, offset = column >> 7, column & (LANES - 1)
        across = self.lane - offset
        ring = self.ring_row & (across >= 3) & (across < 13)
        core = self.core_row & (across >= 4) & (across < 12)
        for plane, line in pairs:
            values = jnp.broadcast_to(line, (8, LANES))
            values = pltpu.roll(values, 0, 1, stride=10, stride_axis=0)
            tile = jnp.concatenate(
                [
                    pltpu.roll(values, (offset + 11) & (LANES - 1), 1),
                    pltpu.roll(values, (offset + 91) & (LANES - 1), 1),
                ],
                axis=0,
            )
            now = field[plane, block, pl.ds(row, 16), :]
            field[plane, block, pl.ds(row, 16), :] = jnp.where(core, 0.0, now) + jnp.where(ring, tile, 0.0)


def each_owned(box_list, box, body):
    def step(patch, slot):
        mine = box_list[0, patch] == box

        @pl.when(mine)
        def _():
            body(patch, slot)

        return slot + jnp.where(mine, 1, 0)

    lax.fori_loop(0, box_list.shape[1], step, jnp.zeros((), I32))


def down_kernel(
    boxes, slabs, n0, x0,
    box_list, coarse, x_low, x_high, packed,
    f_own, rim_top, rim_bot, c1, c2, up, down,
    fb, vb, g1, v1, sem, out_sem,
):
    edges = Edges(boxes, slabs)
    rows0, rows1, rows2 = x0 + 2 * HX, x0 // 2 + HX, x0 // 4 + HX // 2
    n1, n2 = n0 // 2, n0 // 4
    copies = (
        block_copies(x_low, fb, (2, n0), 8, HX, sem.at[0])
        + block_copies(coarse, fb, (2, n0), 8 + HX, x0, sem.at[1])
        + block_copies(x_high, fb, (2, n0), 8 + HX + x0, HX, sem.at[2])
    )
    for copy in copies:
        copy.start()
    zero(fb, (0, 1, n0 + 2, n0 + 3))
    zero_rims(fb, range(2, n0 + 2))
    zero(vb, (0, 1, n0 + 4, n0 + 5))
    zero_rims(vb, range(2, n0 + 4))
    zero(g1, (0, 1, 2, n1 + 5, n1 + 6, n1 + 7))
    zero_rims(g1, range(3, n1 + 5))
    zero(v1, (0, 1, 2, n1 + 7, n1 + 8, n1 + 9))
    zero_rims(v1, range(3, n1 + 7))
    for copy in copies:
        copy.wait()

    tiles = Tiles()

    def place(patch):
        start = (box_list[0, patch] - edges.box) * x0 + box_list[1, patch] - 4 + HX

        @pl.when((start >= 0) & (start < rows0))
        def _():
            tiles.put(
                fb,
                start + 8,
                box_list[2, patch] - 4,
                [(2 + z, packed[pl.ds(patch * n0 + z, 1), :]) for z in range(n0)],
            )

    each(box_list.shape[1], place)

    inner = pl.ds(8 + HX - HU, x0 + 2 * HU)
    out_copy = pltpu.make_async_copy(fb.at[pl.ds(2, n0), :, inner, :], f_own, out_sem)
    out_copy.start()

    relax(vb, 3, (-1, n0 + 1), fb, 2, rows0, HX, edges, n0)

    h1 = HX // 2

    def store1(index, group, first, size, value):
        scale = edges.planes(index - 1, n1)
        if first < h1:
            scale = scale * edges.low()
        if first >= rows1 - h1:
            scale = scale * edges.high()
        g1[index + 3, group, 8 + first : 8 + first + size, :] = value * scale

    restrict(fb, 2, vb, 3, (-1, n1 + 1), rows0, store1)
    for plane in range(n1 + 2):
        for b in range(g1.shape[1]):
            c1[plane, b] = g1[plane + 3, b, 8 + h1 - HU : 8 + rows1 - h1 + HU, :]

    relax(v1, 5, (-2, n1 + 2), g1, 4, rows1, h1, edges, n1)

    h2 = HX // 4

    def store2(index, group, first, size, value):
        if first < h2:
            value = value * edges.low()
        if first >= rows2 - h2:
            value = value * edges.high()
        c2[index, group, first : first + size, :] = value

    restrict(g1, 4, v1, 5, (-2, n2 + 2), rows1, store2, chunk=8)

    r1 = c1.shape[2]
    for target, fine_plane, coarse_first in ((up, n1 + 1, n2 + 2), (down, 0, 0)):
        target[0:rows2] = c2[coarse_first, 0]
        target[rows2 : 2 * rows2] = c2[coarse_first + 1, 0]
        for b in range(c1.shape[1]):
            first = 2 * rows2 + b * r1
            target[first : first + r1] = c1[fine_plane, b]

    slots = rim_top.shape[0] - 24 * fb.shape[1]
    base = 24 * fb.shape[1]

    def keep(patch, slot):
        for z in range(3):
            rim_top[pl.ds(base + z * (slots // 3) + slot, 1), :] = packed[pl.ds(patch * n0 + n0 - 3 + z, 1), :]
            rim_bot[pl.ds(base + z * (slots // 3) + slot, 1), :] = packed[pl.ds(patch * n0 + z, 1), :]

    rim_top[base:, :] = jnp.zeros((slots, LANES), F32)
    rim_bot[base:, :] = jnp.zeros((slots, LANES), F32)
    each_owned(box_list, edges.box, keep)
    for z in range(3):
        for b in range(fb.shape[1]):
            first = 8 * (fb.shape[1] * z + b)
            for rim, plane in ((rim_top, n0 - 1 + z), (rim_bot, 2 + z)):
                rim[first : first + 3, :] = fb[plane, b, 8 + HX - 3 : 8 + HX, :]
                rim[first + 3 : first + 6, :] = fb[plane, b, 8 + HX + x0 : 8 + HX + x0 + 3, :]
                rim[first + 6 : first + 8, :] = jnp.zeros((2, LANES), F32)
    out_copy.wait()


def total_kernel(c2, below, above, copies):
    n2, rows2 = c2.shape[0] - 4, c2.shape[2]
    for plane in range(n2):
        value = c2[2 + plane, 0]
        if plane < 2:
            value = value + below[plane * rows2 : (plane + 1) * rows2]
        if plane >= n2 - 2:
            first = (plane - (n2 - 2)) * rows2
            value = value + above[first : first + rows2]
        for slab in range(copies.shape[0]):
            copies[slab, plane * rows2 : (plane + 1) * rows2] = value


def join_kernel(rows2, c1, below, above, rim_top, rim_bot, s1, up, down):
    n1, r1 = s1.shape[0], c1.shape[2]
    for plane in range(n1):
        s1[plane] = c1[1 + plane]
    for b in range(s1.shape[1]):
        first = 2 * rows2 + b * r1
        s1[0, b] = s1[0, b] + below[first : first + r1]
        s1[n1 - 1, b] = s1[n1 - 1, b] + above[first : first + r1]
    near = r1 - HU
    for p in range(4):
        for b in range(s1.shape[1]):
            first = near * (p * s1.shape[1] + b)
            up[first : first + near] = s1[n1 - 4 + p, b, HU // 2 : HU // 2 + near, :]
            down[first : first + near] = s1[p, b, HU // 2 : HU // 2 + near, :]
    first = near * 4 * s1.shape[1]
    up[first:] = rim_top[...]
    down[first:] = rim_bot[...]


def third_kernel(boxes, slabs, s2, s3, fb, vb):
    edges = Edges(boxes, slabs)
    planes, rows = s2.shape[0], s2.shape[1]
    zero(fb, (0, planes + 1))
    zero(vb, (0, planes + 1))
    zero_rims(fb, range(1, planes + 1))
    zero_rims(vb, range(1, planes + 1))
    for plane in range(planes):
        fb[plane + 1, 0, 8 : 8 + rows, :] = s2[plane]
    relax(vb, 1, (0, planes), fb, 1, rows, HX // 4, edges, None, chunk=32)
    quarter = planes // 4
    h3 = HX // 8
    own = rows // 2 - 2 * h3
    lanes = LANES // 2

    for part in range(2):

        def store(index, group, first, size, value, part=part):
            s3[index, :, lanes * part : lanes * (part + 1)] = value[h3 : h3 + own]

        restrict(
            fb, 1, vb, 1, (quarter * part, quarter * (part + 1)), rows, store, chunk=rows // 2
        )


def coarse_kernel(
    boxes, slabs,
    s3, s2, s1, below, above,
    e1,
    sc, va3, vb3, e3p, f2, v2a, v2b, e2p, f1, v1a, v1b,
):
    edges = Edges(boxes, slabs)
    slab = edges.slab
    half, rows3 = sc.shape[0], sc.shape[2] - 16
    own3 = s3.shape[2]
    zero_rims(va3)
    zero_rims(vb3)
    for box in range(boxes):
        for plane in range(half):
            value = s3[box, plane]
            sc[plane, 0, 8 + box * own3 : 8 + (box + 1) * own3, :] = value
            va3[plane, 0, 8 + box * own3 : 8 + (box + 1) * own3, :] = C * value

    def coarsest(old, new):
        chunk = 16
        lane = iota((chunk, LANES), 1)
        for row in range(0, rows3, chunk):
            inner = slice(row + 8, row + 8 + chunk)
            for plane in range(half):
                middle = old[plane, 0, inner, :]
                before = jnp.where((lane & 63) == 0, 0.0, pltpu.roll(middle, 1, 1))
                after = jnp.where((lane & 63) == 63, 0.0, pltpu.roll(middle, LANES - 1, 1))
                if plane > 0:
                    lower = old[plane - 1, 0, inner, :]
                else:
                    lower = jnp.where(lane < 64, 0.0, pltpu.roll(old[half - 1, 0, inner, :], 64, 1))
                if plane < half - 1:
                    upper = old[plane + 1, 0, inner, :]
                else:
                    upper = jnp.where(lane < 64, pltpu.roll(old[0, 0, inner, :], 64, 1), 0.0)
                beside = old[plane, 0, row + 7 : row + 7 + chunk, :] + old[plane, 0, row + 9 : row + 9 + chunk, :]
                near = beside + ((before + after) + (lower + upper))
                new[plane, 0, inner, :] = (1.0 - OMEGA) * middle + C * (sc[plane, 0, inner, :] + near)

    def double(index):
        coarsest(va3, vb3)
        coarsest(vb3, va3)

    each((CSWEEPS - 1) // 2, double)
    coarsest(va3, vb3)

    n2, rows2 = s2.shape[0] // slabs, s2.shape[1]
    n3 = n2 // 2
    shape = (LANES, LANES)
    copy_low = (iota(shape, 0) == (iota(shape, 1) >> 1)).astype(F32)
    copy_high = (iota(shape, 0) == (iota(shape, 1) >> 1) + 64).astype(F32)
    total3 = 2 * half
    h3 = HX // 8
    window = pl.multiple_of(edges.box * own3, 8)
    for k in range(-2, n3 + 2):
        plane = slab * n3 + k
        inside = (plane >= 0) & (plane < total3)
        safe = jnp.clip(plane, 0, total3 - 1)
        upper = safe >= half
        matrix = jnp.where(upper, copy_high, copy_low) * jnp.where(inside, 1.0, 0.0)
        value = vb3[jnp.where(upper, safe - half, safe), 0, pl.ds(window, own3 + 16), :]
        value = select_dot(value, matrix.astype(BF16))[8 - h3 : 8 + own3 + h3]
        e3p[k + 2, pl.ds(0, own3 + 2 * h3, stride=2), :] = value
        e3p[k + 2, pl.ds(1, own3 + 2 * h3, stride=2), :] = value

    zero_rims(f2)
    zero_rims(v2a)
    zero_rims(v2b)
    planes2 = s2.shape[0]
    for p in range(-5, n2 + 5):
        plane = slab * n2 + p
        inside = jnp.where((plane >= 0) & (plane < planes2), 1.0, 0.0)
        f2[p + 5, 0, 8 : 8 + rows2, :] = s2[jnp.clip(plane, 0, planes2 - 1)] * inside

    def extra2(index, b, first, size):
        return e3p[index >> 1, first : first + size, :]

    h2 = HX // 4
    relax(v2a, 5, (-4, n2 + 4), f2, 5, rows2, h2, edges, n2, extra=extra2, chunk=32)
    relax(v2b, 5, (-3, n2 + 3), f2, 5, rows2, h2, edges, n2, old=v2a, ooff=5, chunk=32)
    relax(v2a, 5, (-2, n2 + 2), f2, 5, rows2, h2, edges, n2, old=v2b, ooff=5, chunk=32)

    n1, rows1 = s1.shape[0], s1.shape[2]
    cut = h2 - HU // 2
    matrix2 = copy_matrix(LANES)
    for k in range(-2, n2 + 2):
        value = select_dot(v2a[k + 5, 0, 8 + cut : 8 + rows2 - cut, :], matrix2)
        for b in range(2):
            part = value[:, LANES * b : LANES * (b + 1)]
            e2p[k + 2, b, pl.ds(0, rows2 - 2 * cut, stride=2), :] = part
            e2p[k + 2, b, pl.ds(1, rows2 - 2 * cut, stride=2), :] = part
    zero_rims(f1)
    zero_rims(v1a)
    zero_rims(v1b)
    near = rows1 - HU
    inner = slice(8 + HU // 2, 8 + HU // 2 + near)
    for b in range(f1.shape[1]):
        for p in range(4):
            first = near * (p * f1.shape[1] + b)
            for plane, message in ((p, below), (4 + n1 + p, above)):
                f1[plane, b, 8:16, :] = jnp.zeros((8, LANES), F32)
                f1[plane, b, rows1 : 8 + rows1, :] = jnp.zeros((8, LANES), F32)
                f1[plane, b, inner, :] = message[first : first + near]
        for p in range(n1):
            f1[4 + p, b, 8 : 8 + rows1, :] = s1[p, b]

    def extra1(index, b, first, size):
        return e2p[(index + 1) >> 1, b, first : first + size, :]

    relax(v1a, 4, (-3, n1 + 3), f1, 4, rows1, HU, edges, n1, extra=extra1)
    relax(v1b, 4, (-2, n1 + 2), f1, 4, rows1, HU, edges, n1, old=v1a, ooff=4)
    relax(e1, 1, (-1, n1 + 1), f1, 4, rows1, HU, edges, n1, old=v1b, ooff=4, shift=0)


def finish_kernel(
    boxes, slabs, n0, x0,
    box_list, e1, f_own, z_below, z_above, below, above,
    out,
    fb, va, vb, ep, ob, sem, out_sem,
):
    edges = Edges(boxes, slabs)
    rows = x0 + 2 * HU
    copies = (
        [pltpu.make_async_copy(f_own, fb.at[pl.ds(3, n0), :, pl.ds(8, rows), :], sem.at[0])]
        + block_copies(z_below, fb, (0, 3), 8 + HU, x0, sem.at[1])
        + block_copies(z_above, fb, (3 + n0, 3), 8 + HU, x0, sem.at[2])
    )
    for copy in copies:
        copy.start()
    zero_rims(fb)
    zero_rims(va)
    zero_rims(vb)
    rim = 8 * 3 * fb.shape[1]
    slots = boxes * max(2, box_list.shape[1] // boxes // 4)
    first = below.shape[0] - rim - 3 * slots
    for z in range(3):
        for b in range(fb.shape[1]):
            at = first + 8 * (fb.shape[1] * z + b)
            for plane, message in ((z, below), (3 + n0 + z, above)):
                fb[plane, b, 8 : 8 + HU, :] = jnp.zeros((HU, LANES), F32)
                fb[plane, b, 8 + HU + x0 : 8 + rows, :] = jnp.zeros((HU, LANES), F32)
                fb[plane, b, 5 + HU : 8 + HU, :] = message[at : at + 3]
                fb[plane, b, 8 + HU + x0 : 11 + HU + x0, :] = message[at + 3 : at + 6]
    matrix = copy_matrix(LANES)
    cut = HU // 2
    r1 = e1.shape[2]
    size1 = r1 - 2 * cut

    def prolong(k):
        for group in range(e1.shape[1]):
            value = select_dot(e1[k, group, cut : r1 - cut, :], matrix)
            for b in range(2):
                part = value[:, LANES * b : LANES * (b + 1)]
                ep[k, 2 * group + b, pl.ds(0, size1, stride=2), :] = part
                ep[k, 2 * group + b, pl.ds(1, size1, stride=2), :] = part

    each(e1.shape[0], prolong)
    for copy in copies:
        copy.wait()
    tiles = Tiles()

    def place(patch, slot):
        lines = [(z, below, z) for z in range(3)] + [(3 + n0 + z, above, z) for z in range(3)]
        tiles.put(
            fb,
            box_list[1, patch] - 4 + HU + 8,
            box_list[2, patch] - 4,
            [(plane, message[pl.ds(first + rim + z * slots + slot, 1), :]) for plane, message, z in lines],
        )

    each_owned(box_list, edges.box, place)

    def extra(index, b, first, size):
        return ep[index >> 1, b, first : first + size, :]

    relax(va, 3, (-2, n0 + 2), fb, 3, rows, HU, edges, n0, extra=extra)
    relax(vb, 3, (-1, n0 + 1), fb, 3, rows, HU, edges, n0, old=va, ooff=3)

    def last(z):
        view = ob.at[pl.ds(z, 1)]
        relax(view, 0, (0, 1), fb.at[pl.ds(z + 3, 1)], 0, rows, HU, edges, None, old=vb.at[pl.ds(z + 2, 3)], ooff=1, shift=-HU, cut=1)
        for copy in block_copies(out.at[pl.ds(z, 1)], ob, (z, 1), 0, x0, out_sem, back=True):
            copy.start()

    each(n0, last)
    for copy in block_copies(out, ob, (0, n0), 0, x0, out_sem, back=True):
        copy.wait()


def shape_of(*dims):
    return jax.ShapeDtypeStruct(dims, F32)


def scratch(*dims):
    return pltpu.VMEM(dims, F32)


def cost(flops, moved):
    return pl.CostEstimate(flops=flops, bytes_accessed=moved, transcendentals=0)


def shift_by(array, axis, step):
    size = lax.axis_size(axis)
    pairs = [(i, i + step) for i in range(size) if 0 <= i + step < size]
    return lax.ppermute(array, axis, pairs)


def per_device(coarse, fine_div, reflux, box_list, cf_mask):
    boxes, slabs = lax.axis_size("box"), lax.axis_size("gz")
    n0, x0, y0 = coarse.shape
    n1, n2 = n0 // 2, n0 // 4
    b0, b1 = y0 // LANES, y0 // LANES // 2
    patches, fine_z, fine_lanes = fine_div.shape
    rows0, rows1, rows2 = x0 + 2 * HX, x0 // 2 + HX, x0 // 4 + HX // 2
    up_rows0, up_rows1 = x0 + 2 * HU, x0 // 2 + 2 * HU
    dma = pltpu.SemaphoreType.DMA

    x_low = shift_by(coarse[:, x0 - HX :], "box", 1)
    x_high = shift_by(coarse[:, :HX], "box", -1)

    z_below = shift_by(coarse[n0 - 3 :], "gz", 1)
    z_above = shift_by(coarse[:3], "gz", -1)

    fine_blocks = fine_lanes // LANES
    packed = pl.pallas_call(
        pack_kernel,
        name="pack",
        out_shape=shape_of(patches * n0, LANES),
        in_specs=[SM, ANY, ANY],
        out_specs=VM,
        scratch_shapes=[
            scratch(fine_blocks, patches, fine_z, LANES),
            scratch(patches, fine_z, LANES),
            dma((fine_blocks + 1,)),
        ],
        compiler_params=PARAMS,
        cost_estimate=cost(10**7, 10**6),
    )(cf_mask.T, fine_div, reflux)
    packed = lax.all_gather(packed, "box", axis=0, tiled=True)

    message = 2 * rows2 + b1 * up_rows1
    slots = boxes * max(2, patches // 4)
    rim = 3 * (8 * b0 + slots)
    f_own, rim_top, rim_bot, c1, c2, up, down = pl.pallas_call(
        functools.partial(down_kernel, boxes, slabs, n0, x0),
        name="down",
        out_shape=(
            shape_of(n0, b0, up_rows0, LANES),
            shape_of(rim, LANES),
            shape_of(rim, LANES),
            shape_of(n1 + 2, b1, up_rows1, LANES),
            shape_of(n2 + 4, 1, rows2, LANES),
            shape_of(message, LANES),
            shape_of(message, LANES),
        ),
        in_specs=[SM, ANY, ANY, ANY, VM],
        out_specs=(ANY,) + (VM,) * 6,
        scratch_shapes=[
            scratch(n0 + 4, b0, rows0 + 16, LANES),
            scratch(n0 + 6, b0, rows0 + 16, LANES),
            scratch(n1 + 8, b1, rows1 + 16, LANES),
            scratch(n1 + 10, b1, rows1 + 16, LANES),
            dma((3,)),
            dma(()),
        ],
        compiler_params=PARAMS,
        cost_estimate=cost(3 * 10**7, 10**7),
    )(box_list.T, coarse, x_low, x_high, packed)

    from_below = shift_by(up, "gz", 1)
    from_above = shift_by(down, "gz", -1)
    copies = pl.pallas_call(
        total_kernel,
        name="total",
        out_shape=shape_of(slabs, n2 * rows2, LANES),
        in_specs=[VM] * 3,
        out_specs=VM,
        compiler_params=PARAMS,
        cost_estimate=cost(10**6, 10**6),
    )(c2, from_below, from_above)
    s2 = lax.all_to_all(copies, "gz", split_axis=0, concat_axis=0, tiled=True)
    s2 = s2.reshape(slabs * n2, rows2, LANES)
    last = 4 * b1 * (up_rows1 - HU) + rim
    s1, up, down = pl.pallas_call(
        functools.partial(join_kernel, rows2),
        name="join",
        out_shape=(shape_of(n1, b1, up_rows1, LANES), shape_of(last, LANES), shape_of(last, LANES)),
        in_specs=[VM] * 5,
        out_specs=(VM,) * 3,
        compiler_params=PARAMS,
        cost_estimate=cost(10**6, 10**6),
    )(c1, from_below, from_above, rim_top, rim_bot)
    below = shift_by(up, "gz", 1)
    above = shift_by(down, "gz", -1)

    planes2, half = slabs * n2, slabs * n2 // 4
    own3 = x0 // 8
    s3 = pl.pallas_call(
        functools.partial(third_kernel, boxes, slabs),
        name="third",
        out_shape=shape_of(half, own3, LANES),
        in_specs=[VM],
        out_specs=VM,
        scratch_shapes=[scratch(planes2 + 2, 1, rows2 + 16, LANES)] * 2,
        compiler_params=PARAMS,
        cost_estimate=cost(10**6, 10**6),
    )(s2)
    s3 = lax.all_gather(s3, "box", axis=0)
    rows3 = boxes * own3
    e1 = pl.pallas_call(
        functools.partial(coarse_kernel, boxes, slabs),
        name="coarse",
        out_shape=shape_of(n1 + 2, b1, up_rows1, LANES),
        in_specs=[VM] * 5,
        out_specs=VM,
        scratch_shapes=[scratch(half, 1, rows3 + 16, LANES)] * 3
        + [scratch(n2 // 2 + 4, rows2, LANES)]
        + [scratch(n2 + 10, 1, rows2 + 16, LANES)] * 3
        + [scratch(n2 + 4, 2, up_rows1, LANES)]
        + [scratch(n1 + 8, b1, up_rows1 + 16, LANES)] * 3,
        compiler_params=PARAMS,
        cost_estimate=cost(10**7, 4 * 10**6),
    )(s3, s2, s1, below, above)

    return pl.pallas_call(
        functools.partial(finish_kernel, boxes, slabs, n0, x0),
        name="finish",
        out_shape=shape_of(n0, x0, y0),
        in_specs=[SM, VM, ANY, ANY, ANY, VM, VM],
        out_specs=ANY,
        scratch_shapes=[scratch(n0 + 6, b0, up_rows0 + 16, LANES)] * 3
        + [
            scratch(n1 + 2, b0, up_rows0, LANES),
            scratch(n0, b0, x0, LANES),
            dma((3,)),
            dma(()),
        ],
        compiler_params=PARAMS,
        cost_estimate=cost(3 * 10**7, 10**7),
    )(box_list.T, e1, f_own, z_below, z_above, below, above)


def solution(mesh):
    return jax.shard_map(
        per_device,
        mesh=mesh,
        in_specs=(P("gz", "box", None), P("box", "gz", None), P("box", "gz", None), P(), P()),
        out_specs=P("gz", "box", None),
        check_vma=False,
    )
```

```python
import functools

import jax
import jax.numpy as jnp
from jax import lax
from jax.experimental import pallas as pl
from jax.experimental.pallas import tpu as pltpu
from jax.sharding import PartitionSpec as P


CSWEEPS = 16
OMEGA = 0.8
C = OMEGA / 6.0
HX = 32
HU = 8
LANES = 128
F32 = jnp.float32
BF16 = jnp.bfloat16
I32 = jnp.int32

VM = pl.BlockSpec(memory_space=pltpu.VMEM)
SM = pl.BlockSpec(memory_space=pltpu.SMEM)
HBM = pl.BlockSpec(memory_space=pltpu.MemorySpace.HBM)


def iota(shape, dim):
    return lax.broadcasted_iota(I32, shape, dim)


def as_matrix(condition):
    return condition.astype(F32).astype(BF16)


def pair_matrix(length):
    shape = (length, length // 2)
    return as_matrix((iota(shape, 0) >> 1) == iota(shape, 1))


def copy_matrix(length):
    shape = (length, 2 * length)
    return as_matrix(iota(shape, 0) == (iota(shape, 1) >> 1))


def select_dot(values, matrix):
    high = values.astype(BF16)
    low = (values - high.astype(F32)).astype(BF16)
    return jnp.dot(high, matrix, preferred_element_type=F32) + jnp.dot(
        low, matrix, preferred_element_type=F32
    )


def each(count, body, unroll=1):
    def step(index, carry):
        body(index)
        return carry

    lax.fori_loop(0, count, step, 0, unroll=unroll)


def beside_lanes(blocks):
    lane = iota(blocks[0].shape, 1)
    right = [pltpu.roll(block, 1, 1) for block in blocks]
    left = [pltpu.roll(block, LANES - 1, 1) for block in blocks]
    sums = []
    for b in range(len(blocks)):
        before = right[b - 1] if b > 0 else 0.0
        after = left[b + 1] if b + 1 < len(blocks) else 0.0
        sums.append(
            jnp.where(lane == 0, before, right[b]) + jnp.where(lane == LANES - 1, after, left[b])
        )
    return sums


def around(field, plane, row, rows, has=(True, True, True)):
    count = field.shape[1]

    def at(p, first):
        return [field[p, b, first : first + rows, :] for b in range(count)]

    sides = [at(plane + p, row + 8) for p in (-1, 1) if has[p + 1]]
    if not has[1]:
        return None, sides[0]
    middle = at(plane, row + 8)
    beside = zip(at(plane, row + 7), at(plane, row + 9), beside_lanes(middle))
    near = [(a + b) + c for a, b, c in beside]
    for side in sides:
        near = [a + b for a, b in zip(near, side)]
    return middle, near


class Edges:
    def __init__(self, boxes, slabs):
        self.box, self.slab = lax.axis_index("box"), lax.axis_index("gz")
        self.boxes, self.slabs = boxes, slabs

    def planes(self, plane, count):
        outside = ((plane < 0) & (self.slab == 0)) | ((plane >= count) & (self.slab == self.slabs - 1))
        return jnp.where(outside, 0.0, 1.0).astype(F32)

    def low(self):
        return jnp.where(self.box == 0, 0.0, 1.0).astype(F32)

    def high(self):
        return jnp.where(self.box == self.boxes - 1, 0.0, 1.0).astype(F32)


def chunks_of(rows, halo, chunk, cut=0):
    out = [] if cut else [(0, halo, -1)]
    inner = (halo, rows - halo)
    for first in range(inner[0], inner[1], chunk):
        out.append((first, min(chunk, inner[1] - first), 0))
    return out if cut else out + [(rows - halo, halo, 1)]


def scale_of(side, edges, plane_scale):
    if side == 0:
        return plane_scale
    row_scale = edges.low() if side < 0 else edges.high()
    return row_scale if plane_scale is None else row_scale * plane_scale


def relax(new, noff, planes, source, soff, rows, halo, edges, count, old=None, ooff=0, extra=None, chunk=16, shift=8, cut=0, s_planes=None, unroll=1):
    def body(index, has=(True, True, True)):
        plane_scale = None if count is None else edges.planes(index + planes[0], count)
        for first, size, side in chunks_of(rows, halo, chunk, cut):
            scale = scale_of(side, edges, plane_scale)
            if old is None:
                middle, near = around(source, index + (planes[0] + soff), first, size, has)
                values = [(C * C) * n for n in near]
                if middle is not None:
                    values = [(1.2 * C) * m + v for m, v in zip(middle, values)]
                if extra is not None:
                    values = [v + extra(index, b, first, size) for b, v in enumerate(values)]
            else:
                middle, near = around(old, index + (planes[0] + ooff), first, size)
                at = index + (planes[0] + soff)
                values = [
                    (1.0 - OMEGA) * m + C * (source[at, b, first + 8 : first + 8 + size, :] + n)
                    for b, (m, n) in enumerate(zip(middle, near))
                ]
            for b, value in enumerate(values):
                if scale is not None:
                    value = value * scale
                new[index + (planes[0] + noff), b, first + shift : first + shift + size, :] = value

    if s_planes is None:
        each(planes[1] - planes[0], body, unroll)
        return
    inner = []
    for plane in range(*planes):
        has = tuple(s_planes[0] <= plane + p < s_planes[1] for p in (-1, 0, 1))
        if all(has):
            inner.append(plane)
        else:
            body(plane - planes[0], has)
    if inner:
        first = inner[0] - planes[0]
        each(len(inner), lambda index: body(index + first), unroll)


def restrict(source, soff, v, voff, pairs, rows, summed, store, chunk=8, v_planes=None, s_planes=None):
    count = v.shape[1]
    width = min(2, count)
    half = rows // 2

    def body(index, has_v=(True,) * 4, has_s=(True,) * 2):
        low_v, low_s = 2 * index + (2 * pairs[0] + voff), 2 * index + (2 * pairs[0] + soff)
        matrix = pair_matrix(width * LANES)
        for first in range(0, half, chunk):
            size = min(chunk, half - first)

            def at(field, plane, b, offset):
                return field[plane, b, pl.ds(8 + 2 * first + offset, size, stride=2), :]

            def both(field, plane, b):
                return at(field, plane, b, 0) + at(field, plane, b, 1)

            def total_of(terms):
                total = terms[0]
                for term in terms[1:]:
                    total = total + term
                return total

            inside = [p for p in (1, 2) if has_v[p]]
            sums = []
            if inside:
                whole = [total_of([both(v, low_v + p - 1, b) for p in inside]) for b in range(count)]
                near = beside_lanes(whole)
            for b in range(count):
                terms = []
                if inside:
                    terms.append(near[b] - 4.0 * whole[b])
                    terms += [at(v, low_v + p - 1, b, -1) + at(v, low_v + p - 1, b, 2) for p in inside]
                terms += [both(source, low_s + p, b) for p in (0, 1) if has_s[p]]
                terms += [both(v, low_v + p - 1, b) for p in (0, 3) if has_v[p]]
                sums.append(total_of(terms))
            for b in range(count):
                summed[b // width, first : first + size, LANES * (b % width) : LANES * (b % width + 1)] = sums[b]
        for group in range(count // width):
            store(index, group, 0.5 * select_dot(summed[group], matrix))

    if v_planes is None:
        each(pairs[1] - pairs[0], body)
        return
    inner = []
    for coarse in range(*pairs):
        has_v = tuple(v_planes[0] <= 2 * coarse + p - 1 < v_planes[1] for p in range(4))
        has_s = tuple(s_planes[0] <= 2 * coarse + p < s_planes[1] for p in range(2))
        if all(has_v + has_s):
            inner.append(coarse)
        else:
            body(coarse - pairs[0], has_v, has_s)
    if inner:
        first = inner[0] - pairs[0]
        each(len(inner), lambda index: body(index + first))


def zero(ref, planes):
    for plane in planes:
        ref[plane] = jnp.zeros(ref.shape[1:], F32)


def zero_rims(ref, planes=None):
    rows = ref.shape[2]
    for plane in range(ref.shape[0]) if planes is None else planes:
        for b in range(ref.shape[1]):
            ref[plane, b, 0:8, :] = jnp.zeros((8, LANES), F32)
            ref[plane, b, rows - 8 : rows, :] = jnp.zeros((8, LANES), F32)


def block_copies(wide, tiled, planes, first, rows, sem, back=False):
    copies = []
    for b in range(tiled.shape[1]):
        pair = (
            wide.at[:, :, pl.ds(LANES * b, LANES)],
            tiled.at[pl.ds(planes[0], planes[1]), b, pl.ds(first, rows), :],
        )
        copies.append(pltpu.make_async_copy(*(pair[::-1] if back else pair), sem))
    return copies


def pack_kernel(mask, fine, flux, coarse, out, x_first, x_last, z_first, z_last, fine_s, flux_s, sem, edge_sem):
    patches, fine_z = fine.shape[0], fine.shape[1]
    n0 = fine_z // 2
    blocks = fine_s.shape[0]
    copies = [
        pltpu.make_async_copy(fine.at[:, :, pl.ds(LANES * b, LANES)], fine_s.at[b], sem.at[b])
        for b in range(blocks)
    ]
    copies.append(pltpu.make_async_copy(flux, flux_s, sem.at[blocks]))
    n, x = coarse.shape[0], coarse.shape[1]
    cuts = [
        pltpu.make_async_copy(coarse.at[pl.ds(n - 2, 2)], z_last, edge_sem.at[0]),
        pltpu.make_async_copy(coarse.at[pl.ds(0, 2)], z_first, edge_sem.at[1]),
        pltpu.make_async_copy(coarse.at[:, pl.ds(x - HX, HX), :], x_last, edge_sem.at[2]),
        pltpu.make_async_copy(coarse.at[:, pl.ds(0, HX), :], x_first, edge_sem.at[3]),
    ]
    for copy in copies + cuts:
        copy.start()
    base = lax.axis_index("box") * patches
    side = (iota((n0, LANES), 1) >> 4) & 3
    source, target = iota((LANES, LANES), 0), iota((LANES, LANES), 1)
    s, i = (source >> 4) & 3, (source & 15) >> 1
    goal = jnp.where(
        s == 0, i + 91, jnp.where(s == 1, i + 1, jnp.where(s == 2, 80 - 10 * i, 89 - 10 * i))
    )
    matrices = [as_matrix(goal == target)]
    for b in range(blocks):
        place = source + LANES * b
        goal = 10 * (8 - (place >> 5)) + ((place & 15) >> 1) + 1
        matrices.append(as_matrix(goal == target))
    for copy in copies:
        copy.wait()
    masked, fine_rows = [], [[] for _ in range(blocks)]
    for patch in range(patches):
        m = [mask[s, base + patch].astype(F32) for s in range(4)]
        factor = jnp.where(side == 0, m[0], jnp.where(side == 1, m[1], jnp.where(side == 2, m[2], m[3])))
        masked.append(
            (flux_s[patch, pl.ds(0, n0, stride=2), :] + flux_s[patch, pl.ds(1, n0, stride=2), :]) * factor
        )
        for b in range(blocks):
            fine_rows[b].append(
                fine_s[b, patch, pl.ds(0, n0, stride=2), :] + fine_s[b, patch, pl.ds(1, n0, stride=2), :]
            )
    total = select_dot(jnp.concatenate(masked, axis=0), matrices[0])
    for b in range(blocks):
        total = total + select_dot(jnp.concatenate(fine_rows[b], axis=0), matrices[b + 1])
    out[...] = 0.125 * total
    for cut in cuts:
        cut.wait()


class Tiles:
    def __init__(self):
        self.lane = iota((16, LANES), 1)
        row = iota((16, LANES), 0)
        self.ring_row = (row >= 3) & (row < 13)
        self.core_row = (row >= 4) & (row < 12)

    def put(self, field, row, column, pairs):
        row = pl.multiple_of(row, 8)
        block, offset = column >> 7, column & (LANES - 1)
        across = self.lane - offset
        ring = self.ring_row & (across >= 3) & (across < 13)
        core = self.core_row & (across >= 4) & (across < 12)
        for plane, line in pairs:
            values = jnp.broadcast_to(line, (8, LANES))
            values = pltpu.roll(values, 0, 1, stride=10, stride_axis=0)
            tile = jnp.concatenate(
                [
                    pltpu.roll(values, (offset + 11) & (LANES - 1), 1),
                    pltpu.roll(values, (offset + 91) & (LANES - 1), 1),
                ],
                axis=0,
            )
            now = field[plane, block, pl.ds(row, 16), :]
            field[plane, block, pl.ds(row, 16), :] = jnp.where(core, 0.0, now) + jnp.where(ring, tile, 0.0)


def listed(box_list, row_of, found):
    def step(patch, count):
        row, keep = row_of(box_list[0, patch], box_list[1, patch])
        found[0, count] = row
        found[1, count] = box_list[2, patch] - 4
        found[2, count] = patch
        return count + jnp.where(keep, 1, 0)

    return lax.fori_loop(0, box_list.shape[1], step, jnp.zeros((), I32), unroll=8)


def down_kernel(
    boxes, slabs, n0, x0,
    box_list, coarse, x_low, x_high, packed,
    f_own, c1, c2, up, down, third_up, third_down,
    fb, vb, g1, v1, summed0, summed1, found, owned, sem, out_sem,
):
    edges = Edges(boxes, slabs)
    rows0, rows1, rows2 = x0 + 2 * HX, x0 // 2 + HX, x0 // 4 + HX // 2
    n1, n2 = n0 // 2, n0 // 4
    copies = (
        block_copies(x_low, fb, (2, n0), 8, HX, sem.at[0])
        + block_copies(coarse, fb, (2, n0), 8 + HX, x0, sem.at[1])
        + block_copies(x_high, fb, (2, n0), 8 + HX + x0, HX, sem.at[2])
    )
    for copy in copies:
        copy.start()

    def near_row(owner, x):
        row = (owner - edges.box) * x0 + x - 4 + HX
        return row + 8, (row >= 0) & (row < rows0)

    def own_row(owner, x):
        return x, owner == edges.box

    near_count = listed(box_list, near_row, found)
    own_count = listed(box_list, own_row, owned)
    for copy in copies:
        copy.wait()
    tiles = Tiles()

    def place(index):
        patch = found[2, index]
        lines = [(2 + z, packed[pl.ds(patch * n0 + z, 1), :]) for z in range(n0)]
        tiles.put(fb, found[0, index], found[1, index], lines)

    lax.fori_loop(0, near_count, lambda index, carry: place(index) or carry, 0)

    inner = pl.ds(8 + HX - HU, x0 + 2 * HU)
    out_copy = pltpu.make_async_copy(fb.at[pl.ds(2, n0), :, inner, :], f_own, out_sem)
    out_copy.start()

    relax(vb, 3, (-1, n0 + 1), fb, 2, rows0, HX, edges, n0, s_planes=(0, n0), unroll=2)

    h1 = HX // 2

    def store1(index, group, value):
        value = value * edges.planes(index - 1, n1)
        g1[index + 3, group, 8 : 8 + h1, :] = value[:h1] * edges.low()
        g1[index + 3, group, 8 + h1 : 8 + rows1 - h1, :] = value[h1 : rows1 - h1]
        g1[index + 3, group, 8 + rows1 - h1 : 8 + rows1, :] = value[rows1 - h1 :] * edges.high()

    restrict(fb, 2, vb, 3, (-1, n1 + 1), rows0, summed0, store1, v_planes=(-1, n0 + 1), s_planes=(0, n0))
    for plane in range(n1 + 2):
        for b in range(g1.shape[1]):
            c1[plane, b] = g1[plane + 3, b, 8 + h1 - HU : 8 + rows1 - h1 + HU, :]

    relax(v1, 5, (-2, n1 + 2), g1, 4, rows1, h1, edges, n1, s_planes=(-1, n1 + 1))

    h2 = HX // 4

    def store2(index, group, value):
        c2[index, group, 0:h2, :] = value[:h2] * edges.low()
        c2[index, group, h2 : rows2 - h2, :] = value[h2 : rows2 - h2]
        c2[index, group, rows2 - h2 : rows2, :] = value[rows2 - h2 :] * edges.high()

    restrict(g1, 4, v1, 5, (-2, n2 + 2), rows1, summed1, store2, v_planes=(-2, n1 + 2), s_planes=(-1, n1 + 1))

    r1 = c1.shape[2]
    for target, fine_plane, coarse_first in ((up, n1 + 1, n2 + 2), (down, 0, 0)):
        target[0:rows2] = c2[coarse_first, 0]
        target[rows2 : 2 * rows2] = c2[coarse_first + 1, 0]
        for b in range(c1.shape[1]):
            first = 2 * rows2 + b * r1
            target[first : first + r1] = c1[fine_plane, b]

    rim = 2 * rows2 + c1.shape[1] * r1
    slots = (up.shape[0] - rim) // 2 - 8 * fb.shape[1]
    wide = third_up.shape[0] // fb.shape[1]
    for b in range(fb.shape[1]):
        at = slice(4 + HX, 4 + HX + wide)
        third_up[wide * b : wide * (b + 1)] = fb[n0 - 1, b, at, :]
        third_down[wide * b : wide * (b + 1)] = fb[4, b, at, :]
        for z in range(2):
            first = rim + 8 * (fb.shape[1] * z + b)
            for target, plane in ((up, n0 + z), (down, 2 + z)):
                target[first : first + 3, :] = fb[plane, b, 8 + HX - 3 : 8 + HX, :]
                target[first + 3 : first + 6, :] = fb[plane, b, 8 + HX + x0 : 8 + HX + x0 + 3, :]
                target[first + 6 : first + 8, :] = jnp.zeros((2, LANES), F32)
    rim = rim + 16 * fb.shape[1]
    up[rim:, :] = jnp.zeros((2 * slots, LANES), F32)
    down[rim:, :] = jnp.zeros((2 * slots, LANES), F32)

    def keep(slot):
        patch = owned[2, slot]
        for z in range(2):
            up[pl.ds(rim + z * slots + slot, 1), :] = packed[pl.ds(patch * n0 + n0 - 2 + z, 1), :]
            down[pl.ds(rim + z * slots + slot, 1), :] = packed[pl.ds(patch * n0 + z, 1), :]

    lax.fori_loop(0, own_count, lambda index, carry: keep(index) or carry, 0)
    out_copy.wait()


def total_kernel(c2, below, above, copies):
    n2, rows2 = c2.shape[0] - 4, c2.shape[2]
    for plane in range(n2):
        value = c2[2 + plane, 0]
        if plane < 2:
            value = value + below[plane * rows2 : (plane + 1) * rows2]
        if plane >= n2 - 2:
            first = (plane - (n2 - 2)) * rows2
            value = value + above[first : first + rows2]
        for slab in range(copies.shape[0]):
            copies[slab, plane * rows2 : (plane + 1) * rows2] = value


def join_kernel(rows2, c1, below, above, third_up, third_down, s1, up, down):
    n1, r1 = s1.shape[0], c1.shape[2]
    for plane in range(n1):
        s1[plane] = c1[1 + plane]
    for b in range(s1.shape[1]):
        first = 2 * rows2 + b * r1
        s1[0, b] = s1[0, b] + below[first : first + r1]
        s1[n1 - 1, b] = s1[n1 - 1, b] + above[first : first + r1]
    near = r1 - HU
    for p in range(4):
        for b in range(s1.shape[1]):
            first = near * (p * s1.shape[1] + b)
            up[first : first + near] = s1[n1 - 4 + p, b, HU // 2 : HU // 2 + near, :]
            down[first : first + near] = s1[p, b, HU // 2 : HU // 2 + near, :]
    first = near * 4 * s1.shape[1]
    up[first:] = third_up[...]
    down[first:] = third_down[...]


def third_kernel(boxes, slabs, s2, s3, fb, vb, summed):
    edges = Edges(boxes, slabs)
    planes, rows = s2.shape[0], s2.shape[1]
    zero(fb, (0, planes + 1))
    zero(vb, (0, planes + 1))
    for plane in range(planes):
        fb[plane + 1, 0, 8 : 8 + rows, :] = s2[plane]
    relax(vb, 1, (0, planes), fb, 1, rows, HX // 4, edges, None, chunk=32)
    quarter = planes // 4
    h3 = HX // 8
    own = rows // 2 - 2 * h3
    lanes = LANES // 2

    for part in range(2):

        def store(index, group, value, part=part):
            s3[index, :, lanes * part : lanes * (part + 1)] = value[h3 : h3 + own]

        restrict(fb, 1, vb, 1, (quarter * part, quarter * (part + 1)), rows, summed, store)


def coarse_levels(
    edges, boxes, slabs, s3, s2, s1, below, above, e1,
    sc, va3, vb3, e3p, f2, v2a, v2b, e2p, f1, v1a, v1b,
):
    slab = edges.slab
    half, rows3 = sc.shape[0], sc.shape[2] - 16
    own3 = s3.shape[2]
    zero_rims(va3)
    zero_rims(vb3)
    for box in range(boxes):
        for plane in range(half):
            value = s3[box, plane]
            sc[plane, 0, 8 + box * own3 : 8 + (box + 1) * own3, :] = value
            va3[plane, 0, 8 + box * own3 : 8 + (box + 1) * own3, :] = C * value

    def coarsest(old, new):
        chunk = 16
        lane = iota((chunk, LANES), 1)
        for row in range(0, rows3, chunk):
            inner = slice(row + 8, row + 8 + chunk)
            for plane in range(half):
                middle = old[plane, 0, inner, :]
                before = jnp.where((lane & 63) == 0, 0.0, pltpu.roll(middle, 1, 1))
                after = jnp.where((lane & 63) == 63, 0.0, pltpu.roll(middle, LANES - 1, 1))
                if plane > 0:
                    lower = old[plane - 1, 0, inner, :]
                else:
                    lower = jnp.where(lane < 64, 0.0, pltpu.roll(old[half - 1, 0, inner, :], 64, 1))
                if plane < half - 1:
                    upper = old[plane + 1, 0, inner, :]
                else:
                    upper = jnp.where(lane < 64, pltpu.roll(old[0, 0, inner, :], 64, 1), 0.0)
                beside = old[plane, 0, row + 7 : row + 7 + chunk, :] + old[plane, 0, row + 9 : row + 9 + chunk, :]
                near = beside + ((before + after) + (lower + upper))
                new[plane, 0, inner, :] = (1.0 - OMEGA) * middle + C * (sc[plane, 0, inner, :] + near)

    def double(index):
        coarsest(va3, vb3)
        coarsest(vb3, va3)

    each((CSWEEPS - 1) // 2, double)
    coarsest(va3, vb3)

    n2, rows2 = s2.shape[0] // slabs, s2.shape[1]
    n3 = n2 // 2
    shape = (LANES, LANES)
    copy_low = (iota(shape, 0) == (iota(shape, 1) >> 1)).astype(F32)
    copy_high = (iota(shape, 0) == (iota(shape, 1) >> 1) + 64).astype(F32)
    total3 = 2 * half
    h3 = HX // 8
    window = pl.multiple_of(edges.box * own3, 8)
    for k in range(-2, n3 + 2):
        plane = slab * n3 + k
        inside = (plane >= 0) & (plane < total3)
        safe = jnp.clip(plane, 0, total3 - 1)
        upper = safe >= half
        matrix = jnp.where(upper, copy_high, copy_low) * jnp.where(inside, 1.0, 0.0)
        value = vb3[jnp.where(upper, safe - half, safe), 0, pl.ds(window, own3 + 16), :]
        value = select_dot(value, matrix.astype(BF16))[8 - h3 : 8 + own3 + h3]
        e3p[k + 2, pl.ds(0, own3 + 2 * h3, stride=2), :] = value
        e3p[k + 2, pl.ds(1, own3 + 2 * h3, stride=2), :] = value

    planes2 = s2.shape[0]
    for p in range(-5, n2 + 5):
        plane = slab * n2 + p
        inside = jnp.where((plane >= 0) & (plane < planes2), 1.0, 0.0)
        f2[p + 5, 0, 8 : 8 + rows2, :] = s2[jnp.clip(plane, 0, planes2 - 1)] * inside

    def extra2(index, b, first, size):
        return e3p[index >> 1, first : first + size, :]

    h2 = HX // 4
    relax(v2a, 5, (-4, n2 + 4), f2, 5, rows2, h2, edges, n2, extra=extra2, chunk=32)
    relax(v2b, 5, (-3, n2 + 3), f2, 5, rows2, h2, edges, n2, old=v2a, ooff=5, chunk=32)
    relax(v2a, 5, (-2, n2 + 2), f2, 5, rows2, h2, edges, n2, old=v2b, ooff=5, chunk=32)

    n1, rows1 = s1.shape[0], s1.shape[2]
    cut = h2 - HU // 2
    matrix2 = copy_matrix(LANES)
    for k in range(-2, n2 + 2):
        value = select_dot(v2a[k + 5, 0, 8 + cut : 8 + rows2 - cut, :], matrix2)
        for b in range(2):
            part = value[:, LANES * b : LANES * (b + 1)]
            e2p[k + 2, b, pl.ds(0, rows2 - 2 * cut, stride=2), :] = part
            e2p[k + 2, b, pl.ds(1, rows2 - 2 * cut, stride=2), :] = part
    near = rows1 - HU
    inner = slice(8 + HU // 2, 8 + HU // 2 + near)
    for b in range(f1.shape[1]):
        for p in range(4):
            first = near * (p * f1.shape[1] + b)
            for plane, message in ((p, below), (4 + n1 + p, above)):
                f1[plane, b, inner, :] = message[first : first + near]
        for p in range(n1):
            f1[4 + p, b, 8 : 8 + rows1, :] = s1[p, b]

    def extra1(index, b, first, size):
        return e2p[(index + 1) >> 1, b, first : first + size, :]

    relax(v1a, 4, (-3, n1 + 3), f1, 4, rows1, HU, edges, n1, extra=extra1)
    relax(v1b, 4, (-2, n1 + 2), f1, 4, rows1, HU, edges, n1, old=v1a, ooff=4)
    relax(e1, 1, (-1, n1 + 1), f1, 4, rows1, HU, edges, n1, old=v1b, ooff=4, shift=0)


def early_kernel(
    boxes, slabs, n0, x0, rim,
    box_list, f_own, z_below, z_above, below, above,
    f_out, v_out,
    fb, va, found, sem, out_sem,
):
    edges = Edges(boxes, slabs)
    rows = x0 + 2 * HU
    copies = (
        [pltpu.make_async_copy(f_own, fb.at[pl.ds(2, n0), :, pl.ds(8, rows), :], sem.at[0])]
        + block_copies(z_below, fb, (0, 2), 8 + HU, x0, sem.at[1])
        + block_copies(z_above, fb, (2 + n0, 2), 8 + HU, x0, sem.at[2])
    )
    for copy in copies:
        copy.start()

    def own_row(owner, x):
        return x - 4 + HU + 8, owner == edges.box

    count = listed(box_list, own_row, found)
    packed = rim + 16 * fb.shape[1]
    slots = (below.shape[0] - packed) // 2
    for copy in copies:
        copy.wait()
    for z in range(2):
        for b in range(fb.shape[1]):
            at = rim + 8 * (fb.shape[1] * z + b)
            for plane, message in ((z, below), (2 + n0 + z, above)):
                fb[plane, b, 5 + HU : 8 + HU, :] = message[at : at + 3]
                fb[plane, b, 8 + HU + x0 : 11 + HU + x0, :] = message[at + 3 : at + 6]
    tiles = Tiles()

    def place(slot):
        lines = [(z, below, z) for z in range(2)] + [(2 + n0 + z, above, z) for z in range(2)]
        lines = [(plane, message[pl.ds(packed + z * slots + slot, 1), :]) for plane, message, z in lines]
        tiles.put(fb, found[0, slot], found[1, slot], lines)

    lax.fori_loop(0, count, lambda index, carry: place(index) or carry, 0)
    f_copy = pltpu.make_async_copy(fb.at[pl.ds(1, n0 + 2)], f_out, out_sem.at[0])
    f_copy.start()
    relax(va, 2, (-2, n0 + 2), fb, 2, rows, HU, edges, n0, s_planes=(-2, n0 + 2), unroll=2)
    v_copy = pltpu.make_async_copy(va, v_out, out_sem.at[1])
    v_copy.start()
    f_copy.wait()
    v_copy.wait()


def tail_kernel(
    boxes, slabs, n0, x0,
    s3, s2, s1, below, above, f_in, v_in,
    out,
    sc, va3, vb3, e3p, f2, v2a, v2b, e2p, f1, v1a, v1b, e1,
    fb, va, vb, ob, sem, out_sem,
):
    f_copy = pltpu.make_async_copy(f_in, fb, sem.at[0])
    v_copy = pltpu.make_async_copy(v_in, va.at[pl.ds(1, n0 + 4)], sem.at[1])
    f_copy.start()
    v_copy.start()
    edges = Edges(boxes, slabs)
    coarse_levels(
        edges, boxes, slabs, s3, s2, s1, below, above, e1,
        sc, va3, vb3, e3p, f2, v2a, v2b, e2p, f1, v1a, v1b,
    )
    f_copy.wait()
    v_copy.wait()
    rows = x0 + 2 * HU
    matrix = copy_matrix(LANES)
    cut = HU // 2
    r1 = e1.shape[2]
    size1 = r1 - 2 * cut
    first = 4 * s1.shape[1] * (r1 - HU)
    wide = (below.shape[0] - first) // fb.shape[1]
    for b in range(fb.shape[1]):
        at = slice(4 + HU, 4 + HU + wide)
        for plane, message in ((1, below), (4 + n0, above)):
            va[plane, b, at, :] = va[plane, b, at, :] + (C * C) * message[first + wide * b : first + wide * (b + 1)]

    def prolong(k):
        for group in range(e1.shape[1]):
            value = select_dot(e1[k, group, cut : r1 - cut, :], matrix)
            for b in range(2):
                part = value[:, LANES * b : LANES * (b + 1)]
                for plane in (2 * k + 1, 2 * k + 2):
                    for start in (8, 9):
                        at = pl.ds(start, size1, stride=2)
                        va[plane, 2 * group + b, at, :] = va[plane, 2 * group + b, at, :] + part

    each(e1.shape[0], prolong)
    relax(vb, 3, (-1, n0 + 1), fb, 1, rows, HU, edges, n0, old=va, ooff=3, unroll=2)

    def last(z):
        view = ob.at[pl.ds(z, 1)]
        relax(view, 0, (0, 1), fb.at[pl.ds(z + 1, 1)], 0, rows, HU, edges, None, old=vb.at[pl.ds(z + 2, 3)], ooff=1, shift=-HU, cut=1)
        for copy in block_copies(out.at[pl.ds(z, 1)], ob, (z, 1), 0, x0, out_sem, back=True):
            copy.start()

    each(n0, last, unroll=2)
    for copy in block_copies(out, ob, (0, n0), 0, x0, out_sem, back=True):
        copy.wait()


def shape_of(*dims):
    return jax.ShapeDtypeStruct(dims, F32)


def scratch(*dims):
    return pltpu.VMEM(dims, F32)


def in_hbm(array):
    return pltpu.with_memory_space_constraint(array, pltpu.MemorySpace.HBM)


def limit(mebibytes):
    return pltpu.CompilerParams(vmem_limit_bytes=mebibytes << 20)


def cost(flops, moved):
    return pl.CostEstimate(flops=flops, bytes_accessed=moved, transcendentals=0)


def shift_by(array, axis, step):
    size = lax.axis_size(axis)
    pairs = [(i, i + step) for i in range(size) if 0 <= i + step < size]
    return lax.ppermute(array, axis, pairs)


def per_device(coarse, fine_div, reflux, box_list, cf_mask):
    boxes, slabs = lax.axis_size("box"), lax.axis_size("gz")
    n0, x0, y0 = coarse.shape
    n1, n2 = n0 // 2, n0 // 4
    b0, b1 = y0 // LANES, y0 // LANES // 2
    patches, fine_z, fine_lanes = fine_div.shape
    rows0, rows1, rows2 = x0 + 2 * HX, x0 // 2 + HX, x0 // 4 + HX // 2
    up_rows0, up_rows1 = x0 + 2 * HU, x0 // 2 + 2 * HU
    dma = pltpu.SemaphoreType.DMA

    fine_blocks = fine_lanes // LANES
    packed, x_first, x_last, z_first, z_last = pl.pallas_call(
        pack_kernel,
        name="pack",
        out_shape=(
            shape_of(patches * n0, LANES),
            shape_of(n0, HX, y0),
            shape_of(n0, HX, y0),
            shape_of(2, x0, y0),
            shape_of(2, x0, y0),
        ),
        in_specs=[SM, HBM, HBM, HBM],
        out_specs=(VM,) * 5,
        scratch_shapes=[
            scratch(fine_blocks, patches, fine_z, LANES),
            scratch(patches, fine_z, LANES),
            dma((fine_blocks + 1,)),
            dma((4,)),
        ],
        compiler_params=limit(4),
        cost_estimate=cost(10**7, 10**6),
    )(in_hbm(cf_mask.T), in_hbm(fine_div), in_hbm(reflux), in_hbm(coarse))
    z_below = shift_by(z_last, "gz", 1)
    z_above = shift_by(z_first, "gz", -1)
    x_low = shift_by(x_last, "box", 1)
    x_high = shift_by(x_first, "box", -1)
    packed = lax.all_gather(packed, "box", axis=0, tiled=True)

    slots = boxes * max(2, patches // 4)
    rim = 2 * rows2 + b1 * up_rows1
    message = rim + 2 * (8 * b0 + slots)
    f_own, c1, c2, up, down, third_up, third_down = pl.pallas_call(
        functools.partial(down_kernel, boxes, slabs, n0, x0),
        name="down",
        out_shape=(
            pltpu.MemorySpace.HBM((n0, b0, up_rows0, LANES), F32),
            shape_of(n1 + 2, b1, up_rows1, LANES),
            shape_of(n2 + 4, 1, rows2, LANES),
            shape_of(message, LANES),
            shape_of(message, LANES),
            shape_of(b0 * (x0 + HU), LANES),
            shape_of(b0 * (x0 + HU), LANES),
        ),
        in_specs=[SM, HBM, HBM, HBM, VM],
        out_specs=(HBM,) + (VM,) * 6,
        scratch_shapes=[
            scratch(n0 + 4, b0, rows0 + 16, LANES),
            scratch(n0 + 6, b0, rows0 + 16, LANES),
            scratch(n1 + 8, b1, rows1 + 16, LANES),
            scratch(n1 + 10, b1, rows1 + 16, LANES),
            scratch(b0 // 2, rows1, 2 * LANES),
            scratch(max(1, b1 // 2), rows2, min(2, b1) * LANES),
            pltpu.SMEM((3, box_list.shape[0]), I32),
            pltpu.SMEM((3, box_list.shape[0]), I32),
            dma((3,)),
            dma(()),
        ],
        compiler_params=limit(20),
        cost_estimate=cost(3 * 10**7, 10**7),
    )(in_hbm(box_list.T), in_hbm(coarse), x_low, x_high, packed)

    from_below = shift_by(up, "gz", 1)
    from_above = shift_by(down, "gz", -1)
    copies = pl.pallas_call(
        total_kernel,
        name="total",
        out_shape=shape_of(slabs, n2 * rows2, LANES),
        in_specs=[VM] * 3,
        out_specs=VM,
        compiler_params=limit(3),
        cost_estimate=cost(10**6, 10**6),
    )(c2, from_below, from_above)
    s2 = lax.all_to_all(copies, "gz", split_axis=0, concat_axis=0, tiled=True)
    s2 = s2.reshape(slabs * n2, rows2, LANES)
    last = 4 * b1 * (up_rows1 - HU) + b0 * (x0 + HU)
    s1, up, down = pl.pallas_call(
        functools.partial(join_kernel, rows2),
        name="join",
        out_shape=(shape_of(n1, b1, up_rows1, LANES), shape_of(last, LANES), shape_of(last, LANES)),
        in_specs=[VM] * 5,
        out_specs=(VM,) * 3,
        compiler_params=limit(5),
        cost_estimate=cost(10**6, 10**6),
    )(c1, from_below, from_above, third_up, third_down)
    below = shift_by(up, "gz", 1)
    above = shift_by(down, "gz", -1)

    hbm = pltpu.MemorySpace.HBM
    f_wide, v_wide = pl.pallas_call(
        functools.partial(early_kernel, boxes, slabs, n0, x0, rim),
        name="early",
        out_shape=(
            hbm((n0 + 2, b0, up_rows0 + 16, LANES), F32),
            hbm((n0 + 4, b0, up_rows0 + 16, LANES), F32),
        ),
        in_specs=[SM, HBM, HBM, HBM, VM, VM],
        out_specs=(HBM, HBM),
        scratch_shapes=[
            scratch(n0 + 4, b0, up_rows0 + 16, LANES),
            scratch(n0 + 4, b0, up_rows0 + 16, LANES),
            pltpu.SMEM((3, box_list.shape[0]), I32),
            dma((3,)),
            dma((2,)),
        ],
        compiler_params=limit(14),
        cost_estimate=cost(2 * 10**7, 10**7),
    )(in_hbm(box_list.T), in_hbm(f_own), in_hbm(z_below), in_hbm(z_above), from_below, from_above)

    planes2, half = slabs * n2, slabs * n2 // 4
    own3 = x0 // 8
    s3 = pl.pallas_call(
        functools.partial(third_kernel, boxes, slabs),
        name="third",
        out_shape=shape_of(half, own3, LANES),
        in_specs=[VM],
        out_specs=VM,
        scratch_shapes=[scratch(planes2 + 2, 1, rows2 + 16, LANES)] * 2 + [scratch(1, rows2 // 2, LANES)],
        compiler_params=limit(4),
        cost_estimate=cost(10**6, 10**6),
    )(s2)
    s3 = lax.all_gather(s3, "box", axis=0)
    rows3 = boxes * own3
    return pl.pallas_call(
        functools.partial(tail_kernel, boxes, slabs, n0, x0),
        name="tail",
        out_shape=shape_of(n0, x0, y0),
        in_specs=[VM] * 5 + [HBM, HBM],
        out_specs=HBM,
        scratch_shapes=[scratch(half, 1, rows3 + 16, LANES)] * 3
        + [scratch(n2 // 2 + 4, rows2, LANES)]
        + [scratch(n2 + 10, 1, rows2 + 16, LANES)] * 3
        + [scratch(n2 + 4, 2, up_rows1, LANES)]
        + [scratch(n1 + 8, b1, up_rows1 + 16, LANES)] * 3
        + [scratch(n1 + 2, b1, up_rows1, LANES)]
        + [scratch(n0 + 2, b0, up_rows0 + 16, LANES)]
        + [scratch(n0 + 6, b0, up_rows0 + 16, LANES)] * 2
        + [scratch(n0, b0, x0, LANES), dma((2,)), dma(())],
        compiler_params=limit(28),
        cost_estimate=cost(4 * 10**7, 10**7),
    )(s3, s2, s1, below, above, in_hbm(f_wide), in_hbm(v_wide))


def solution(mesh):
    return jax.shard_map(
        per_device,
        mesh=mesh,
        in_specs=(P("gz", "box", None), P("box", "gz", None), P("box", "gz", None), P(), P()),
        out_specs=P("gz", "box", None),
        check_vma=False,
    )
```

```python
import functools

import jax
import jax.numpy as jnp
from jax import lax
from jax.experimental import pallas as pl
from jax.experimental.pallas import tpu as pltpu
from jax.sharding import PartitionSpec as P


CSWEEPS = 16
OMEGA = 0.8
C = OMEGA / 6.0
HX = 32
HU = 8
LANES = 128
F32 = jnp.float32
BF16 = jnp.bfloat16
I32 = jnp.int32

VM = pl.BlockSpec(memory_space=pltpu.VMEM)
SM = pl.BlockSpec(memory_space=pltpu.SMEM)
HBM = pl.BlockSpec(memory_space=pltpu.MemorySpace.HBM)


def iota(shape, dim):
    return lax.broadcasted_iota(I32, shape, dim)


def as_matrix(condition):
    return condition.astype(F32).astype(BF16)


def pair_matrix(length):
    shape = (length, length // 2)
    return as_matrix((iota(shape, 0) >> 1) == iota(shape, 1))


def copy_matrix(length):
    shape = (length, 2 * length)
    return as_matrix(iota(shape, 0) == (iota(shape, 1) >> 1))


def select_dot(values, matrix):
    high = values.astype(BF16)
    low = (values - high.astype(F32)).astype(BF16)
    return jnp.dot(high, matrix, preferred_element_type=F32) + jnp.dot(
        low, matrix, preferred_element_type=F32
    )


def each(count, body, unroll=1):
    def step(index, carry):
        body(index)
        return carry

    lax.fori_loop(0, count, step, 0, unroll=unroll)


def beside_lanes(blocks):
    lane = iota(blocks[0].shape, 1)
    right = [pltpu.roll(block, 1, 1) for block in blocks]
    left = [pltpu.roll(block, LANES - 1, 1) for block in blocks]
    sums = []
    for b in range(len(blocks)):
        before = right[b - 1] if b > 0 else 0.0
        after = left[b + 1] if b + 1 < len(blocks) else 0.0
        sums.append(
            jnp.where(lane == 0, before, right[b]) + jnp.where(lane == LANES - 1, after, left[b])
        )
    return sums


def around(field, plane, row, rows, has=(True, True, True)):
    count = field.shape[1]

    def at(p, first):
        return [field[p, b, first : first + rows, :] for b in range(count)]

    sides = [at(plane + p, row + 8) for p in (-1, 1) if has[p + 1]]
    if not has[1]:
        return None, sides[0]
    middle = at(plane, row + 8)
    beside = zip(at(plane, row + 7), at(plane, row + 9), beside_lanes(middle))
    near = [(a + b) + c for a, b, c in beside]
    for side in sides:
        near = [a + b for a, b in zip(near, side)]
    return middle, near


class Edges:
    def __init__(self, boxes, slabs):
        self.box, self.slab = lax.axis_index("box"), lax.axis_index("gz")
        self.boxes, self.slabs = boxes, slabs

    def planes(self, plane, count):
        outside = ((plane < 0) & (self.slab == 0)) | ((plane >= count) & (self.slab == self.slabs - 1))
        return jnp.where(outside, 0.0, 1.0).astype(F32)

    def low(self):
        return jnp.where(self.box == 0, 0.0, 1.0).astype(F32)

    def high(self):
        return jnp.where(self.box == self.boxes - 1, 0.0, 1.0).astype(F32)


def chunks_of(rows, halo, chunk, cut=0):
    out = [] if cut else [(0, halo, -1)]
    inner = (halo, rows - halo)
    for first in range(inner[0], inner[1], chunk):
        out.append((first, min(chunk, inner[1] - first), 0))
    return out if cut else out + [(rows - halo, halo, 1)]


def scale_of(side, edges, plane_scale):
    if side == 0:
        return plane_scale
    row_scale = edges.low() if side < 0 else edges.high()
    return row_scale if plane_scale is None else row_scale * plane_scale


def relax(new, noff, planes, source, soff, rows, halo, edges, count, old=None, ooff=0, extra=None, chunk=16, shift=8, cut=0, s_planes=None, unroll=1):
    def body(index, has=(True, True, True)):
        plane_scale = None if count is None else edges.planes(index + planes[0], count)
        for first, size, side in chunks_of(rows, halo, chunk, cut):
            scale = scale_of(side, edges, plane_scale)
            if old is None:
                middle, near = around(source, index + (planes[0] + soff), first, size, has)
                values = [(C * C) * n for n in near]
                if middle is not None:
                    values = [(1.2 * C) * m + v for m, v in zip(middle, values)]
                if extra is not None:
                    values = [v + extra(index, b, first, size) for b, v in enumerate(values)]
            else:
                middle, near = around(old, index + (planes[0] + ooff), first, size)
                at = index + (planes[0] + soff)
                values = [
                    (1.0 - OMEGA) * m + C * (source[at, b, first + 8 : first + 8 + size, :] + n)
                    for b, (m, n) in enumerate(zip(middle, near))
                ]
            for b, value in enumerate(values):
                if scale is not None:
                    value = value * scale
                new[index + (planes[0] + noff), b, first + shift : first + shift + size, :] = value

    if s_planes is None:
        each(planes[1] - planes[0], body, unroll)
        return
    inner = []
    for plane in range(*planes):
        has = tuple(s_planes[0] <= plane + p < s_planes[1] for p in (-1, 0, 1))
        if all(has):
            inner.append(plane)
        else:
            body(plane - planes[0], has)
    if inner:
        first = inner[0] - planes[0]
        each(len(inner), lambda index: body(index + first), unroll)


def restrict(source, soff, v, voff, pairs, rows, summed, store, chunk=8, v_planes=None, s_planes=None):
    count = v.shape[1]
    width = min(2, count)
    half = rows // 2

    def body(index, has_v=(True,) * 4, has_s=(True,) * 2):
        low_v, low_s = 2 * index + (2 * pairs[0] + voff), 2 * index + (2 * pairs[0] + soff)
        matrix = pair_matrix(width * LANES)
        for first in range(0, half, chunk):
            size = min(chunk, half - first)

            def at(field, plane, b, offset):
                return field[plane, b, pl.ds(8 + 2 * first + offset, size, stride=2), :]

            def both(field, plane, b):
                return at(field, plane, b, 0) + at(field, plane, b, 1)

            def total_of(terms):
                total = terms[0]
                for term in terms[1:]:
                    total = total + term
                return total

            inside = [p for p in (1, 2) if has_v[p]]
            sums = []
            if inside:
                whole = [total_of([both(v, low_v + p - 1, b) for p in inside]) for b in range(count)]
                near = beside_lanes(whole)
            for b in range(count):
                terms = []
                if inside:
                    terms.append(near[b] - 4.0 * whole[b])
                    terms += [at(v, low_v + p - 1, b, -1) + at(v, low_v + p - 1, b, 2) for p in inside]
                terms += [both(source, low_s + p, b) for p in (0, 1) if has_s[p]]
                terms += [both(v, low_v + p - 1, b) for p in (0, 3) if has_v[p]]
                sums.append(total_of(terms))
            for b in range(count):
                summed[b // width, first : first + size, LANES * (b % width) : LANES * (b % width + 1)] = sums[b]
        for group in range(count // width):
            store(index, group, 0.5 * select_dot(summed[group], matrix))

    if v_planes is None:
        each(pairs[1] - pairs[0], body)
        return
    inner = []
    for coarse in range(*pairs):
        has_v = tuple(v_planes[0] <= 2 * coarse + p - 1 < v_planes[1] for p in range(4))
        has_s = tuple(s_planes[0] <= 2 * coarse + p < s_planes[1] for p in range(2))
        if all(has_v + has_s):
            inner.append(coarse)
        else:
            body(coarse - pairs[0], has_v, has_s)
    if inner:
        first = inner[0] - pairs[0]
        each(len(inner), lambda index: body(index + first))


def zero(ref, planes):
    for plane in planes:
        ref[plane] = jnp.zeros(ref.shape[1:], F32)


def zero_rims(ref, planes=None):
    rows = ref.shape[2]
    for plane in range(ref.shape[0]) if planes is None else planes:
        for b in range(ref.shape[1]):
            ref[plane, b, 0:8, :] = jnp.zeros((8, LANES), F32)
            ref[plane, b, rows - 8 : rows, :] = jnp.zeros((8, LANES), F32)


def block_copies(wide, tiled, planes, first, rows, sem, back=False):
    copies = []
    for b in range(tiled.shape[1]):
        pair = (
            wide.at[:, :, pl.ds(LANES * b, LANES)],
            tiled.at[pl.ds(planes[0], planes[1]), b, pl.ds(first, rows), :],
        )
        copies.append(pltpu.make_async_copy(*(pair[::-1] if back else pair), sem))
    return copies


def pack_kernel(
    mask_in, fine, flux, coarse, out, x_first, x_last, z_first, z_last, mask, fine_s, flux_s, sem, edge_sem
):
    patches, fine_z = fine.shape[0], fine.shape[1]
    n0 = fine_z // 2
    blocks = fine_s.shape[0]
    copies = [
        pltpu.make_async_copy(fine.at[:, :, pl.ds(LANES * b, LANES)], fine_s.at[b], sem.at[b])
        for b in range(blocks)
    ]
    copies.append(pltpu.make_async_copy(flux, flux_s, sem.at[blocks]))
    copies.append(pltpu.make_async_copy(mask_in, mask, sem.at[blocks + 1]))
    n, x = coarse.shape[0], coarse.shape[1]
    cuts = [
        pltpu.make_async_copy(coarse.at[pl.ds(n - 2, 2)], z_last, edge_sem.at[0]),
        pltpu.make_async_copy(coarse.at[pl.ds(0, 2)], z_first, edge_sem.at[1]),
        pltpu.make_async_copy(coarse.at[:, pl.ds(x - HX, HX), :], x_last, edge_sem.at[2]),
        pltpu.make_async_copy(coarse.at[:, pl.ds(0, HX), :], x_first, edge_sem.at[3]),
    ]
    for copy in copies + cuts:
        copy.start()
    base = lax.axis_index("box") * patches
    side = (iota((n0, LANES), 1) >> 4) & 3
    source, target = iota((LANES, LANES), 0), iota((LANES, LANES), 1)
    s, i = (source >> 4) & 3, (source & 15) >> 1
    goal = jnp.where(
        s == 0, i + 91, jnp.where(s == 1, i + 1, jnp.where(s == 2, 80 - 10 * i, 89 - 10 * i))
    )
    matrices = [as_matrix(goal == target)]
    for b in range(blocks):
        place = source + LANES * b
        goal = 10 * (8 - (place >> 5)) + ((place & 15) >> 1) + 1
        matrices.append(as_matrix(goal == target))
    for copy in copies:
        copy.wait()
    masked, fine_rows = [], [[] for _ in range(blocks)]
    for patch in range(patches):
        m = [mask[s, base + patch].astype(F32) for s in range(4)]
        factor = jnp.where(side == 0, m[0], jnp.where(side == 1, m[1], jnp.where(side == 2, m[2], m[3])))
        masked.append(
            (flux_s[patch, pl.ds(0, n0, stride=2), :] + flux_s[patch, pl.ds(1, n0, stride=2), :]) * factor
        )
        for b in range(blocks):
            fine_rows[b].append(
                fine_s[b, patch, pl.ds(0, n0, stride=2), :] + fine_s[b, patch, pl.ds(1, n0, stride=2), :]
            )
    total = select_dot(jnp.concatenate(masked, axis=0), matrices[0])
    for b in range(blocks):
        total = total + select_dot(jnp.concatenate(fine_rows[b], axis=0), matrices[b + 1])
    out[...] = 0.125 * total
    for cut in cuts:
        cut.wait()


class Tiles:
    def __init__(self):
        self.lane = iota((16, LANES), 1)
        row = iota((16, LANES), 0)
        self.ring_row = (row >= 3) & (row < 13)
        self.core_row = (row >= 4) & (row < 12)

    def put(self, field, row, column, pairs):
        row = pl.multiple_of(row, 8)
        block, offset = column >> 7, column & (LANES - 1)
        across = self.lane - offset
        ring = self.ring_row & (across >= 3) & (across < 13)
        core = self.core_row & (across >= 4) & (across < 12)
        for plane, line in pairs:
            values = jnp.broadcast_to(line, (8, LANES))
            values = pltpu.roll(values, 0, 1, stride=10, stride_axis=0)
            tile = jnp.concatenate(
                [
                    pltpu.roll(values, (offset + 11) & (LANES - 1), 1),
                    pltpu.roll(values, (offset + 91) & (LANES - 1), 1),
                ],
                axis=0,
            )
            now = field[plane, block, pl.ds(row, 16), :]
            field[plane, block, pl.ds(row, 16), :] = jnp.where(core, 0.0, now) + jnp.where(ring, tile, 0.0)


def listed(box_list, row_of, found):
    def step(patch, count):
        row, keep = row_of(box_list[0, patch], box_list[1, patch])
        found[0, count] = row
        found[1, count] = box_list[2, patch] - 4
        found[2, count] = patch
        return count + jnp.where(keep, 1, 0)

    return lax.fori_loop(0, box_list.shape[1], step, jnp.zeros((), I32), unroll=8)


def down_kernel(
    boxes, slabs, n0, x0,
    box_list, coarse, x_low, x_high, packed,
    f_own, v_own, c1, c2, up, down, third_up, third_down,
    fb, vb, g1, v1, summed0, summed1, patches, found, owned, sem, out_sem,
):
    edges = Edges(boxes, slabs)
    rows0, rows1, rows2 = x0 + 2 * HX, x0 // 2 + HX, x0 // 4 + HX // 2
    n1, n2 = n0 // 2, n0 // 4
    copies = (
        block_copies(x_low, fb, (2, n0), 8, HX, sem.at[0])
        + block_copies(coarse, fb, (2, n0), 8 + HX, x0, sem.at[1])
        + block_copies(x_high, fb, (2, n0), 8 + HX + x0, HX, sem.at[2])
    )
    fetch = pltpu.make_async_copy(box_list, patches, sem.at[3])
    fetch.start()
    for copy in copies:
        copy.start()
    fetch.wait()

    def near_row(owner, x):
        row = (owner - edges.box) * x0 + x - 4 + HX
        return row + 8, (row >= 0) & (row < rows0)

    def own_row(owner, x):
        return x, owner == edges.box

    near_count = listed(patches, near_row, found)
    own_count = listed(patches, own_row, owned)
    for copy in copies:
        copy.wait()
    tiles = Tiles()

    def place(index):
        patch = found[2, index]
        lines = [(2 + z, packed[pl.ds(patch * n0 + z, 1), :]) for z in range(n0)]
        tiles.put(fb, found[0, index], found[1, index], lines)

    lax.fori_loop(0, near_count, lambda index, carry: place(index) or carry, 0)

    inner = pl.ds(8 + HX - HU, x0 + 2 * HU)
    f_copy = pltpu.make_async_copy(fb.at[pl.ds(2, n0), :, inner, :], f_own, out_sem.at[0])
    f_copy.start()

    relax(vb, 3, (-1, n0 + 1), fb, 2, rows0, HX, edges, n0, s_planes=(0, n0), unroll=2)
    v_copy = pltpu.make_async_copy(vb.at[pl.ds(4, n0 - 2), :, inner, :], v_own, out_sem.at[1])
    v_copy.start()

    h1 = HX // 2

    def store1(index, group, value):
        value = value * edges.planes(index - 1, n1)
        g1[index + 3, group, 8 : 8 + h1, :] = value[:h1] * edges.low()
        g1[index + 3, group, 8 + h1 : 8 + rows1 - h1, :] = value[h1 : rows1 - h1]
        g1[index + 3, group, 8 + rows1 - h1 : 8 + rows1, :] = value[rows1 - h1 :] * edges.high()

    restrict(fb, 2, vb, 3, (-1, n1 + 1), rows0, summed0, store1, v_planes=(-1, n0 + 1), s_planes=(0, n0))
    for plane in range(n1 + 2):
        for b in range(g1.shape[1]):
            c1[plane, b] = g1[plane + 3, b, 8 + h1 - HU : 8 + rows1 - h1 + HU, :]

    relax(v1, 5, (-2, n1 + 2), g1, 4, rows1, h1, edges, n1, s_planes=(-1, n1 + 1))

    h2 = HX // 4

    def store2(index, group, value):
        c2[index, group, 0:h2, :] = value[:h2] * edges.low()
        c2[index, group, h2 : rows2 - h2, :] = value[h2 : rows2 - h2]
        c2[index, group, rows2 - h2 : rows2, :] = value[rows2 - h2 :] * edges.high()

    restrict(g1, 4, v1, 5, (-2, n2 + 2), rows1, summed1, store2, v_planes=(-2, n1 + 2), s_planes=(-1, n1 + 1))

    r1 = c1.shape[2]
    for target, fine_plane, coarse_first in ((up, n1 + 1, n2 + 2), (down, 0, 0)):
        target[0:rows2] = c2[coarse_first, 0]
        target[rows2 : 2 * rows2] = c2[coarse_first + 1, 0]
        for b in range(c1.shape[1]):
            first = 2 * rows2 + b * r1
            target[first : first + r1] = c1[fine_plane, b]

    rim = 2 * rows2 + c1.shape[1] * r1
    slots = (up.shape[0] - rim) // 2 - 8 * fb.shape[1]
    wide = third_up.shape[0] // fb.shape[1]
    for b in range(fb.shape[1]):
        at = slice(4 + HX, 4 + HX + wide)
        third_up[wide * b : wide * (b + 1)] = fb[n0 - 1, b, at, :]
        third_down[wide * b : wide * (b + 1)] = fb[4, b, at, :]
        for z in range(2):
            first = rim + 8 * (fb.shape[1] * z + b)
            for target, plane in ((up, n0 + z), (down, 2 + z)):
                target[first : first + 3, :] = fb[plane, b, 8 + HX - 3 : 8 + HX, :]
                target[first + 3 : first + 6, :] = fb[plane, b, 8 + HX + x0 : 8 + HX + x0 + 3, :]
                target[first + 6 : first + 8, :] = jnp.zeros((2, LANES), F32)
    rim = rim + 16 * fb.shape[1]
    up[rim:, :] = jnp.zeros((2 * slots, LANES), F32)
    down[rim:, :] = jnp.zeros((2 * slots, LANES), F32)

    def keep(slot):
        patch = owned[2, slot]
        for z in range(2):
            up[pl.ds(rim + z * slots + slot, 1), :] = packed[pl.ds(patch * n0 + n0 - 2 + z, 1), :]
            down[pl.ds(rim + z * slots + slot, 1), :] = packed[pl.ds(patch * n0 + z, 1), :]

    lax.fori_loop(0, own_count, lambda index, carry: keep(index) or carry, 0)
    f_copy.wait()
    v_copy.wait()


def total_kernel(c2, below, above, copies):
    n2, rows2 = c2.shape[0] - 4, c2.shape[2]
    for plane in range(n2):
        value = c2[2 + plane, 0]
        if plane < 2:
            value = value + below[plane * rows2 : (plane + 1) * rows2]
        if plane >= n2 - 2:
            first = (plane - (n2 - 2)) * rows2
            value = value + above[first : first + rows2]
        for slab in range(copies.shape[0]):
            copies[slab, plane * rows2 : (plane + 1) * rows2] = value


def join_kernel(rows2, c1, below, above, third_up, third_down, s1, up, down):
    n1, r1 = s1.shape[0], c1.shape[2]
    for plane in range(n1):
        s1[plane] = c1[1 + plane]
    for b in range(s1.shape[1]):
        first = 2 * rows2 + b * r1
        s1[0, b] = s1[0, b] + below[first : first + r1]
        s1[n1 - 1, b] = s1[n1 - 1, b] + above[first : first + r1]
    near = r1 - HU
    for p in range(4):
        for b in range(s1.shape[1]):
            first = near * (p * s1.shape[1] + b)
            up[first : first + near] = s1[n1 - 4 + p, b, HU // 2 : HU // 2 + near, :]
            down[first : first + near] = s1[p, b, HU // 2 : HU // 2 + near, :]
    first = near * 4 * s1.shape[1]
    up[first:] = third_up[...]
    down[first:] = third_down[...]


def third_kernel(boxes, slabs, s2, s3, fb, vb, summed):
    edges = Edges(boxes, slabs)
    planes, rows = s2.shape[0], s2.shape[1]
    zero(fb, (0, planes + 1))
    zero(vb, (0, planes + 1))
    for plane in range(planes):
        fb[plane + 1, 0, 8 : 8 + rows, :] = s2[plane]
    relax(vb, 1, (0, planes), fb, 1, rows, HX // 4, edges, None, chunk=32)
    quarter = planes // 4
    h3 = HX // 8
    own = rows // 2 - 2 * h3
    lanes = LANES // 2

    for part in range(2):

        def store(index, group, value, part=part):
            s3[index, :, lanes * part : lanes * (part + 1)] = value[h3 : h3 + own]

        restrict(fb, 1, vb, 1, (quarter * part, quarter * (part + 1)), rows, summed, store)


def middle_kernel(
    boxes, slabs,
    s3, s2,
    e2p,
    sc, va3, vb3, e3p, f2, v2a, v2b,
):
    edges = Edges(boxes, slabs)
    slab = edges.slab
    half, rows3 = sc.shape[0], sc.shape[2] - 16
    own3 = s3.shape[2]
    zero_rims(va3)
    zero_rims(vb3)
    for box in range(boxes):
        for plane in range(half):
            value = s3[box, plane]
            sc[plane, 0, 8 + box * own3 : 8 + (box + 1) * own3, :] = value
            va3[plane, 0, 8 + box * own3 : 8 + (box + 1) * own3, :] = C * value

    def coarsest(old, new):
        chunk = 16
        lane = iota((chunk, LANES), 1)
        for row in range(0, rows3, chunk):
            inner = slice(row + 8, row + 8 + chunk)
            for plane in range(half):
                middle = old[plane, 0, inner, :]
                before = jnp.where((lane & 63) == 0, 0.0, pltpu.roll(middle, 1, 1))
                after = jnp.where((lane & 63) == 63, 0.0, pltpu.roll(middle, LANES - 1, 1))
                if plane > 0:
                    lower = old[plane - 1, 0, inner, :]
                else:
                    lower = jnp.where(lane < 64, 0.0, pltpu.roll(old[half - 1, 0, inner, :], 64, 1))
                if plane < half - 1:
                    upper = old[plane + 1, 0, inner, :]
                else:
                    upper = jnp.where(lane < 64, pltpu.roll(old[0, 0, inner, :], 64, 1), 0.0)
                beside = old[plane, 0, row + 7 : row + 7 + chunk, :] + old[plane, 0, row + 9 : row + 9 + chunk, :]
                near = beside + ((before + after) + (lower + upper))
                new[plane, 0, inner, :] = (1.0 - OMEGA) * middle + C * (sc[plane, 0, inner, :] + near)

    def double(index):
        coarsest(va3, vb3)
        coarsest(vb3, va3)

    each((CSWEEPS - 1) // 2, double)
    coarsest(va3, vb3)

    n2, rows2 = s2.shape[0] // slabs, s2.shape[1]
    n3 = n2 // 2
    shape = (LANES, LANES)
    copy_low = (iota(shape, 0) == (iota(shape, 1) >> 1)).astype(F32)
    copy_high = (iota(shape, 0) == (iota(shape, 1) >> 1) + 64).astype(F32)
    total3 = 2 * half
    h3 = HX // 8
    window = pl.multiple_of(edges.box * own3, 8)
    for k in range(-2, n3 + 2):
        plane = slab * n3 + k
        inside = (plane >= 0) & (plane < total3)
        safe = jnp.clip(plane, 0, total3 - 1)
        upper = safe >= half
        matrix = jnp.where(upper, copy_high, copy_low) * jnp.where(inside, 1.0, 0.0)
        value = vb3[jnp.where(upper, safe - half, safe), 0, pl.ds(window, own3 + 16), :]
        value = select_dot(value, matrix.astype(BF16))[8 - h3 : 8 + own3 + h3]
        e3p[k + 2, pl.ds(0, own3 + 2 * h3, stride=2), :] = value
        e3p[k + 2, pl.ds(1, own3 + 2 * h3, stride=2), :] = value

    planes2 = s2.shape[0]
    for p in range(-5, n2 + 5):
        plane = slab * n2 + p
        inside = jnp.where((plane >= 0) & (plane < planes2), 1.0, 0.0)
        f2[p + 5, 0, 8 : 8 + rows2, :] = s2[jnp.clip(plane, 0, planes2 - 1)] * inside

    def extra2(index, b, first, size):
        return e3p[index >> 1, first : first + size, :]

    h2 = HX // 4
    relax(v2a, 5, (-4, n2 + 4), f2, 5, rows2, h2, edges, n2, extra=extra2, chunk=32)
    relax(v2b, 5, (-3, n2 + 3), f2, 5, rows2, h2, edges, n2, old=v2a, ooff=5, chunk=32)
    relax(v2a, 5, (-2, n2 + 2), f2, 5, rows2, h2, edges, n2, old=v2b, ooff=5, chunk=32)

    cut = h2 - HU // 2
    matrix2 = copy_matrix(LANES)
    for k in range(-2, n2 + 2):
        value = select_dot(v2a[k + 5, 0, 8 + cut : 8 + rows2 - cut, :], matrix2)
        for b in range(2):
            part = value[:, LANES * b : LANES * (b + 1)]
            e2p[k + 2, b, pl.ds(0, rows2 - 2 * cut, stride=2), :] = part
            e2p[k + 2, b, pl.ds(1, rows2 - 2 * cut, stride=2), :] = part


def first_level(edges, s1, below, above, e2p, e1, f1, v1a, v1b):
    n1, rows1 = s1.shape[0], s1.shape[2]
    near = rows1 - HU
    inner = slice(8 + HU // 2, 8 + HU // 2 + near)
    for b in range(f1.shape[1]):
        for p in range(4):
            first = near * (p * f1.shape[1] + b)
            for plane, message in ((p, below), (4 + n1 + p, above)):
                f1[plane, b, inner, :] = message[first : first + near]
        for p in range(n1):
            f1[4 + p, b, 8 : 8 + rows1, :] = s1[p, b]

    def extra1(index, b, first, size):
        return e2p[(index + 1) >> 1, b, first : first + size, :]

    relax(v1a, 4, (-3, n1 + 3), f1, 4, rows1, HU, edges, n1, extra=extra1)
    relax(v1b, 4, (-2, n1 + 2), f1, 4, rows1, HU, edges, n1, old=v1a, ooff=4)
    relax(e1, 1, (-1, n1 + 1), f1, 4, rows1, HU, edges, n1, old=v1b, ooff=4, shift=0)


def early_kernel(
    boxes, slabs, n0, x0, rim,
    box_list, f_own, z_below, z_above, below, above,
    f_rim, v_rim,
    fb, va, patches, found, sem, out_sem,
):
    edges = Edges(boxes, slabs)
    rows = x0 + 2 * HU
    fetch = pltpu.make_async_copy(box_list, patches, sem.at[4])
    copies = (
        [
            pltpu.make_async_copy(f_own.at[pl.ds(0, 2)], fb.at[pl.ds(2, 2), :, pl.ds(8, rows), :], sem.at[0]),
            pltpu.make_async_copy(f_own.at[pl.ds(n0 - 2, 2)], fb.at[pl.ds(4, 2), :, pl.ds(8, rows), :], sem.at[3]),
        ]
        + block_copies(z_below, fb, (0, 2), 8 + HU, x0, sem.at[1])
        + block_copies(z_above, fb, (6, 2), 8 + HU, x0, sem.at[2])
    )
    fetch.start()
    for copy in copies:
        copy.start()
    fetch.wait()

    def own_row(owner, x):
        return x - 4 + HU + 8, owner == edges.box

    count = listed(patches, own_row, found)
    packed = rim + 16 * fb.shape[1]
    slots = (below.shape[0] - packed) // 2
    for copy in copies:
        copy.wait()
    for z in range(2):
        for b in range(fb.shape[1]):
            at = rim + 8 * (fb.shape[1] * z + b)
            for plane, message in ((z, below), (6 + z, above)):
                fb[plane, b, 5 + HU : 8 + HU, :] = message[at : at + 3]
                fb[plane, b, 8 + HU + x0 : 11 + HU + x0, :] = message[at + 3 : at + 6]
    tiles = Tiles()

    def place(slot):
        lines = [(z, below, z) for z in range(2)] + [(6 + z, above, z) for z in range(2)]
        lines = [(plane, message[pl.ds(packed + z * slots + slot, 1), :]) for plane, message, z in lines]
        tiles.put(fb, found[0, slot], found[1, slot], lines)

    lax.fori_loop(0, count, lambda index, carry: place(index) or carry, 0)
    outs = [
        pltpu.make_async_copy(fb.at[pl.ds(1, 1)], f_rim.at[pl.ds(0, 1)], out_sem.at[0]),
        pltpu.make_async_copy(fb.at[pl.ds(6, 1)], f_rim.at[pl.ds(1, 1)], out_sem.at[1]),
        pltpu.make_async_copy(va.at[pl.ds(0, 3)], v_rim.at[pl.ds(0, 3)], out_sem.at[2]),
        pltpu.make_async_copy(va.at[pl.ds(3, 3)], v_rim.at[pl.ds(3, 3)], out_sem.at[3]),
    ]
    outs[0].start()
    outs[1].start()
    relax(va, 2, (-2, 1), fb, 2, rows, HU, edges, n0, s_planes=(-2, n0), unroll=2)
    outs[2].start()
    relax(va, 4 - n0, (n0 - 1, n0 + 2), fb, 6 - n0, rows, HU, edges, n0, s_planes=(0, n0 + 2), unroll=2)
    outs[3].start()
    for out in outs:
        out.wait()


def tail_kernel(
    boxes, slabs, n0, x0,
    e2p, s1, below, above, f_own, f_rim, v_own, v_rim,
    out,
    f1, v1a, v1b, e1,
    fb, va, vb, ob, sem, out_sem,
):
    inner = pl.ds(8, x0 + 2 * HU)
    copies = [
        pltpu.make_async_copy(v_own, va.at[pl.ds(4, n0 - 2), :, inner, :], sem.at[0]),
        pltpu.make_async_copy(v_rim.at[pl.ds(0, 3)], va.at[pl.ds(1, 3)], sem.at[1]),
        pltpu.make_async_copy(v_rim.at[pl.ds(3, 3)], va.at[pl.ds(n0 + 2, 3)], sem.at[2]),
        pltpu.make_async_copy(f_own, fb.at[pl.ds(1, n0), :, inner, :], sem.at[3]),
        pltpu.make_async_copy(f_rim.at[pl.ds(0, 1)], fb.at[pl.ds(0, 1)], sem.at[4]),
        pltpu.make_async_copy(f_rim.at[pl.ds(1, 1)], fb.at[pl.ds(n0 + 1, 1)], sem.at[5]),
    ]
    for copy in copies:
        copy.start()
    edges = Edges(boxes, slabs)
    first_level(edges, s1, below, above, e2p, e1, f1, v1a, v1b)
    for copy in copies:
        copy.wait()
    rows = x0 + 2 * HU
    matrix = copy_matrix(LANES)
    cut = HU // 2
    r1 = e1.shape[2]
    size1 = r1 - 2 * cut
    first = 4 * s1.shape[1] * (r1 - HU)
    wide = (below.shape[0] - first) // fb.shape[1]
    for b in range(fb.shape[1]):
        at = slice(4 + HU, 4 + HU + wide)
        for plane, message in ((1, below), (4 + n0, above)):
            va[plane, b, at, :] = va[plane, b, at, :] + (C * C) * message[first + wide * b : first + wide * (b + 1)]

    def prolong(k):
        for group in range(e1.shape[1]):
            value = select_dot(e1[k, group, cut : r1 - cut, :], matrix)
            for b in range(2):
                part = value[:, LANES * b : LANES * (b + 1)]
                for plane in (2 * k + 1, 2 * k + 2):
                    for start in (8, 9):
                        at = pl.ds(start, size1, stride=2)
                        va[plane, 2 * group + b, at, :] = va[plane, 2 * group + b, at, :] + part

    each(e1.shape[0], prolong)
    relax(vb, 3, (-1, n0 + 1), fb, 1, rows, HU, edges, n0, old=va, ooff=3, unroll=2)

    def last(z):
        view = ob.at[pl.ds(z, 1)]
        relax(view, 0, (0, 1), fb.at[pl.ds(z + 1, 1)], 0, rows, HU, edges, None, old=vb.at[pl.ds(z + 2, 3)], ooff=1, shift=-HU, cut=1)
        for copy in block_copies(out.at[pl.ds(z, 1)], ob, (z, 1), 0, x0, out_sem, back=True):
            copy.start()

    each(n0, last, unroll=2)
    for copy in block_copies(out, ob, (0, n0), 0, x0, out_sem, back=True):
        copy.wait()


def shape_of(*dims):
    return jax.ShapeDtypeStruct(dims, F32)


def scratch(*dims):
    return pltpu.VMEM(dims, F32)


def in_hbm(array):
    return pltpu.with_memory_space_constraint(array, pltpu.MemorySpace.HBM)


def limit(mebibytes):
    return pltpu.CompilerParams(vmem_limit_bytes=mebibytes << 20)


def cost(flops, moved):
    return pl.CostEstimate(flops=flops, bytes_accessed=moved, transcendentals=0)


def shift_by(array, axis, step):
    size = lax.axis_size(axis)
    pairs = [(i, i + step) for i in range(size) if 0 <= i + step < size]
    return lax.ppermute(array, axis, pairs)


def per_device(coarse, fine_div, reflux, box_list, cf_mask):
    boxes, slabs = lax.axis_size("box"), lax.axis_size("gz")
    n0, x0, y0 = coarse.shape
    n1, n2 = n0 // 2, n0 // 4
    b0, b1 = y0 // LANES, y0 // LANES // 2
    patches, fine_z, fine_lanes = fine_div.shape
    rows0, rows1, rows2 = x0 + 2 * HX, x0 // 2 + HX, x0 // 4 + HX // 2
    up_rows0, up_rows1 = x0 + 2 * HU, x0 // 2 + 2 * HU
    dma = pltpu.SemaphoreType.DMA
    hbm = pltpu.MemorySpace.HBM
    table = pltpu.SMEM((3, box_list.shape[0]), I32)

    fine_blocks = fine_lanes // LANES
    packed, x_first, x_last, z_first, z_last = pl.pallas_call(
        pack_kernel,
        name="pack",
        out_shape=(
            shape_of(patches * n0, LANES),
            shape_of(n0, HX, y0),
            shape_of(n0, HX, y0),
            shape_of(2, x0, y0),
            shape_of(2, x0, y0),
        ),
        in_specs=[HBM] * 4,
        out_specs=(VM,) * 5,
        scratch_shapes=[
            pltpu.SMEM(cf_mask.shape[::-1], I32),
            scratch(fine_blocks, patches, fine_z, LANES),
            scratch(patches, fine_z, LANES),
            dma((fine_blocks + 2,)),
            dma((4,)),
        ],
        compiler_params=limit(4),
        cost_estimate=cost(10**7, 10**6),
    )(in_hbm(cf_mask.T), in_hbm(fine_div), in_hbm(reflux), in_hbm(coarse))
    z_below = shift_by(z_last, "gz", 1)
    z_above = shift_by(z_first, "gz", -1)
    x_low = shift_by(x_last, "box", 1)
    x_high = shift_by(x_first, "box", -1)
    packed = lax.all_gather(packed, "box", axis=0, tiled=True)

    slots = boxes * max(2, patches // 4)
    rim = 2 * rows2 + b1 * up_rows1
    message = rim + 2 * (8 * b0 + slots)
    f_own, v_own, c1, c2, up, down, third_up, third_down = pl.pallas_call(
        functools.partial(down_kernel, boxes, slabs, n0, x0),
        name="down",
        out_shape=(
            hbm((n0, b0, up_rows0, LANES), F32),
            hbm((n0 - 2, b0, up_rows0, LANES), F32),
            shape_of(n1 + 2, b1, up_rows1, LANES),
            shape_of(n2 + 4, 1, rows2, LANES),
            shape_of(message, LANES),
            shape_of(message, LANES),
            shape_of(b0 * (x0 + HU), LANES),
            shape_of(b0 * (x0 + HU), LANES),
        ),
        in_specs=[HBM] * 4 + [VM],
        out_specs=(HBM,) * 2 + (VM,) * 6,
        scratch_shapes=[
            scratch(n0 + 4, b0, rows0 + 16, LANES),
            scratch(n0 + 6, b0, rows0 + 16, LANES),
            scratch(n1 + 8, b1, rows1 + 16, LANES),
            scratch(n1 + 10, b1, rows1 + 16, LANES),
            scratch(b0 // 2, rows1, 2 * LANES),
            scratch(max(1, b1 // 2), rows2, min(2, b1) * LANES),
            table,
            table,
            table,
            dma((4,)),
            dma((2,)),
        ],
        compiler_params=limit(20),
        cost_estimate=cost(3 * 10**7, 10**7),
    )(in_hbm(box_list.T), in_hbm(coarse), x_low, x_high, packed)

    from_below = shift_by(up, "gz", 1)
    from_above = shift_by(down, "gz", -1)
    copies = pl.pallas_call(
        total_kernel,
        name="total",
        out_shape=shape_of(slabs, n2 * rows2, LANES),
        in_specs=[VM] * 3,
        out_specs=VM,
        compiler_params=limit(3),
        cost_estimate=cost(10**6, 10**6),
    )(c2, from_below, from_above)
    s2 = lax.all_to_all(copies, "gz", split_axis=0, concat_axis=0, tiled=True)
    s2 = s2.reshape(slabs * n2, rows2, LANES)
    last = 4 * b1 * (up_rows1 - HU) + b0 * (x0 + HU)
    s1, up, down = pl.pallas_call(
        functools.partial(join_kernel, rows2),
        name="join",
        out_shape=(shape_of(n1, b1, up_rows1, LANES), shape_of(last, LANES), shape_of(last, LANES)),
        in_specs=[VM] * 5,
        out_specs=(VM,) * 3,
        compiler_params=limit(5),
        cost_estimate=cost(10**6, 10**6),
    )(c1, from_below, from_above, third_up, third_down)
    below = shift_by(up, "gz", 1)
    above = shift_by(down, "gz", -1)

    up_wide = up_rows0 + 16
    f_rim, v_rim = pl.pallas_call(
        functools.partial(early_kernel, boxes, slabs, n0, x0, rim),
        name="early",
        out_shape=(hbm((2, b0, up_wide, LANES), F32), hbm((6, b0, up_wide, LANES), F32)),
        in_specs=[HBM, HBM, HBM, HBM, VM, VM],
        out_specs=(HBM, HBM),
        scratch_shapes=[
            scratch(8, b0, up_wide, LANES),
            scratch(6, b0, up_wide, LANES),
            table,
            table,
            dma((5,)),
            dma((4,)),
        ],
        compiler_params=limit(10),
        cost_estimate=cost(2 * 10**7, 10**7),
    )(in_hbm(box_list.T), in_hbm(f_own), in_hbm(z_below), in_hbm(z_above), from_below, from_above)

    planes2, half = slabs * n2, slabs * n2 // 4
    own3 = x0 // 8
    s3 = pl.pallas_call(
        functools.partial(third_kernel, boxes, slabs),
        name="third",
        out_shape=shape_of(half, own3, LANES),
        in_specs=[VM],
        out_specs=VM,
        scratch_shapes=[scratch(planes2 + 2, 1, rows2 + 16, LANES)] * 2 + [scratch(1, rows2 // 2, LANES)],
        compiler_params=limit(4),
        cost_estimate=cost(10**6, 10**6),
    )(s2)
    s3 = lax.all_gather(s3, "box", axis=0)
    rows3 = boxes * own3
    e2p = pl.pallas_call(
        functools.partial(middle_kernel, boxes, slabs),
        name="middle",
        out_shape=shape_of(n2 + 4, 2, up_rows1, LANES),
        in_specs=[VM] * 2,
        out_specs=VM,
        scratch_shapes=[scratch(half, 1, rows3 + 16, LANES)] * 3
        + [scratch(n2 // 2 + 4, rows2, LANES)]
        + [scratch(n2 + 10, 1, rows2 + 16, LANES)] * 3,
        compiler_params=limit(8),
        cost_estimate=cost(10**7, 2 * 10**6),
    )(s3, s2)
    return pl.pallas_call(
        functools.partial(tail_kernel, boxes, slabs, n0, x0),
        name="tail",
        out_shape=shape_of(n0, x0, y0),
        in_specs=[VM] * 4 + [HBM] * 4,
        out_specs=HBM,
        scratch_shapes=[scratch(n1 + 8, b1, up_rows1 + 16, LANES)] * 3
        + [scratch(n1 + 2, b1, up_rows1, LANES)]
        + [scratch(n0 + 2, b0, up_rows0 + 16, LANES)]
        + [scratch(n0 + 6, b0, up_rows0 + 16, LANES)] * 2
        + [scratch(n0, b0, x0, LANES), dma((6,)), dma(())],
        compiler_params=limit(24),
        cost_estimate=cost(4 * 10**7, 10**7),
    )(e2p, s1, below, above, in_hbm(f_own), in_hbm(f_rim), in_hbm(v_own), in_hbm(v_rim))


def solution(mesh):
    return jax.shard_map(
        per_device,
        mesh=mesh,
        in_specs=(P("gz", "box", None), P("box", "gz", None), P("box", "gz", None), P(), P()),
        out_specs=P("gz", "box", None),
        check_vma=False,
    )
```

```python
import functools

import jax
import jax.numpy as jnp
from jax import lax
from jax.experimental import pallas as pl
from jax.experimental.pallas import tpu as pltpu
from jax.sharding import PartitionSpec as P


CSWEEPS = 16
OMEGA = 0.8
C = OMEGA / 6.0
HX = 32
HU = 8
LANES = 128
F32 = jnp.float32
BF16 = jnp.bfloat16
I32 = jnp.int32

VM = pl.BlockSpec(memory_space=pltpu.VMEM)
SM = pl.BlockSpec(memory_space=pltpu.SMEM)
HBM = pl.BlockSpec(memory_space=pltpu.MemorySpace.HBM)


def iota(shape, dim):
    return lax.broadcasted_iota(I32, shape, dim)


def as_matrix(condition):
    return condition.astype(F32).astype(BF16)


def pair_matrix(length):
    shape = (length, length // 2)
    return as_matrix((iota(shape, 0) >> 1) == iota(shape, 1))


def copy_matrix(length):
    shape = (length, 2 * length)
    return as_matrix(iota(shape, 0) == (iota(shape, 1) >> 1))


def select_dot(values, matrix):
    high = values.astype(BF16)
    low = (values - high.astype(F32)).astype(BF16)
    return jnp.dot(high, matrix, preferred_element_type=F32) + jnp.dot(
        low, matrix, preferred_element_type=F32
    )


def each(count, body, unroll=1):
    def step(index, carry):
        body(index)
        return carry

    lax.fori_loop(0, count, step, 0, unroll=unroll)


def beside_lanes(blocks):
    lane = iota(blocks[0].shape, 1)
    right = [pltpu.roll(block, 1, 1) for block in blocks]
    left = [pltpu.roll(block, LANES - 1, 1) for block in blocks]
    sums = []
    for b in range(len(blocks)):
        before = right[b - 1] if b > 0 else 0.0
        after = left[b + 1] if b + 1 < len(blocks) else 0.0
        sums.append(
            jnp.where(lane == 0, before, right[b]) + jnp.where(lane == LANES - 1, after, left[b])
        )
    return sums


def around(field, plane, row, rows, has=(True, True, True)):
    count = field.shape[1]

    def at(p, first):
        return [field[p, b, first : first + rows, :] for b in range(count)]

    sides = [at(plane + p, row + 8) for p in (-1, 1) if has[p + 1]]
    if not has[1]:
        return None, sides[0]
    middle = at(plane, row + 8)
    beside = zip(at(plane, row + 7), at(plane, row + 9), beside_lanes(middle))
    near = [(a + b) + c for a, b, c in beside]
    for side in sides:
        near = [a + b for a, b in zip(near, side)]
    return middle, near


class Edges:
    def __init__(self, boxes, slabs):
        self.box, self.slab = lax.axis_index("box"), lax.axis_index("gz")
        self.boxes, self.slabs = boxes, slabs

    def planes(self, plane, count):
        outside = ((plane < 0) & (self.slab == 0)) | ((plane >= count) & (self.slab == self.slabs - 1))
        return jnp.where(outside, 0.0, 1.0).astype(F32)

    def low(self):
        return jnp.where(self.box == 0, 0.0, 1.0).astype(F32)

    def high(self):
        return jnp.where(self.box == self.boxes - 1, 0.0, 1.0).astype(F32)


def chunks_of(rows, halo, chunk, cut=0):
    out = [] if cut else [(0, halo, -1)]
    inner = (halo, rows - halo)
    for first in range(inner[0], inner[1], chunk):
        out.append((first, min(chunk, inner[1] - first), 0))
    return out if cut else out + [(rows - halo, halo, 1)]


def scale_of(side, edges, plane_scale):
    if side == 0:
        return plane_scale
    row_scale = edges.low() if side < 0 else edges.high()
    return row_scale if plane_scale is None else row_scale * plane_scale


def relax(new, noff, planes, source, soff, rows, halo, edges, count, old=None, ooff=0, extra=None, chunk=16, shift=8, cut=0, s_planes=None, unroll=1):
    def body(index, has=(True, True, True)):
        plane_scale = None if count is None else edges.planes(index + planes[0], count)
        for first, size, side in chunks_of(rows, halo, chunk, cut):
            scale = scale_of(side, edges, plane_scale)
            if old is None:
                middle, near = around(source, index + (planes[0] + soff), first, size, has)
                values = [(C * C) * n for n in near]
                if middle is not None:
                    values = [(1.2 * C) * m + v for m, v in zip(middle, values)]
                if extra is not None:
                    values = [v + extra(index, b, first, size) for b, v in enumerate(values)]
            else:
                middle, near = around(old, index + (planes[0] + ooff), first, size)
                at = index + (planes[0] + soff)
                values = [
                    (1.0 - OMEGA) * m + C * (source[at, b, first + 8 : first + 8 + size, :] + n)
                    for b, (m, n) in enumerate(zip(middle, near))
                ]
            for b, value in enumerate(values):
                if scale is not None:
                    value = value * scale
                new[index + (planes[0] + noff), b, first + shift : first + shift + size, :] = value

    if s_planes is None:
        each(planes[1] - planes[0], body, unroll)
        return
    inner = []
    for plane in range(*planes):
        has = tuple(s_planes[0] <= plane + p < s_planes[1] for p in (-1, 0, 1))
        if all(has):
            inner.append(plane)
        else:
            body(plane - planes[0], has)
    if inner:
        first = inner[0] - planes[0]
        each(len(inner), lambda index: body(index + first), unroll)


def restrict(source, soff, v, voff, pairs, rows, summed, store, chunk=8, v_planes=None, s_planes=None, unroll=1):
    count = v.shape[1]
    width = min(2, count)
    half = rows // 2

    def body(index, has_v=(True,) * 4, has_s=(True,) * 2):
        low_v, low_s = 2 * index + (2 * pairs[0] + voff), 2 * index + (2 * pairs[0] + soff)
        for first in range(0, half, chunk):
            size = min(chunk, half - first)

            def at(field, plane, b, offset):
                return field[plane, b, pl.ds(8 + 2 * first + offset, size, stride=2), :]

            def both(field, plane, b):
                return at(field, plane, b, 0) + at(field, plane, b, 1)

            def total_of(terms):
                total = terms[0]
                for term in terms[1:]:
                    total = total + term
                return total

            inside = [p for p in (1, 2) if has_v[p]]
            sums = []
            if inside:
                whole = [total_of([both(v, low_v + p - 1, b) for p in inside]) for b in range(count)]
                near = beside_lanes(whole)
            for b in range(count):
                terms = []
                if inside:
                    terms.append(near[b] - 4.0 * whole[b])
                    terms += [at(v, low_v + p - 1, b, -1) + at(v, low_v + p - 1, b, 2) for p in inside]
                terms += [both(source, low_s + p, b) for p in (0, 1) if has_s[p]]
                terms += [both(v, low_v + p - 1, b) for p in (0, 3) if has_v[p]]
                sums.append(total_of(terms))
            for b in range(count):
                cut = slice(LANES * (b % width), LANES * (b % width + 1))
                summed[index, b // width, first : first + size, cut] = sums[b]

    def finish():
        matrix = pair_matrix(width * LANES)
        for index in range(pairs[1] - pairs[0]):
            for group in range(count // width):
                store(index, group, 0.5 * select_dot(summed[index, group], matrix))

    if v_planes is None:
        each(pairs[1] - pairs[0], body, unroll)
        finish()
        return
    inner = []
    for coarse in range(*pairs):
        has_v = tuple(v_planes[0] <= 2 * coarse + p - 1 < v_planes[1] for p in range(4))
        has_s = tuple(s_planes[0] <= 2 * coarse + p < s_planes[1] for p in range(2))
        if all(has_v + has_s):
            inner.append(coarse)
        else:
            body(coarse - pairs[0], has_v, has_s)
    if inner:
        first = inner[0] - pairs[0]
        each(len(inner), lambda index: body(index + first), unroll)
    finish()


def zero(ref, planes):
    for plane in planes:
        ref[plane] = jnp.zeros(ref.shape[1:], F32)


def zero_rims(ref, planes=None):
    rows = ref.shape[2]
    for plane in range(ref.shape[0]) if planes is None else planes:
        for b in range(ref.shape[1]):
            ref[plane, b, 0:8, :] = jnp.zeros((8, LANES), F32)
            ref[plane, b, rows - 8 : rows, :] = jnp.zeros((8, LANES), F32)


def block_copies(wide, tiled, planes, first, rows, sem, back=False):
    copies = []
    for b in range(tiled.shape[1]):
        pair = (
            wide.at[:, :, pl.ds(LANES * b, LANES)],
            tiled.at[pl.ds(planes[0], planes[1]), b, pl.ds(first, rows), :],
        )
        copies.append(pltpu.make_async_copy(*(pair[::-1] if back else pair), sem))
    return copies


def pack_kernel(
    mask_in, fine, flux, coarse, out, x_first, x_last, z_first, z_last, mask, fine_s, flux_s, sem, edge_sem
):
    patches, fine_z = fine.shape[0], fine.shape[1]
    n0 = fine_z // 2
    blocks = fine_s.shape[0]
    copies = [
        pltpu.make_async_copy(fine.at[:, :, pl.ds(LANES * b, LANES)], fine_s.at[b], sem.at[b])
        for b in range(blocks)
    ]
    copies.append(pltpu.make_async_copy(flux, flux_s, sem.at[blocks]))
    copies.append(pltpu.make_async_copy(mask_in, mask, sem.at[blocks + 1]))
    n, x = coarse.shape[0], coarse.shape[1]
    cuts = [
        pltpu.make_async_copy(coarse.at[pl.ds(n - 2, 2)], z_last, edge_sem.at[0]),
        pltpu.make_async_copy(coarse.at[pl.ds(0, 2)], z_first, edge_sem.at[1]),
        pltpu.make_async_copy(coarse.at[:, pl.ds(x - HX, HX), :], x_last, edge_sem.at[2]),
        pltpu.make_async_copy(coarse.at[:, pl.ds(0, HX), :], x_first, edge_sem.at[3]),
    ]
    for copy in copies + cuts:
        copy.start()
    base = lax.axis_index("box") * patches
    side = (iota((n0, LANES), 1) >> 4) & 3
    source, target = iota((LANES, LANES), 0), iota((LANES, LANES), 1)
    s, i = (source >> 4) & 3, (source & 15) >> 1
    goal = jnp.where(
        s == 0, i + 91, jnp.where(s == 1, i + 1, jnp.where(s == 2, 80 - 10 * i, 89 - 10 * i))
    )
    matrices = [as_matrix(goal == target)]
    for b in range(blocks):
        place = source + LANES * b
        goal = 10 * (8 - (place >> 5)) + ((place & 15) >> 1) + 1
        matrices.append(as_matrix(goal == target))
    for copy in copies:
        copy.wait()
    masked, fine_rows = [], [[] for _ in range(blocks)]
    for patch in range(patches):
        m = [mask[s, base + patch].astype(F32) for s in range(4)]
        factor = jnp.where(side == 0, m[0], jnp.where(side == 1, m[1], jnp.where(side == 2, m[2], m[3])))
        masked.append(
            (flux_s[patch, pl.ds(0, n0, stride=2), :] + flux_s[patch, pl.ds(1, n0, stride=2), :]) * factor
        )
        for b in range(blocks):
            fine_rows[b].append(
                fine_s[b, patch, pl.ds(0, n0, stride=2), :] + fine_s[b, patch, pl.ds(1, n0, stride=2), :]
            )
    total = select_dot(jnp.concatenate(masked, axis=0), matrices[0])
    for b in range(blocks):
        total = total + select_dot(jnp.concatenate(fine_rows[b], axis=0), matrices[b + 1])
    out[...] = 0.125 * total
    for cut in cuts:
        cut.wait()


class Tiles:
    def __init__(self):
        self.lane = iota((16, LANES), 1)
        row = iota((16, LANES), 0)
        self.ring_row = (row >= 3) & (row < 13)
        self.core_row = (row >= 4) & (row < 12)

    def put(self, field, row, column, pairs):
        row = pl.multiple_of(row, 8)
        block, offset = column >> 7, column & (LANES - 1)
        across = self.lane - offset
        ring = self.ring_row & (across >= 3) & (across < 13)
        core = self.core_row & (across >= 4) & (across < 12)
        for plane, line in pairs:
            values = jnp.broadcast_to(line, (8, LANES))
            values = pltpu.roll(values, 0, 1, stride=10, stride_axis=0)
            tile = jnp.concatenate(
                [
                    pltpu.roll(values, (offset + 11) & (LANES - 1), 1),
                    pltpu.roll(values, (offset + 91) & (LANES - 1), 1),
                ],
                axis=0,
            )
            now = field[plane, block, pl.ds(row, 16), :]
            field[plane, block, pl.ds(row, 16), :] = jnp.where(core, 0.0, now) + jnp.where(ring, tile, 0.0)


def listed(box_list, row_of, found):
    def step(patch, count):
        row, keep = row_of(box_list[0, patch], box_list[1, patch])
        found[0, count] = row
        found[1, count] = box_list[2, patch] - 4
        found[2, count] = patch
        return count + jnp.where(keep, 1, 0)

    return lax.fori_loop(0, box_list.shape[1], step, jnp.zeros((), I32), unroll=8)


def down_kernel(
    boxes, slabs, n0, x0,
    box_list, coarse, x_low, x_high, packed,
    f_own, v_own, c1, c2, up, down, late_up, late_down,
    fb, vb, g1, v1, summed0, summed1, patches, found, owned, sem, out_sem,
):
    edges = Edges(boxes, slabs)
    rows0, rows1, rows2 = x0 + 2 * HX, x0 // 2 + HX, x0 // 4 + HX // 2
    n1, n2 = n0 // 2, n0 // 4
    copies = (
        block_copies(x_low, fb, (2, n0), 8, HX, sem.at[0])
        + block_copies(coarse, fb, (2, n0), 8 + HX, x0, sem.at[1])
        + block_copies(x_high, fb, (2, n0), 8 + HX + x0, HX, sem.at[2])
    )
    fetch = pltpu.make_async_copy(box_list, patches, sem.at[3])
    fetch.start()
    for copy in copies:
        copy.start()
    fetch.wait()

    def near_row(owner, x):
        row = (owner - edges.box) * x0 + x - 4 + HX
        return row + 8, (row >= 0) & (row < rows0)

    def own_row(owner, x):
        return x, owner == edges.box

    near_count = listed(patches, near_row, found)
    own_count = listed(patches, own_row, owned)
    for copy in copies:
        copy.wait()
    tiles = Tiles()

    def place(index):
        patch = found[2, index]
        lines = [(2 + z, packed[pl.ds(patch * n0 + z, 1), :]) for z in range(n0)]
        tiles.put(fb, found[0, index], found[1, index], lines)

    lax.fori_loop(0, near_count, lambda index, carry: place(index) or carry, 0)

    inner = pl.ds(8 + HX - HU, x0 + 2 * HU)
    f_copy = pltpu.make_async_copy(fb.at[pl.ds(2, n0), :, inner, :], f_own, out_sem.at[0])
    f_copy.start()

    relax(vb, 3, (-1, n0 + 1), fb, 2, rows0, HX, edges, n0, s_planes=(0, n0), unroll=2)
    v_copy = pltpu.make_async_copy(vb.at[pl.ds(4, n0 - 2), :, inner, :], v_own, out_sem.at[1])
    v_copy.start()

    h1 = HX // 2

    def store1(index, group, value):
        value = value * edges.planes(index - 1, n1)
        g1[index + 3, group, 8 : 8 + h1, :] = value[:h1] * edges.low()
        g1[index + 3, group, 8 + h1 : 8 + rows1 - h1, :] = value[h1 : rows1 - h1]
        g1[index + 3, group, 8 + rows1 - h1 : 8 + rows1, :] = value[rows1 - h1 :] * edges.high()

    restrict(fb, 2, vb, 3, (-1, n1 + 1), rows0, summed0, store1, v_planes=(-1, n0 + 1), s_planes=(0, n0))
    for plane in range(n1 + 2):
        for b in range(g1.shape[1]):
            c1[plane, b] = g1[plane + 3, b, 8 + h1 - HU : 8 + rows1 - h1 + HU, :]

    relax(v1, 5, (-2, n1 + 2), g1, 4, rows1, h1, edges, n1, s_planes=(-1, n1 + 1), unroll=2)

    h2 = HX // 4

    def store2(index, group, value):
        c2[index, group, 0:h2, :] = value[:h2] * edges.low()
        c2[index, group, h2 : rows2 - h2, :] = value[h2 : rows2 - h2]
        c2[index, group, rows2 - h2 : rows2, :] = value[rows2 - h2 :] * edges.high()

    restrict(g1, 4, v1, 5, (-2, n2 + 2), rows1, summed1, store2, v_planes=(-2, n1 + 2), s_planes=(-1, n1 + 1))

    r1 = c1.shape[2]
    for target, late, fine_plane, coarse_first in ((up, late_up, n1 + 1, n2 + 2), (down, late_down, 0, 0)):
        target[0:rows2] = c2[coarse_first, 0]
        target[rows2 : 2 * rows2] = c2[coarse_first + 1, 0]
        for b in range(c1.shape[1]):
            late[r1 * b : r1 * (b + 1)] = c1[fine_plane, b]
    rim = 2 * rows2
    slots = (up.shape[0] - rim) // 2 - 8 * fb.shape[1]
    begin = c1.shape[1] * r1
    wide = (late_up.shape[0] - begin) // fb.shape[1]
    for b in range(fb.shape[1]):
        at = slice(4 + HX, 4 + HX + wide)
        late_up[begin + wide * b : begin + wide * (b + 1)] = fb[n0 - 1, b, at, :]
        late_down[begin + wide * b : begin + wide * (b + 1)] = fb[4, b, at, :]
        for z in range(2):
            first = rim + 8 * (fb.shape[1] * z + b)
            for target, plane in ((up, n0 + z), (down, 2 + z)):
                target[first : first + 3, :] = fb[plane, b, 8 + HX - 3 : 8 + HX, :]
                target[first + 3 : first + 6, :] = fb[plane, b, 8 + HX + x0 : 8 + HX + x0 + 3, :]
                target[first + 6 : first + 8, :] = jnp.zeros((2, LANES), F32)
    rim = rim + 16 * fb.shape[1]
    up[rim:, :] = jnp.zeros((2 * slots, LANES), F32)
    down[rim:, :] = jnp.zeros((2 * slots, LANES), F32)

    def keep(slot):
        patch = owned[2, slot]
        for z in range(2):
            up[pl.ds(rim + z * slots + slot, 1), :] = packed[pl.ds(patch * n0 + n0 - 2 + z, 1), :]
            down[pl.ds(rim + z * slots + slot, 1), :] = packed[pl.ds(patch * n0 + z, 1), :]

    lax.fori_loop(0, own_count, lambda index, carry: keep(index) or carry, 0)
    f_copy.wait()
    v_copy.wait()


def total_kernel(c2, below, above, copies):
    n2, rows2 = c2.shape[0] - 4, c2.shape[2]
    for plane in range(n2):
        value = c2[2 + plane, 0]
        if plane < 2:
            value = value + below[plane * rows2 : (plane + 1) * rows2]
        if plane >= n2 - 2:
            first = (plane - (n2 - 2)) * rows2
            value = value + above[first : first + rows2]
        for slab in range(copies.shape[0]):
            copies[slab, plane * rows2 : (plane + 1) * rows2] = value


def join_kernel(c1, below, above, s1, up, down):
    n1, r1 = s1.shape[0], c1.shape[2]
    for plane in range(n1):
        s1[plane] = c1[1 + plane]
    for b in range(s1.shape[1]):
        first = b * r1
        s1[0, b] = s1[0, b] + below[first : first + r1]
        s1[n1 - 1, b] = s1[n1 - 1, b] + above[first : first + r1]
    near = r1 - HU
    for p in range(4):
        for b in range(s1.shape[1]):
            first = near * (p * s1.shape[1] + b)
            up[first : first + near] = s1[n1 - 4 + p, b, HU // 2 : HU // 2 + near, :]
            down[first : first + near] = s1[p, b, HU // 2 : HU // 2 + near, :]


def third_kernel(boxes, slabs, s2, s3, fb, vb, summed):
    edges = Edges(boxes, slabs)
    planes, rows = s2.shape[0], s2.shape[1]
    zero(fb, (0, planes + 1))
    zero(vb, (0, planes + 1))
    for plane in range(planes):
        fb[plane + 1, 0, 8 : 8 + rows, :] = s2[plane]
    relax(vb, 1, (0, planes), fb, 1, rows, HX // 4, edges, None, chunk=32, unroll=4)
    quarter = planes // 4
    h3 = HX // 8
    own = rows // 2 - 2 * h3
    lanes = LANES // 2

    for part in range(2):

        def store(index, group, value, part=part):
            s3[index, :, lanes * part : lanes * (part + 1)] = value[h3 : h3 + own]

        restrict(fb, 1, vb, 1, (quarter * part, quarter * (part + 1)), rows, summed, store, unroll=quarter)


def middle_kernel(
    boxes, slabs,
    s3, s2,
    e2p,
    sc, va3, vb3, e3p, f2, v2a, v2b,
):
    edges = Edges(boxes, slabs)
    slab = edges.slab
    half, rows3 = sc.shape[0], sc.shape[2] - 16
    own3 = s3.shape[2]
    zero_rims(va3)
    zero_rims(vb3)
    for box in range(boxes):
        for plane in range(half):
            value = s3[box, plane]
            sc[plane, 0, 8 + box * own3 : 8 + (box + 1) * own3, :] = value
            va3[plane, 0, 8 + box * own3 : 8 + (box + 1) * own3, :] = C * value

    def coarsest(old, new):
        chunk = 16
        lane = iota((chunk, LANES), 1)
        for row in range(0, rows3, chunk):
            inner = slice(row + 8, row + 8 + chunk)
            for plane in range(half):
                middle = old[plane, 0, inner, :]
                before = jnp.where((lane & 63) == 0, 0.0, pltpu.roll(middle, 1, 1))
                after = jnp.where((lane & 63) == 63, 0.0, pltpu.roll(middle, LANES - 1, 1))
                if plane > 0:
                    lower = old[plane - 1, 0, inner, :]
                else:
                    lower = jnp.where(lane < 64, 0.0, pltpu.roll(old[half - 1, 0, inner, :], 64, 1))
                if plane < half - 1:
                    upper = old[plane + 1, 0, inner, :]
                else:
                    upper = jnp.where(lane < 64, pltpu.roll(old[0, 0, inner, :], 64, 1), 0.0)
                beside = old[plane, 0, row + 7 : row + 7 + chunk, :] + old[plane, 0, row + 9 : row + 9 + chunk, :]
                near = beside + ((before + after) + (lower + upper))
                new[plane, 0, inner, :] = (1.0 - OMEGA) * middle + C * (sc[plane, 0, inner, :] + near)

    def double(index):
        coarsest(va3, vb3)
        coarsest(vb3, va3)

    each((CSWEEPS - 1) // 2, double)
    coarsest(va3, vb3)

    n2, rows2 = s2.shape[0] // slabs, s2.shape[1]
    n3 = n2 // 2
    shape = (LANES, LANES)
    copy_low = (iota(shape, 0) == (iota(shape, 1) >> 1)).astype(F32)
    copy_high = (iota(shape, 0) == (iota(shape, 1) >> 1) + 64).astype(F32)
    total3 = 2 * half
    h3 = HX // 8
    window = pl.multiple_of(edges.box * own3, 8)
    for k in range(-2, n3 + 2):
        plane = slab * n3 + k
        inside = (plane >= 0) & (plane < total3)
        safe = jnp.clip(plane, 0, total3 - 1)
        upper = safe >= half
        matrix = jnp.where(upper, copy_high, copy_low) * jnp.where(inside, 1.0, 0.0)
        value = vb3[jnp.where(upper, safe - half, safe), 0, pl.ds(window, own3 + 16), :]
        value = select_dot(value, matrix.astype(BF16))[8 - h3 : 8 + own3 + h3]
        e3p[k + 2, pl.ds(0, own3 + 2 * h3, stride=2), :] = value
        e3p[k + 2, pl.ds(1, own3 + 2 * h3, stride=2), :] = value

    planes2 = s2.shape[0]
    for p in range(-5, n2 + 5):
        plane = slab * n2 + p
        inside = jnp.where((plane >= 0) & (plane < planes2), 1.0, 0.0)
        f2[p + 5, 0, 8 : 8 + rows2, :] = s2[jnp.clip(plane, 0, planes2 - 1)] * inside

    def extra2(index, b, first, size):
        return e3p[index >> 1, first : first + size, :]

    h2 = HX // 4
    relax(v2a, 5, (-4, n2 + 4), f2, 5, rows2, h2, edges, n2, extra=extra2, chunk=32, unroll=2)
    relax(v2b, 5, (-3, n2 + 3), f2, 5, rows2, h2, edges, n2, old=v2a, ooff=5, chunk=32, unroll=2)
    relax(v2a, 5, (-2, n2 + 2), f2, 5, rows2, h2, edges, n2, old=v2b, ooff=5, chunk=32, unroll=2)

    cut = h2 - HU // 2
    matrix2 = copy_matrix(LANES)
    for k in range(-2, n2 + 2):
        value = select_dot(v2a[k + 5, 0, 8 + cut : 8 + rows2 - cut, :], matrix2)
        for b in range(2):
            part = value[:, LANES * b : LANES * (b + 1)]
            e2p[k + 2, b, pl.ds(0, rows2 - 2 * cut, stride=2), :] = part
            e2p[k + 2, b, pl.ds(1, rows2 - 2 * cut, stride=2), :] = part


def first_level(edges, s1, below, above, e2p, e1, f1, v1a, v1b):
    n1, rows1 = s1.shape[0], s1.shape[2]
    near = rows1 - HU
    inner = slice(8 + HU // 2, 8 + HU // 2 + near)
    for b in range(f1.shape[1]):
        for p in range(4):
            first = near * (p * f1.shape[1] + b)
            for plane, message in ((p, below), (4 + n1 + p, above)):
                f1[plane, b, inner, :] = message[first : first + near]
        for p in range(n1):
            f1[4 + p, b, 8 : 8 + rows1, :] = s1[p, b]

    def extra1(index, b, first, size):
        return e2p[(index + 1) >> 1, b, first : first + size, :]

    relax(v1a, 4, (-3, n1 + 3), f1, 4, rows1, HU, edges, n1, extra=extra1, unroll=2)
    relax(v1b, 4, (-2, n1 + 2), f1, 4, rows1, HU, edges, n1, old=v1a, ooff=4, unroll=2)
    relax(e1, 1, (-1, n1 + 1), f1, 4, rows1, HU, edges, n1, old=v1b, ooff=4, shift=0, unroll=2)


def early_kernel(
    boxes, slabs, n0, x0, rim,
    box_list, f_own, z_below, z_above, below, above,
    f_rim, v_rim,
    fb, va, patches, found, sem, out_sem,
):
    edges = Edges(boxes, slabs)
    rows = x0 + 2 * HU
    fetch = pltpu.make_async_copy(box_list, patches, sem.at[4])
    copies = (
        [
            pltpu.make_async_copy(f_own.at[pl.ds(0, 2)], fb.at[pl.ds(2, 2), :, pl.ds(8, rows), :], sem.at[0]),
            pltpu.make_async_copy(f_own.at[pl.ds(n0 - 2, 2)], fb.at[pl.ds(4, 2), :, pl.ds(8, rows), :], sem.at[3]),
        ]
        + block_copies(z_below, fb, (0, 2), 8 + HU, x0, sem.at[1])
        + block_copies(z_above, fb, (6, 2), 8 + HU, x0, sem.at[2])
    )
    fetch.start()
    for copy in copies:
        copy.start()
    fetch.wait()

    def own_row(owner, x):
        return x - 4 + HU + 8, owner == edges.box

    count = listed(patches, own_row, found)
    packed = rim + 16 * fb.shape[1]
    slots = (below.shape[0] - packed) // 2
    for copy in copies:
        copy.wait()
    for z in range(2):
        for b in range(fb.shape[1]):
            at = rim + 8 * (fb.shape[1] * z + b)
            for plane, message in ((z, below), (6 + z, above)):
                fb[plane, b, 5 + HU : 8 + HU, :] = message[at : at + 3]
                fb[plane, b, 8 + HU + x0 : 11 + HU + x0, :] = message[at + 3 : at + 6]
    tiles = Tiles()

    def place(slot):
        lines = [(z, below, z) for z in range(2)] + [(6 + z, above, z) for z in range(2)]
        lines = [(plane, message[pl.ds(packed + z * slots + slot, 1), :]) for plane, message, z in lines]
        tiles.put(fb, found[0, slot], found[1, slot], lines)

    lax.fori_loop(0, count, lambda index, carry: place(index) or carry, 0)
    outs = [
        pltpu.make_async_copy(fb.at[pl.ds(1, 1)], f_rim.at[pl.ds(0, 1)], out_sem.at[0]),
        pltpu.make_async_copy(fb.at[pl.ds(6, 1)], f_rim.at[pl.ds(1, 1)], out_sem.at[1]),
        pltpu.make_async_copy(va.at[pl.ds(0, 3)], v_rim.at[pl.ds(0, 3)], out_sem.at[2]),
        pltpu.make_async_copy(va.at[pl.ds(3, 3)], v_rim.at[pl.ds(3, 3)], out_sem.at[3]),
    ]
    outs[0].start()
    outs[1].start()
    relax(va, 2, (-2, 1), fb, 2, rows, HU, edges, n0, s_planes=(-2, n0), unroll=2)
    outs[2].start()
    relax(va, 4 - n0, (n0 - 1, n0 + 2), fb, 6 - n0, rows, HU, edges, n0, s_planes=(0, n0 + 2), unroll=2)
    outs[3].start()
    for out in outs:
        out.wait()


def tail_kernel(
    boxes, slabs, n0, x0,
    e2p, s1, below, above, late_below, late_above, f_own, f_rim, v_own, v_rim,
    out,
    f1, v1a, v1b, e1,
    fb, va, vb, ob, sem, out_sem,
):
    inner = pl.ds(8, x0 + 2 * HU)
    copies = [
        pltpu.make_async_copy(v_own, va.at[pl.ds(4, n0 - 2), :, inner, :], sem.at[0]),
        pltpu.make_async_copy(v_rim.at[pl.ds(0, 3)], va.at[pl.ds(1, 3)], sem.at[1]),
        pltpu.make_async_copy(v_rim.at[pl.ds(3, 3)], va.at[pl.ds(n0 + 2, 3)], sem.at[2]),
        pltpu.make_async_copy(f_own, fb.at[pl.ds(1, n0), :, inner, :], sem.at[3]),
        pltpu.make_async_copy(f_rim.at[pl.ds(0, 1)], fb.at[pl.ds(0, 1)], sem.at[4]),
        pltpu.make_async_copy(f_rim.at[pl.ds(1, 1)], fb.at[pl.ds(n0 + 1, 1)], sem.at[5]),
    ]
    for copy in copies:
        copy.start()
    edges = Edges(boxes, slabs)
    first_level(edges, s1, below, above, e2p, e1, f1, v1a, v1b)
    for copy in copies:
        copy.wait()
    rows = x0 + 2 * HU
    matrix = copy_matrix(LANES)
    cut = HU // 2
    r1 = e1.shape[2]
    size1 = r1 - 2 * cut
    begin = s1.shape[1] * r1
    wide = (late_below.shape[0] - begin) // fb.shape[1]
    for b in range(fb.shape[1]):
        at = slice(4 + HU, 4 + HU + wide)
        for plane, message in ((1, late_below), (4 + n0, late_above)):
            first = begin + wide * b
            va[plane, b, at, :] = va[plane, b, at, :] + (C * C) * message[first : first + wide]

    def prolong(k):
        for group in range(e1.shape[1]):
            value = select_dot(e1[k, group, cut : r1 - cut, :], matrix)
            for b in range(2):
                part = value[:, LANES * b : LANES * (b + 1)]
                for plane in (2 * k + 1, 2 * k + 2):
                    for start in (8, 9):
                        at = pl.ds(start, size1, stride=2)
                        va[plane, 2 * group + b, at, :] = va[plane, 2 * group + b, at, :] + part

    each(e1.shape[0], prolong, unroll=2)
    relax(vb, 3, (-1, n0 + 1), fb, 1, rows, HU, edges, n0, old=va, ooff=3, unroll=2)

    def last(z):
        view = ob.at[pl.ds(z, 1)]
        relax(view, 0, (0, 1), fb.at[pl.ds(z + 1, 1)], 0, rows, HU, edges, None, old=vb.at[pl.ds(z + 2, 3)], ooff=1, shift=-HU, cut=1)
        for copy in block_copies(out.at[pl.ds(z, 1)], ob, (z, 1), 0, x0, out_sem, back=True):
            copy.start()

    each(n0, last, unroll=2)
    for copy in block_copies(out, ob, (0, n0), 0, x0, out_sem, back=True):
        copy.wait()


def shape_of(*dims):
    return jax.ShapeDtypeStruct(dims, F32)


def scratch(*dims):
    return pltpu.VMEM(dims, F32)


def in_hbm(array):
    return pltpu.with_memory_space_constraint(array, pltpu.MemorySpace.HBM)


def limit(mebibytes):
    return pltpu.CompilerParams(vmem_limit_bytes=mebibytes << 20)


def cost(flops, moved):
    return pl.CostEstimate(flops=flops, bytes_accessed=moved, transcendentals=0)


def shift_by(array, axis, step):
    size = lax.axis_size(axis)
    pairs = [(i, i + step) for i in range(size) if 0 <= i + step < size]
    return lax.ppermute(array, axis, pairs)


def per_device(coarse, fine_div, reflux, box_list, cf_mask):
    boxes, slabs = lax.axis_size("box"), lax.axis_size("gz")
    n0, x0, y0 = coarse.shape
    n1, n2 = n0 // 2, n0 // 4
    b0, b1 = y0 // LANES, y0 // LANES // 2
    patches, fine_z, fine_lanes = fine_div.shape
    rows0, rows1, rows2 = x0 + 2 * HX, x0 // 2 + HX, x0 // 4 + HX // 2
    up_rows0, up_rows1 = x0 + 2 * HU, x0 // 2 + 2 * HU
    dma = pltpu.SemaphoreType.DMA
    hbm = pltpu.MemorySpace.HBM
    table = pltpu.SMEM((3, box_list.shape[0]), I32)

    fine_blocks = fine_lanes // LANES
    packed, x_first, x_last, z_first, z_last = pl.pallas_call(
        pack_kernel,
        name="pack",
        out_shape=(
            shape_of(patches * n0, LANES),
            shape_of(n0, HX, y0),
            shape_of(n0, HX, y0),
            shape_of(2, x0, y0),
            shape_of(2, x0, y0),
        ),
        in_specs=[HBM] * 4,
        out_specs=(VM,) * 5,
        scratch_shapes=[
            pltpu.SMEM(cf_mask.shape[::-1], I32),
            scratch(fine_blocks, patches, fine_z, LANES),
            scratch(patches, fine_z, LANES),
            dma((fine_blocks + 2,)),
            dma((4,)),
        ],
        compiler_params=limit(4),
        cost_estimate=cost(10**7, 10**6),
    )(in_hbm(cf_mask.T), in_hbm(fine_div), in_hbm(reflux), in_hbm(coarse))
    z_below = shift_by(z_last, "gz", 1)
    z_above = shift_by(z_first, "gz", -1)
    x_low = shift_by(x_last, "box", 1)
    x_high = shift_by(x_first, "box", -1)
    packed = lax.all_gather(packed, "box", axis=0, tiled=True)

    slots = boxes * max(2, patches // 4)
    rim = 2 * rows2
    message = rim + 2 * (8 * b0 + slots)
    f_own, v_own, c1, c2, up, down, late_up, late_down = pl.pallas_call(
        functools.partial(down_kernel, boxes, slabs, n0, x0),
        name="down",
        out_shape=(
            hbm((n0, b0, up_rows0, LANES), F32),
            hbm((n0 - 2, b0, up_rows0, LANES), F32),
            shape_of(n1 + 2, b1, up_rows1, LANES),
            shape_of(n2 + 4, 1, rows2, LANES),
            shape_of(message, LANES),
            shape_of(message, LANES),
            shape_of(b1 * up_rows1 + b0 * (x0 + HU), LANES),
            shape_of(b1 * up_rows1 + b0 * (x0 + HU), LANES),
        ),
        in_specs=[HBM] * 4 + [VM],
        out_specs=(HBM,) * 2 + (VM,) * 6,
        scratch_shapes=[
            scratch(n0 + 4, b0, rows0 + 16, LANES),
            scratch(n0 + 6, b0, rows0 + 16, LANES),
            scratch(n1 + 8, b1, rows1 + 16, LANES),
            scratch(n1 + 10, b1, rows1 + 16, LANES),
            scratch(n1 + 2, b0 // 2, rows1, 2 * LANES),
            scratch(n2 + 4, max(1, b1 // 2), rows2, min(2, b1) * LANES),
            table,
            table,
            table,
            dma((4,)),
            dma((2,)),
        ],
        compiler_params=limit(20),
        cost_estimate=cost(3 * 10**7, 10**7),
    )(in_hbm(box_list.T), in_hbm(coarse), x_low, x_high, packed)

    from_below = shift_by(up, "gz", 1)
    from_above = shift_by(down, "gz", -1)
    late_below = shift_by(late_up, "gz", 1)
    late_above = shift_by(late_down, "gz", -1)
    copies = pl.pallas_call(
        total_kernel,
        name="total",
        out_shape=shape_of(slabs, n2 * rows2, LANES),
        in_specs=[VM] * 3,
        out_specs=VM,
        compiler_params=limit(3),
        cost_estimate=cost(10**6, 10**6),
    )(c2, from_below, from_above)
    s2 = lax.all_to_all(copies, "gz", split_axis=0, concat_axis=0, tiled=True)
    s2 = s2.reshape(slabs * n2, rows2, LANES)
    last = 4 * b1 * (up_rows1 - HU)
    s1, up, down = pl.pallas_call(
        join_kernel,
        name="join",
        out_shape=(shape_of(n1, b1, up_rows1, LANES), shape_of(last, LANES), shape_of(last, LANES)),
        in_specs=[VM] * 3,
        out_specs=(VM,) * 3,
        compiler_params=limit(5),
        cost_estimate=cost(10**6, 10**6),
    )(c1, late_below, late_above)
    below = shift_by(up, "gz", 1)
    above = shift_by(down, "gz", -1)

    up_wide = up_rows0 + 16
    f_rim, v_rim = pl.pallas_call(
        functools.partial(early_kernel, boxes, slabs, n0, x0, rim),
        name="early",
        out_shape=(hbm((2, b0, up_wide, LANES), F32), hbm((6, b0, up_wide, LANES), F32)),
        in_specs=[HBM, HBM, HBM, HBM, VM, VM],
        out_specs=(HBM, HBM),
        scratch_shapes=[
            scratch(8, b0, up_wide, LANES),
            scratch(6, b0, up_wide, LANES),
            table,
            table,
            dma((5,)),
            dma((4,)),
        ],
        compiler_params=limit(10),
        cost_estimate=cost(2 * 10**7, 10**7),
    )(in_hbm(box_list.T), in_hbm(f_own), in_hbm(z_below), in_hbm(z_above), from_below, from_above)

    planes2, half = slabs * n2, slabs * n2 // 4
    own3 = x0 // 8
    s3 = pl.pallas_call(
        functools.partial(third_kernel, boxes, slabs),
        name="third",
        out_shape=shape_of(half, own3, LANES),
        in_specs=[VM],
        out_specs=VM,
        scratch_shapes=[scratch(planes2 + 2, 1, rows2 + 16, LANES)] * 2 + [scratch(half, 1, rows2 // 2, LANES)],
        compiler_params=limit(4),
        cost_estimate=cost(10**6, 10**6),
    )(s2)
    s3 = lax.all_gather(s3, "box", axis=0)
    rows3 = boxes * own3
    e2p = pl.pallas_call(
        functools.partial(middle_kernel, boxes, slabs),
        name="middle",
        out_shape=shape_of(n2 + 4, 2, up_rows1, LANES),
        in_specs=[VM] * 2,
        out_specs=VM,
        scratch_shapes=[scratch(half, 1, rows3 + 16, LANES)] * 3
        + [scratch(n2 // 2 + 4, rows2, LANES)]
        + [scratch(n2 + 10, 1, rows2 + 16, LANES)] * 3,
        compiler_params=limit(8),
        cost_estimate=cost(10**7, 2 * 10**6),
    )(s3, s2)
    return pl.pallas_call(
        functools.partial(tail_kernel, boxes, slabs, n0, x0),
        name="tail",
        out_shape=shape_of(n0, x0, y0),
        in_specs=[VM] * 6 + [HBM] * 4,
        out_specs=HBM,
        scratch_shapes=[scratch(n1 + 8, b1, up_rows1 + 16, LANES)] * 3
        + [scratch(n1 + 2, b1, up_rows1, LANES)]
        + [scratch(n0 + 2, b0, up_rows0 + 16, LANES)]
        + [scratch(n0 + 6, b0, up_rows0 + 16, LANES)] * 2
        + [scratch(n0, b0, x0, LANES), dma((6,)), dma(())],
        compiler_params=limit(24),
        cost_estimate=cost(4 * 10**7, 10**7),
    )(e2p, s1, below, above, late_below, late_above, in_hbm(f_own), in_hbm(f_rim), in_hbm(v_own), in_hbm(v_rim))


def solution(mesh):
    return jax.shard_map(
        per_device,
        mesh=mesh,
        in_specs=(P("gz", "box", None), P("box", "gz", None), P("box", "gz", None), P(), P()),
        out_specs=P("gz", "box", None),
        check_vma=False,
    )
```

```python
import functools

import jax
import jax.numpy as jnp
from jax import lax
from jax.experimental import pallas as pl
from jax.experimental.pallas import tpu as pltpu
from jax.sharding import PartitionSpec as P


CSWEEPS = 16
OMEGA = 0.8
C = OMEGA / 6.0
HX = 32
HU = 8
LANES = 128
F32 = jnp.float32
BF16 = jnp.bfloat16
I32 = jnp.int32

VM = pl.BlockSpec(memory_space=pltpu.VMEM)
SM = pl.BlockSpec(memory_space=pltpu.SMEM)
HBM = pl.BlockSpec(memory_space=pltpu.MemorySpace.HBM)


def iota(shape, dim):
    return lax.broadcasted_iota(I32, shape, dim)


def as_matrix(condition):
    return condition.astype(F32).astype(BF16)


def pair_matrix(length):
    shape = (length, length // 2)
    return as_matrix((iota(shape, 0) >> 1) == iota(shape, 1))


def copy_matrix(length):
    shape = (length, 2 * length)
    return as_matrix(iota(shape, 0) == (iota(shape, 1) >> 1))


def select_dot(values, matrix):
    high = values.astype(BF16)
    low = (values - high.astype(F32)).astype(BF16)
    return jnp.dot(high, matrix, preferred_element_type=F32) + jnp.dot(
        low, matrix, preferred_element_type=F32
    )


def each(count, body, unroll=1):
    def step(index, carry):
        body(index)
        return carry

    lax.fori_loop(0, count, step, 0, unroll=unroll)


def beside_lanes(blocks):
    lane = iota(blocks[0].shape, 1)
    right = [pltpu.roll(block, 1, 1) for block in blocks]
    left = [pltpu.roll(block, LANES - 1, 1) for block in blocks]
    sums = []
    for b in range(len(blocks)):
        before = right[b - 1] if b > 0 else 0.0
        after = left[b + 1] if b + 1 < len(blocks) else 0.0
        sums.append(
            jnp.where(lane == 0, before, right[b]) + jnp.where(lane == LANES - 1, after, left[b])
        )
    return sums


def around(field, plane, row, rows, has=(True, True, True)):
    count = field.shape[1]

    def at(p, first):
        return [field[p, b, first : first + rows, :] for b in range(count)]

    sides = [at(plane + p, row + 8) for p in (-1, 1) if has[p + 1]]
    if not has[1]:
        return None, sides[0]
    middle = at(plane, row + 8)
    beside = zip(at(plane, row + 7), at(plane, row + 9), beside_lanes(middle))
    near = [(a + b) + c for a, b, c in beside]
    for side in sides:
        near = [a + b for a, b in zip(near, side)]
    return middle, near


class Edges:
    def __init__(self, boxes, slabs):
        self.box, self.slab = lax.axis_index("box"), lax.axis_index("gz")
        self.boxes, self.slabs = boxes, slabs

    def planes(self, plane, count):
        outside = ((plane < 0) & (self.slab == 0)) | ((plane >= count) & (self.slab == self.slabs - 1))
        return jnp.where(outside, 0.0, 1.0).astype(F32)

    def low(self):
        return jnp.where(self.box == 0, 0.0, 1.0).astype(F32)

    def high(self):
        return jnp.where(self.box == self.boxes - 1, 0.0, 1.0).astype(F32)


def chunks_of(rows, halo, chunk, cut=0):
    out = [] if cut else [(0, halo, -1)]
    inner = (halo, rows - halo)
    for first in range(inner[0], inner[1], chunk):
        out.append((first, min(chunk, inner[1] - first), 0))
    return out if cut else out + [(rows - halo, halo, 1)]


def scale_of(side, edges, plane_scale):
    if side == 0:
        return plane_scale
    row_scale = edges.low() if side < 0 else edges.high()
    return row_scale if plane_scale is None else row_scale * plane_scale


def relax(new, noff, planes, source, soff, rows, halo, edges, count, old=None, ooff=0, extra=None, chunk=16, shift=8, cut=0, s_planes=None, unroll=1):
    def body(index, has=(True, True, True)):
        plane_scale = None if count is None else edges.planes(index + planes[0], count)
        for first, size, side in chunks_of(rows, halo, chunk, cut):
            scale = scale_of(side, edges, plane_scale)
            if old is None:
                middle, near = around(source, index + (planes[0] + soff), first, size, has)
                values = [(C * C) * n for n in near]
                if middle is not None:
                    values = [(1.2 * C) * m + v for m, v in zip(middle, values)]
                if extra is not None:
                    values = [v + extra(index, b, first, size) for b, v in enumerate(values)]
            else:
                middle, near = around(old, index + (planes[0] + ooff), first, size)
                at = index + (planes[0] + soff)
                values = [
                    (1.0 - OMEGA) * m + C * (source[at, b, first + 8 : first + 8 + size, :] + n)
                    for b, (m, n) in enumerate(zip(middle, near))
                ]
            for b, value in enumerate(values):
                if scale is not None:
                    value = value * scale
                new[index + (planes[0] + noff), b, first + shift : first + shift + size, :] = value

    if s_planes is None:
        each(planes[1] - planes[0], body, unroll)
        return
    inner = []
    for plane in range(*planes):
        has = tuple(s_planes[0] <= plane + p < s_planes[1] for p in (-1, 0, 1))
        if all(has):
            inner.append(plane)
        else:
            body(plane - planes[0], has)
    if inner:
        first = inner[0] - planes[0]
        each(len(inner), lambda index: body(index + first), unroll)


def restrict(source, soff, v, voff, pairs, rows, summed, store, chunk=8, v_planes=None, s_planes=None, unroll=1):
    count = v.shape[1]
    width = min(2, count)
    half = rows // 2

    def body(index, has_v=(True,) * 4, has_s=(True,) * 2):
        low_v, low_s = 2 * index + (2 * pairs[0] + voff), 2 * index + (2 * pairs[0] + soff)
        for first in range(0, half, chunk):
            size = min(chunk, half - first)

            def at(field, plane, b, offset):
                return field[plane, b, pl.ds(8 + 2 * first + offset, size, stride=2), :]

            def both(field, plane, b):
                return at(field, plane, b, 0) + at(field, plane, b, 1)

            def total_of(terms):
                total = terms[0]
                for term in terms[1:]:
                    total = total + term
                return total

            inside = [p for p in (1, 2) if has_v[p]]
            sums = []
            if inside:
                whole = [total_of([both(v, low_v + p - 1, b) for p in inside]) for b in range(count)]
                near = beside_lanes(whole)
            for b in range(count):
                terms = []
                if inside:
                    terms.append(near[b] - 4.0 * whole[b])
                    terms += [at(v, low_v + p - 1, b, -1) + at(v, low_v + p - 1, b, 2) for p in inside]
                terms += [both(source, low_s + p, b) for p in (0, 1) if has_s[p]]
                terms += [both(v, low_v + p - 1, b) for p in (0, 3) if has_v[p]]
                sums.append(total_of(terms))
            for b in range(count):
                cut = slice(LANES * (b % width), LANES * (b % width + 1))
                summed[index, b // width, first : first + size, cut] = sums[b]

    def finish():
        matrix = pair_matrix(width * LANES)
        for index in range(pairs[1] - pairs[0]):
            for group in range(count // width):
                store(index, group, 0.5 * select_dot(summed[index, group], matrix))

    if v_planes is None:
        each(pairs[1] - pairs[0], body, unroll)
        finish()
        return
    inner = []
    for coarse in range(*pairs):
        has_v = tuple(v_planes[0] <= 2 * coarse + p - 1 < v_planes[1] for p in range(4))
        has_s = tuple(s_planes[0] <= 2 * coarse + p < s_planes[1] for p in range(2))
        if all(has_v + has_s):
            inner.append(coarse)
        else:
            body(coarse - pairs[0], has_v, has_s)
    if inner:
        first = inner[0] - pairs[0]
        each(len(inner), lambda index: body(index + first), unroll)
    finish()


def zero(ref, planes):
    for plane in planes:
        ref[plane] = jnp.zeros(ref.shape[1:], F32)


def zero_rims(ref, planes=None):
    rows = ref.shape[2]
    for plane in range(ref.shape[0]) if planes is None else planes:
        for b in range(ref.shape[1]):
            ref[plane, b, 0:8, :] = jnp.zeros((8, LANES), F32)
            ref[plane, b, rows - 8 : rows, :] = jnp.zeros((8, LANES), F32)


def block_copies(wide, tiled, planes, first, rows, sem, back=False):
    copies = []
    for b in range(tiled.shape[1]):
        pair = (
            wide.at[:, :, pl.ds(LANES * b, LANES)],
            tiled.at[pl.ds(planes[0], planes[1]), b, pl.ds(first, rows), :],
        )
        copies.append(pltpu.make_async_copy(*(pair[::-1] if back else pair), sem))
    return copies


def pack_kernel(
    mask_in, fine, flux, coarse, out, x_first, x_last, z_first, z_last, mask, fine_s, flux_s, sem, edge_sem
):
    patches, fine_z = fine.shape[0], fine.shape[1]
    n0 = fine_z // 2
    blocks = fine_s.shape[0]
    copies = [
        pltpu.make_async_copy(fine.at[:, :, pl.ds(LANES * b, LANES)], fine_s.at[b], sem.at[b])
        for b in range(blocks)
    ]
    copies.append(pltpu.make_async_copy(flux, flux_s, sem.at[blocks]))
    copies.append(pltpu.make_async_copy(mask_in, mask, sem.at[blocks + 1]))
    n, x = coarse.shape[0], coarse.shape[1]
    cuts = [
        pltpu.make_async_copy(coarse.at[pl.ds(n - 2, 2)], z_last, edge_sem.at[0]),
        pltpu.make_async_copy(coarse.at[pl.ds(0, 2)], z_first, edge_sem.at[1]),
        pltpu.make_async_copy(coarse.at[:, pl.ds(x - HX, HX), :], x_last, edge_sem.at[2]),
        pltpu.make_async_copy(coarse.at[:, pl.ds(0, HX), :], x_first, edge_sem.at[3]),
    ]
    for copy in copies + cuts:
        copy.start()
    base = lax.axis_index("box") * patches
    side = (iota((n0, LANES), 1) >> 4) & 3
    source, target = iota((LANES, LANES), 0), iota((LANES, LANES), 1)
    s, i = (source >> 4) & 3, (source & 15) >> 1
    goal = jnp.where(
        s == 0, i + 91, jnp.where(s == 1, i + 1, jnp.where(s == 2, 80 - 10 * i, 89 - 10 * i))
    )
    matrices = [as_matrix(goal == target)]
    for b in range(blocks):
        place = source + LANES * b
        goal = 10 * (8 - (place >> 5)) + ((place & 15) >> 1) + 1
        matrices.append(as_matrix(goal == target))
    for copy in copies:
        copy.wait()
    masked, fine_rows = [], [[] for _ in range(blocks)]
    for patch in range(patches):
        m = [mask[s, base + patch].astype(F32) for s in range(4)]
        factor = jnp.where(side == 0, m[0], jnp.where(side == 1, m[1], jnp.where(side == 2, m[2], m[3])))
        masked.append(
            (flux_s[patch, pl.ds(0, n0, stride=2), :] + flux_s[patch, pl.ds(1, n0, stride=2), :]) * factor
        )
        for b in range(blocks):
            fine_rows[b].append(
                fine_s[b, patch, pl.ds(0, n0, stride=2), :] + fine_s[b, patch, pl.ds(1, n0, stride=2), :]
            )
    total = select_dot(jnp.concatenate(masked, axis=0), matrices[0])
    for b in range(blocks):
        total = total + select_dot(jnp.concatenate(fine_rows[b], axis=0), matrices[b + 1])
    out[...] = 0.125 * total
    for cut in cuts:
        cut.wait()


class Tiles:
    def __init__(self):
        self.lane = iota((16, LANES), 1)
        row = iota((16, LANES), 0)
        self.ring_row = (row >= 3) & (row < 13)
        self.core_row = (row >= 4) & (row < 12)

    def put(self, field, row, column, pairs):
        row = pl.multiple_of(row, 8)
        block, offset = column >> 7, column & (LANES - 1)
        across = self.lane - offset
        ring = self.ring_row & (across >= 3) & (across < 13)
        core = self.core_row & (across >= 4) & (across < 12)
        for plane, line in pairs:
            values = jnp.broadcast_to(line, (8, LANES))
            values = pltpu.roll(values, 0, 1, stride=10, stride_axis=0)
            tile = jnp.concatenate(
                [
                    pltpu.roll(values, (offset + 11) & (LANES - 1), 1),
                    pltpu.roll(values, (offset + 91) & (LANES - 1), 1),
                ],
                axis=0,
            )
            now = field[plane, block, pl.ds(row, 16), :]
            field[plane, block, pl.ds(row, 16), :] = jnp.where(core, 0.0, now) + jnp.where(ring, tile, 0.0)


def listed(table, keeps, found):
    def step(patch, counts):
        owner, x = table[0, patch], table[1, patch]
        for row, count in enumerate(counts):
            found[row, count] = patch
        return tuple(count + jnp.where(keep(owner, x), 1, 0) for keep, count in zip(keeps, counts))

    zeros = (jnp.zeros((), I32),) * len(keeps)
    return lax.fori_loop(0, table.shape[1], step, zeros, unroll=8)


def down_kernel(
    boxes, slabs, n0, x0,
    box_list, coarse, x_low, x_high, packed,
    f_own, v_own, c1, c2, up, down, late_up, late_down,
    fb, vb, g1, v1, summed0, summed1, patches, found, sem, out_sem,
):
    edges = Edges(boxes, slabs)
    rows0, rows1, rows2 = x0 + 2 * HX, x0 // 2 + HX, x0 // 4 + HX // 2
    n1, n2 = n0 // 2, n0 // 4
    copies = (
        block_copies(x_low, fb, (2, n0), 8, HX, sem.at[0])
        + block_copies(coarse, fb, (2, n0), 8 + HX, x0, sem.at[1])
        + block_copies(x_high, fb, (2, n0), 8 + HX + x0, HX, sem.at[2])
    )
    fetch = pltpu.make_async_copy(box_list, patches, sem.at[3])
    fetch.start()
    for copy in copies:
        copy.start()
    fetch.wait()

    def row_of(owner, x):
        return (owner - edges.box) * x0 + x - 4 + HX

    def is_near(owner, x):
        row = row_of(owner, x)
        return (row >= 0) & (row < rows0)

    near_count, own_count = listed(patches, (is_near, lambda owner, x: owner == edges.box), found)
    for copy in copies:
        copy.wait()
    tiles = Tiles()

    def place(index):
        patch = found[0, index]
        lines = [(2 + z, packed[pl.ds(patch * n0 + z, 1), :]) for z in range(n0)]
        tiles.put(fb, row_of(patches[0, patch], patches[1, patch]) + 8, patches[2, patch] - 4, lines)

    lax.fori_loop(0, near_count, lambda index, carry: place(index) or carry, 0)

    inner = pl.ds(8 + HX - HU, x0 + 2 * HU)
    f_copy = pltpu.make_async_copy(fb.at[pl.ds(2, n0), :, inner, :], f_own, out_sem.at[0])
    f_copy.start()

    relax(vb, 3, (-1, n0 + 1), fb, 2, rows0, HX, edges, n0, s_planes=(0, n0), unroll=2)
    v_copy = pltpu.make_async_copy(vb.at[pl.ds(4, n0 - 2), :, inner, :], v_own, out_sem.at[1])
    v_copy.start()

    h1 = HX // 2

    def store1(index, group, value):
        value = value * edges.planes(index - 1, n1)
        g1[index + 3, group, 8 : 8 + h1, :] = value[:h1] * edges.low()
        g1[index + 3, group, 8 + h1 : 8 + rows1 - h1, :] = value[h1 : rows1 - h1]
        g1[index + 3, group, 8 + rows1 - h1 : 8 + rows1, :] = value[rows1 - h1 :] * edges.high()

    restrict(fb, 2, vb, 3, (-1, n1 + 1), rows0, summed0, store1, v_planes=(-1, n0 + 1), s_planes=(0, n0))
    for plane in range(n1 + 2):
        for b in range(g1.shape[1]):
            c1[plane, b] = g1[plane + 3, b, 8 + h1 - HU : 8 + rows1 - h1 + HU, :]

    relax(v1, 5, (-2, n1 + 2), g1, 4, rows1, h1, edges, n1, s_planes=(-1, n1 + 1), unroll=2)

    h2 = HX // 4

    def store2(index, group, value):
        c2[index, group, 0:h2, :] = value[:h2] * edges.low()
        c2[index, group, h2 : rows2 - h2, :] = value[h2 : rows2 - h2]
        c2[index, group, rows2 - h2 : rows2, :] = value[rows2 - h2 :] * edges.high()

    restrict(g1, 4, v1, 5, (-2, n2 + 2), rows1, summed1, store2, v_planes=(-2, n1 + 2), s_planes=(-1, n1 + 1))

    near = c1.shape[2] - HU
    for target, fine_plane, coarse_first in ((up, n1 + 1, n2 + 2), (down, 0, 0)):
        target[0:rows2] = c2[coarse_first, 0]
        target[rows2 : 2 * rows2] = c2[coarse_first + 1, 0]
        for b in range(c1.shape[1]):
            first = target.shape[0] - near * (c1.shape[1] - b)
            target[first : first + near] = c1[fine_plane, b, HU // 2 : HU // 2 + near, :]
    rim = 2 * rows2
    slots = (up.shape[0] - rim - near * c1.shape[1]) // 2 - 8 * fb.shape[1]
    wide = late_up.shape[0] // fb.shape[1]
    for b in range(fb.shape[1]):
        at = slice(4 + HX, 4 + HX + wide)
        late_up[wide * b : wide * (b + 1)] = fb[n0 - 1, b, at, :]
        late_down[wide * b : wide * (b + 1)] = fb[4, b, at, :]
        for z in range(2):
            first = rim + 8 * (fb.shape[1] * z + b)
            for target, plane in ((up, n0 + z), (down, 2 + z)):
                target[first : first + 3, :] = fb[plane, b, 8 + HX - 3 : 8 + HX, :]
                target[first + 3 : first + 6, :] = fb[plane, b, 8 + HX + x0 : 8 + HX + x0 + 3, :]
                target[first + 6 : first + 8, :] = jnp.zeros((2, LANES), F32)
    rim = rim + 16 * fb.shape[1]
    up[rim : rim + 2 * slots, :] = jnp.zeros((2 * slots, LANES), F32)
    down[rim : rim + 2 * slots, :] = jnp.zeros((2 * slots, LANES), F32)

    def keep(slot):
        patch = found[1, slot]
        for z in range(2):
            up[pl.ds(rim + z * slots + slot, 1), :] = packed[pl.ds(patch * n0 + n0 - 2 + z, 1), :]
            down[pl.ds(rim + z * slots + slot, 1), :] = packed[pl.ds(patch * n0 + z, 1), :]

    lax.fori_loop(0, own_count, lambda index, carry: keep(index) or carry, 0)
    f_copy.wait()
    v_copy.wait()


def total_kernel(c2, below, above, copies):
    n2, rows2 = c2.shape[0] - 4, c2.shape[2]
    for plane in range(n2):
        value = c2[2 + plane, 0]
        if plane < 2:
            value = value + below[plane * rows2 : (plane + 1) * rows2]
        if plane >= n2 - 2:
            first = (plane - (n2 - 2)) * rows2
            value = value + above[first : first + rows2]
        for slab in range(copies.shape[0]):
            copies[slab, plane * rows2 : (plane + 1) * rows2] = value


def join_kernel(c1, below, above, s1, up, down):
    n1, r1 = s1.shape[0], c1.shape[2]
    for plane in range(n1):
        s1[plane] = c1[1 + plane]
    near = r1 - HU
    cells = slice(HU // 2, HU // 2 + near)
    for b in range(s1.shape[1]):
        first = below.shape[0] - near * (s1.shape[1] - b)
        s1[0, b, cells, :] = s1[0, b, cells, :] + below[first : first + near]
        s1[n1 - 1, b, cells, :] = s1[n1 - 1, b, cells, :] + above[first : first + near]
    for p in range(4):
        for b in range(s1.shape[1]):
            first = near * (p * s1.shape[1] + b)
            up[first : first + near] = s1[n1 - 4 + p, b, HU // 2 : HU // 2 + near, :]
            down[first : first + near] = s1[p, b, HU // 2 : HU // 2 + near, :]


def third_kernel(boxes, slabs, s2, s3, fb, vb, summed):
    edges = Edges(boxes, slabs)
    planes, rows = s2.shape[0], s2.shape[1]
    zero(fb, (0, planes + 1))
    zero(vb, (0, planes + 1))
    for plane in range(planes):
        fb[plane + 1, 0, 8 : 8 + rows, :] = s2[plane]
    relax(vb, 1, (0, planes), fb, 1, rows, HX // 4, edges, None, chunk=32, unroll=4)
    quarter = planes // 4
    h3 = HX // 8
    own = rows // 2 - 2 * h3
    lanes = LANES // 2

    for part in range(2):

        def store(index, group, value, part=part):
            s3[index, :, lanes * part : lanes * (part + 1)] = value[h3 : h3 + own]

        restrict(fb, 1, vb, 1, (quarter * part, quarter * (part + 1)), rows, summed, store, unroll=quarter)


def middle_kernel(
    boxes, slabs,
    s3, s2,
    e2p,
    sc, va3, vb3, e3p, f2, v2a, v2b,
):
    edges = Edges(boxes, slabs)
    slab = edges.slab
    half, rows3 = sc.shape[0], sc.shape[2] - 16
    own3 = s3.shape[2]
    zero_rims(va3)
    zero_rims(vb3)
    for box in range(boxes):
        for plane in range(half):
            value = s3[box, plane]
            sc[plane, 0, 8 + box * own3 : 8 + (box + 1) * own3, :] = value
            va3[plane, 0, 8 + box * own3 : 8 + (box + 1) * own3, :] = C * value

    def coarsest(old, new):
        chunk = 16
        lane = iota((chunk, LANES), 1)
        for row in range(0, rows3, chunk):
            inner = slice(row + 8, row + 8 + chunk)
            for plane in range(half):
                middle = old[plane, 0, inner, :]
                before = jnp.where((lane & 63) == 0, 0.0, pltpu.roll(middle, 1, 1))
                after = jnp.where((lane & 63) == 63, 0.0, pltpu.roll(middle, LANES - 1, 1))
                if plane > 0:
                    lower = old[plane - 1, 0, inner, :]
                else:
                    lower = jnp.where(lane < 64, 0.0, pltpu.roll(old[half - 1, 0, inner, :], 64, 1))
                if plane < half - 1:
                    upper = old[plane + 1, 0, inner, :]
                else:
                    upper = jnp.where(lane < 64, pltpu.roll(old[0, 0, inner, :], 64, 1), 0.0)
                beside = old[plane, 0, row + 7 : row + 7 + chunk, :] + old[plane, 0, row + 9 : row + 9 + chunk, :]
                near = beside + ((before + after) + (lower + upper))
                new[plane, 0, inner, :] = (1.0 - OMEGA) * middle + C * (sc[plane, 0, inner, :] + near)

    def double(index):
        coarsest(va3, vb3)
        coarsest(vb3, va3)

    each((CSWEEPS - 1) // 2, double)
    coarsest(va3, vb3)

    n2, rows2 = s2.shape[0] // slabs, s2.shape[1]
    n3 = n2 // 2
    shape = (LANES, LANES)
    copy_low = (iota(shape, 0) == (iota(shape, 1) >> 1)).astype(F32)
    copy_high = (iota(shape, 0) == (iota(shape, 1) >> 1) + 64).astype(F32)
    total3 = 2 * half
    h3 = HX // 8
    window = pl.multiple_of(edges.box * own3, 8)
    for k in range(-2, n3 + 2):
        plane = slab * n3 + k
        inside = (plane >= 0) & (plane < total3)
        safe = jnp.clip(plane, 0, total3 - 1)
        upper = safe >= half
        matrix = jnp.where(upper, copy_high, copy_low) * jnp.where(inside, 1.0, 0.0)
        value = vb3[jnp.where(upper, safe - half, safe), 0, pl.ds(window, own3 + 16), :]
        value = select_dot(value, matrix.astype(BF16))[8 - h3 : 8 + own3 + h3]
        e3p[k + 2, pl.ds(0, own3 + 2 * h3, stride=2), :] = value
        e3p[k + 2, pl.ds(1, own3 + 2 * h3, stride=2), :] = value

    planes2 = s2.shape[0]
    for p in range(-5, n2 + 5):
        plane = slab * n2 + p
        inside = jnp.where((plane >= 0) & (plane < planes2), 1.0, 0.0)
        f2[p + 5, 0, 8 : 8 + rows2, :] = s2[jnp.clip(plane, 0, planes2 - 1)] * inside

    def extra2(index, b, first, size):
        return e3p[index >> 1, first : first + size, :]

    h2 = HX // 4
    relax(v2a, 5, (-4, n2 + 4), f2, 5, rows2, h2, edges, n2, extra=extra2, chunk=32, unroll=2)
    relax(v2b, 5, (-3, n2 + 3), f2, 5, rows2, h2, edges, n2, old=v2a, ooff=5, chunk=32, unroll=2)
    relax(v2a, 5, (-2, n2 + 2), f2, 5, rows2, h2, edges, n2, old=v2b, ooff=5, chunk=32, unroll=2)

    cut = h2 - HU // 2
    matrix2 = copy_matrix(LANES)
    for k in range(-2, n2 + 2):
        value = select_dot(v2a[k + 5, 0, 8 + cut : 8 + rows2 - cut, :], matrix2)
        for b in range(2):
            part = value[:, LANES * b : LANES * (b + 1)]
            e2p[k + 2, b, pl.ds(0, rows2 - 2 * cut, stride=2), :] = part
            e2p[k + 2, b, pl.ds(1, rows2 - 2 * cut, stride=2), :] = part


def first_level(edges, s1, below, above, e2p, e1, f1, v1a, v1b):
    n1, rows1 = s1.shape[0], s1.shape[2]
    near = rows1 - HU
    inner = slice(8 + HU // 2, 8 + HU // 2 + near)
    for b in range(f1.shape[1]):
        for p in range(4):
            first = near * (p * f1.shape[1] + b)
            for plane, message in ((p, below), (4 + n1 + p, above)):
                f1[plane, b, inner, :] = message[first : first + near]
        for p in range(n1):
            f1[4 + p, b, 8 : 8 + rows1, :] = s1[p, b]

    def extra1(index, b, first, size):
        return e2p[(index + 1) >> 1, b, first : first + size, :]

    relax(v1a, 4, (-3, n1 + 3), f1, 4, rows1, HU, edges, n1, extra=extra1, unroll=2)
    relax(v1b, 4, (-2, n1 + 2), f1, 4, rows1, HU, edges, n1, old=v1a, ooff=4, unroll=2)
    relax(e1, 1, (-1, n1 + 1), f1, 4, rows1, HU, edges, n1, old=v1b, ooff=4, shift=0, unroll=2)


def early_kernel(
    boxes, slabs, n0, x0, rim,
    box_list, f_own, z_below, z_above, below, above,
    f_rim, v_rim,
    fb, va, patches, found, sem, out_sem,
):
    edges = Edges(boxes, slabs)
    rows = x0 + 2 * HU
    fetch = pltpu.make_async_copy(box_list, patches, sem.at[4])
    copies = (
        [
            pltpu.make_async_copy(f_own.at[pl.ds(0, 2)], fb.at[pl.ds(2, 2), :, pl.ds(8, rows), :], sem.at[0]),
            pltpu.make_async_copy(f_own.at[pl.ds(n0 - 2, 2)], fb.at[pl.ds(4, 2), :, pl.ds(8, rows), :], sem.at[3]),
        ]
        + block_copies(z_below, fb, (0, 2), 8 + HU, x0, sem.at[1])
        + block_copies(z_above, fb, (6, 2), 8 + HU, x0, sem.at[2])
    )
    fetch.start()
    for copy in copies:
        copy.start()
    fetch.wait()

    (count,) = listed(patches, (lambda owner, x: owner == edges.box,), found)
    packed = rim + 16 * fb.shape[1]
    slots = boxes * max(2, patches.shape[1] // boxes // 4)
    for copy in copies:
        copy.wait()
    for z in range(2):
        for b in range(fb.shape[1]):
            at = rim + 8 * (fb.shape[1] * z + b)
            for plane, message in ((z, below), (6 + z, above)):
                fb[plane, b, 5 + HU : 8 + HU, :] = message[at : at + 3]
                fb[plane, b, 8 + HU + x0 : 11 + HU + x0, :] = message[at + 3 : at + 6]
    tiles = Tiles()

    def place(slot):
        lines = [(z, below, z) for z in range(2)] + [(6 + z, above, z) for z in range(2)]
        lines = [(plane, message[pl.ds(packed + z * slots + slot, 1), :]) for plane, message, z in lines]
        patch = found[0, slot]
        tiles.put(fb, patches[1, patch] - 4 + HU + 8, patches[2, patch] - 4, lines)

    lax.fori_loop(0, count, lambda index, carry: place(index) or carry, 0)
    outs = [
        pltpu.make_async_copy(fb.at[pl.ds(1, 1)], f_rim.at[pl.ds(0, 1)], out_sem.at[0]),
        pltpu.make_async_copy(fb.at[pl.ds(6, 1)], f_rim.at[pl.ds(1, 1)], out_sem.at[1]),
        pltpu.make_async_copy(va.at[pl.ds(0, 3)], v_rim.at[pl.ds(0, 3)], out_sem.at[2]),
        pltpu.make_async_copy(va.at[pl.ds(3, 3)], v_rim.at[pl.ds(3, 3)], out_sem.at[3]),
    ]
    outs[0].start()
    outs[1].start()
    relax(va, 2, (-2, 1), fb, 2, rows, HU, edges, n0, s_planes=(-2, n0), unroll=2)
    outs[2].start()
    relax(va, 4 - n0, (n0 - 1, n0 + 2), fb, 6 - n0, rows, HU, edges, n0, s_planes=(0, n0 + 2), unroll=2)
    outs[3].start()
    for out in outs:
        out.wait()


def tail_kernel(
    boxes, slabs, n0, x0,
    e2p, s1, below, above, late_below, late_above, f_own, f_rim, v_own, v_rim,
    out,
    f1, v1a, v1b, e1,
    fb, va, vb, ob, sem, out_sem,
):
    inner = pl.ds(8, x0 + 2 * HU)
    copies = [
        pltpu.make_async_copy(v_own, va.at[pl.ds(4, n0 - 2), :, inner, :], sem.at[0]),
        pltpu.make_async_copy(v_rim.at[pl.ds(0, 3)], va.at[pl.ds(1, 3)], sem.at[1]),
        pltpu.make_async_copy(v_rim.at[pl.ds(3, 3)], va.at[pl.ds(n0 + 2, 3)], sem.at[2]),
        pltpu.make_async_copy(f_own, fb.at[pl.ds(1, n0), :, inner, :], sem.at[3]),
        pltpu.make_async_copy(f_rim.at[pl.ds(0, 1)], fb.at[pl.ds(0, 1)], sem.at[4]),
        pltpu.make_async_copy(f_rim.at[pl.ds(1, 1)], fb.at[pl.ds(n0 + 1, 1)], sem.at[5]),
    ]
    for copy in copies:
        copy.start()
    edges = Edges(boxes, slabs)
    first_level(edges, s1, below, above, e2p, e1, f1, v1a, v1b)
    for copy in copies:
        copy.wait()
    rows = x0 + 2 * HU
    matrix = copy_matrix(LANES)
    cut = HU // 2
    r1 = e1.shape[2]
    size1 = r1 - 2 * cut
    wide = late_below.shape[0] // fb.shape[1]
    for b in range(fb.shape[1]):
        at = slice(4 + HU, 4 + HU + wide)
        for plane, message in ((1, late_below), (4 + n0, late_above)):
            first = wide * b
            va[plane, b, at, :] = va[plane, b, at, :] + (C * C) * message[first : first + wide]

    def prolong(k):
        for group in range(e1.shape[1]):
            value = select_dot(e1[k, group, cut : r1 - cut, :], matrix)
            for b in range(2):
                part = value[:, LANES * b : LANES * (b + 1)]
                for plane in (2 * k + 1, 2 * k + 2):
                    for start in (8, 9):
                        at = pl.ds(start, size1, stride=2)
                        va[plane, 2 * group + b, at, :] = va[plane, 2 * group + b, at, :] + part

    each(e1.shape[0], prolong, unroll=2)
    relax(vb, 3, (-1, n0 + 1), fb, 1, rows, HU, edges, n0, old=va, ooff=3, unroll=2)

    def last(z):
        view = ob.at[pl.ds(z, 1)]
        relax(view, 0, (0, 1), fb.at[pl.ds(z + 1, 1)], 0, rows, HU, edges, None, old=vb.at[pl.ds(z + 2, 3)], ooff=1, shift=-HU, cut=1)
        for copy in block_copies(out.at[pl.ds(z, 1)], ob, (z, 1), 0, x0, out_sem, back=True):
            copy.start()

    each(n0, last, unroll=2)
    for copy in block_copies(out, ob, (0, n0), 0, x0, out_sem, back=True):
        copy.wait()


def shape_of(*dims):
    return jax.ShapeDtypeStruct(dims, F32)


def scratch(*dims):
    return pltpu.VMEM(dims, F32)


def in_hbm(array):
    return pltpu.with_memory_space_constraint(array, pltpu.MemorySpace.HBM)


def limit(mebibytes):
    return pltpu.CompilerParams(vmem_limit_bytes=mebibytes << 20)


def cost(flops, moved):
    return pl.CostEstimate(flops=flops, bytes_accessed=moved, transcendentals=0)


def shift_by(array, axis, step):
    size = lax.axis_size(axis)
    pairs = [(i, i + step) for i in range(size) if 0 <= i + step < size]
    return lax.ppermute(array, axis, pairs)


def per_device(coarse, fine_div, reflux, box_list, cf_mask):
    boxes, slabs = lax.axis_size("box"), lax.axis_size("gz")
    n0, x0, y0 = coarse.shape
    n1, n2 = n0 // 2, n0 // 4
    b0, b1 = y0 // LANES, y0 // LANES // 2
    patches, fine_z, fine_lanes = fine_div.shape
    rows0, rows1, rows2 = x0 + 2 * HX, x0 // 2 + HX, x0 // 4 + HX // 2
    up_rows0, up_rows1 = x0 + 2 * HU, x0 // 2 + 2 * HU
    dma = pltpu.SemaphoreType.DMA
    hbm = pltpu.MemorySpace.HBM
    table = pltpu.SMEM((3, box_list.shape[0]), I32)

    fine_blocks = fine_lanes // LANES
    packed, x_first, x_last, z_first, z_last = pl.pallas_call(
        pack_kernel,
        name="pack",
        out_shape=(
            shape_of(patches * n0, LANES),
            shape_of(n0, HX, y0),
            shape_of(n0, HX, y0),
            shape_of(2, x0, y0),
            shape_of(2, x0, y0),
        ),
        in_specs=[HBM] * 4,
        out_specs=(VM,) * 5,
        scratch_shapes=[
            pltpu.SMEM(cf_mask.shape[::-1], I32),
            scratch(fine_blocks, patches, fine_z, LANES),
            scratch(patches, fine_z, LANES),
            dma((fine_blocks + 2,)),
            dma((4,)),
        ],
        compiler_params=limit(4),
        cost_estimate=cost(10**7, 10**6),
    )(in_hbm(cf_mask.T), in_hbm(fine_div), in_hbm(reflux), in_hbm(coarse))
    z_below = shift_by(z_last, "gz", 1)
    z_above = shift_by(z_first, "gz", -1)
    x_low = shift_by(x_last, "box", 1)
    x_high = shift_by(x_first, "box", -1)
    packed = lax.all_gather(packed, "box", axis=0, tiled=True)

    slots = boxes * max(2, patches // 4)
    rim = 2 * rows2
    message = rim + 2 * (8 * b0 + slots) + b1 * (up_rows1 - HU)
    f_own, v_own, c1, c2, up, down, late_up, late_down = pl.pallas_call(
        functools.partial(down_kernel, boxes, slabs, n0, x0),
        name="down",
        out_shape=(
            hbm((n0, b0, up_rows0, LANES), F32),
            hbm((n0 - 2, b0, up_rows0, LANES), F32),
            shape_of(n1 + 2, b1, up_rows1, LANES),
            shape_of(n2 + 4, 1, rows2, LANES),
            shape_of(message, LANES),
            shape_of(message, LANES),
            shape_of(b0 * (x0 + HU), LANES),
            shape_of(b0 * (x0 + HU), LANES),
        ),
        in_specs=[HBM] * 4 + [VM],
        out_specs=(HBM,) * 2 + (VM,) * 6,
        scratch_shapes=[
            scratch(n0 + 4, b0, rows0 + 16, LANES),
            scratch(n0 + 6, b0, rows0 + 16, LANES),
            scratch(n1 + 8, b1, rows1 + 16, LANES),
            scratch(n1 + 10, b1, rows1 + 16, LANES),
            scratch(n1 + 2, b0 // 2, rows1, 2 * LANES),
            scratch(n2 + 4, max(1, b1 // 2), rows2, min(2, b1) * LANES),
            table,
            table,
            dma((4,)),
            dma((2,)),
        ],
        compiler_params=limit(20),
        cost_estimate=cost(3 * 10**7, 10**7),
    )(in_hbm(box_list.T), in_hbm(coarse), x_low, x_high, packed)

    from_below = shift_by(up, "gz", 1)
    from_above = shift_by(down, "gz", -1)
    late_below = shift_by(late_up, "gz", 1)
    late_above = shift_by(late_down, "gz", -1)
    copies = pl.pallas_call(
        total_kernel,
        name="total",
        out_shape=shape_of(slabs, n2 * rows2, LANES),
        in_specs=[VM] * 3,
        out_specs=VM,
        compiler_params=limit(3),
        cost_estimate=cost(10**6, 10**6),
    )(c2, from_below, from_above)
    s2 = lax.all_to_all(copies, "gz", split_axis=0, concat_axis=0, tiled=True)
    s2 = s2.reshape(slabs * n2, rows2, LANES)
    last = 4 * b1 * (up_rows1 - HU)
    s1, up, down = pl.pallas_call(
        join_kernel,
        name="join",
        out_shape=(shape_of(n1, b1, up_rows1, LANES), shape_of(last, LANES), shape_of(last, LANES)),
        in_specs=[VM] * 3,
        out_specs=(VM,) * 3,
        compiler_params=limit(5),
        cost_estimate=cost(10**6, 10**6),
    )(c1, from_below, from_above)
    below = shift_by(up, "gz", 1)
    above = shift_by(down, "gz", -1)

    up_wide = up_rows0 + 16
    f_rim, v_rim = pl.pallas_call(
        functools.partial(early_kernel, boxes, slabs, n0, x0, rim),
        name="early",
        out_shape=(hbm((2, b0, up_wide, LANES), F32), hbm((6, b0, up_wide, LANES), F32)),
        in_specs=[HBM, HBM, HBM, HBM, VM, VM],
        out_specs=(HBM, HBM),
        scratch_shapes=[
            scratch(8, b0, up_wide, LANES),
            scratch(6, b0, up_wide, LANES),
            table,
            table,
            dma((5,)),
            dma((4,)),
        ],
        compiler_params=limit(10),
        cost_estimate=cost(2 * 10**7, 10**7),
    )(in_hbm(box_list.T), in_hbm(f_own), in_hbm(z_below), in_hbm(z_above), from_below, from_above)

    planes2, half = slabs * n2, slabs * n2 // 4
    own3 = x0 // 8
    s3 = pl.pallas_call(
        functools.partial(third_kernel, boxes, slabs),
        name="third",
        out_shape=shape_of(half, own3, LANES),
        in_specs=[VM],
        out_specs=VM,
        scratch_shapes=[scratch(planes2 + 2, 1, rows2 + 16, LANES)] * 2 + [scratch(half, 1, rows2 // 2, LANES)],
        compiler_params=limit(4),
        cost_estimate=cost(10**6, 10**6),
    )(s2)
    s3 = lax.all_gather(s3, "box", axis=0)
    rows3 = boxes * own3
    e2p = pl.pallas_call(
        functools.partial(middle_kernel, boxes, slabs),
        name="middle",
        out_shape=shape_of(n2 + 4, 2, up_rows1, LANES),
        in_specs=[VM] * 2,
        out_specs=VM,
        scratch_shapes=[scratch(half, 1, rows3 + 16, LANES)] * 3
        + [scratch(n2 // 2 + 4, rows2, LANES)]
        + [scratch(n2 + 10, 1, rows2 + 16, LANES)] * 3,
        compiler_params=limit(8),
        cost_estimate=cost(10**7, 2 * 10**6),
    )(s3, s2)
    return pl.pallas_call(
        functools.partial(tail_kernel, boxes, slabs, n0, x0),
        name="tail",
        out_shape=shape_of(n0, x0, y0),
        in_specs=[VM] * 6 + [HBM] * 4,
        out_specs=HBM,
        scratch_shapes=[scratch(n1 + 8, b1, up_rows1 + 16, LANES)] * 3
        + [scratch(n1 + 2, b1, up_rows1, LANES)]
        + [scratch(n0 + 2, b0, up_rows0 + 16, LANES)]
        + [scratch(n0 + 6, b0, up_rows0 + 16, LANES)] * 2
        + [scratch(n0, b0, x0, LANES), dma((6,)), dma(())],
        compiler_params=limit(24),
        cost_estimate=cost(4 * 10**7, 10**7),
    )(e2p, s1, below, above, late_below, late_above, in_hbm(f_own), in_hbm(f_rim), in_hbm(v_own), in_hbm(v_rim))


def solution(mesh):
    return jax.shard_map(
        per_device,
        mesh=mesh,
        in_specs=(P("gz", "box", None), P("box", "gz", None), P("box", "gz", None), P(), P()),
        out_specs=P("gz", "box", None),
        check_vma=False,
    )
```

```python
import functools

import jax
import jax.numpy as jnp
from jax import lax
from jax.experimental import pallas as pl
from jax.experimental.pallas import tpu as pltpu
from jax.sharding import PartitionSpec as P


CSWEEPS = 16
OMEGA = 0.8
C = OMEGA / 6.0
HX = 32
HU = 8
LANES = 128
F32 = jnp.float32
BF16 = jnp.bfloat16
I32 = jnp.int32

VM = pl.BlockSpec(memory_space=pltpu.VMEM)
SM = pl.BlockSpec(memory_space=pltpu.SMEM)
HBM = pl.BlockSpec(memory_space=pltpu.MemorySpace.HBM)


def iota(shape, dim):
    return lax.broadcasted_iota(I32, shape, dim)


def as_matrix(condition):
    return condition.astype(F32).astype(BF16)


def pair_matrix(length):
    shape = (length, length // 2)
    return as_matrix((iota(shape, 0) >> 1) == iota(shape, 1))


def copy_matrix(length):
    shape = (length, 2 * length)
    return as_matrix(iota(shape, 0) == (iota(shape, 1) >> 1))


def select_dot(values, matrix):
    high = values.astype(BF16)
    low = (values - high.astype(F32)).astype(BF16)
    return jnp.dot(high, matrix, preferred_element_type=F32) + jnp.dot(
        low, matrix, preferred_element_type=F32
    )


def each(count, body, unroll=1):
    def step(index, carry):
        body(index)
        return carry

    lax.fori_loop(0, count, step, 0, unroll=unroll)


def beside_lanes(blocks):
    lane = iota(blocks[0].shape, 1)
    right = [pltpu.roll(block, 1, 1) for block in blocks]
    left = [pltpu.roll(block, LANES - 1, 1) for block in blocks]
    sums = []
    for b in range(len(blocks)):
        before = right[b - 1] if b > 0 else 0.0
        after = left[b + 1] if b + 1 < len(blocks) else 0.0
        sums.append(
            jnp.where(lane == 0, before, right[b]) + jnp.where(lane == LANES - 1, after, left[b])
        )
    return sums


def around(field, plane, row, rows, has=(True, True, True)):
    count = field.shape[1]

    def at(p, first):
        return [field[p, b, first : first + rows, :] for b in range(count)]

    sides = [at(plane + p, row + 8) for p in (-1, 1) if has[p + 1]]
    if not has[1]:
        return None, sides[0]
    middle = at(plane, row + 8)
    beside = zip(at(plane, row + 7), at(plane, row + 9), beside_lanes(middle))
    near = [(a + b) + c for a, b, c in beside]
    for side in sides:
        near = [a + b for a, b in zip(near, side)]
    return middle, near


class Edges:
    def __init__(self, boxes, slabs):
        self.box, self.slab = lax.axis_index("box"), lax.axis_index("gz")
        self.boxes, self.slabs = boxes, slabs

    def planes(self, plane, count):
        outside = ((plane < 0) & (self.slab == 0)) | ((plane >= count) & (self.slab == self.slabs - 1))
        return jnp.where(outside, 0.0, 1.0).astype(F32)

    def low(self):
        return jnp.where(self.box == 0, 0.0, 1.0).astype(F32)

    def high(self):
        return jnp.where(self.box == self.boxes - 1, 0.0, 1.0).astype(F32)


def chunks_of(rows, halo, chunk, cut=0):
    out = [] if cut else [(0, halo, -1)]
    inner = (halo, rows - halo)
    for first in range(inner[0], inner[1], chunk):
        out.append((first, min(chunk, inner[1] - first), 0))
    return out if cut else out + [(rows - halo, halo, 1)]


def scale_of(side, edges, plane_scale):
    if side == 0:
        return plane_scale
    row_scale = edges.low() if side < 0 else edges.high()
    return row_scale if plane_scale is None else row_scale * plane_scale


def relax(new, noff, planes, source, soff, rows, halo, edges, count, old=None, ooff=0, extra=None, chunk=16, shift=8, cut=0, s_planes=None, unroll=1):
    def body(index, has=(True, True, True)):
        plane_scale = None if count is None else edges.planes(index + planes[0], count)
        for first, size, side in chunks_of(rows, halo, chunk, cut):
            scale = scale_of(side, edges, plane_scale)
            if old is None:
                middle, near = around(source, index + (planes[0] + soff), first, size, has)
                values = [(C * C) * n for n in near]
                if middle is not None:
                    values = [(1.2 * C) * m + v for m, v in zip(middle, values)]
                if extra is not None:
                    values = [v + extra(index, b, first, size) for b, v in enumerate(values)]
            else:
                middle, near = around(old, index + (planes[0] + ooff), first, size)
                at = index + (planes[0] + soff)
                values = [
                    (1.0 - OMEGA) * m + C * (source[at, b, first + 8 : first + 8 + size, :] + n)
                    for b, (m, n) in enumerate(zip(middle, near))
                ]
            for b, value in enumerate(values):
                if scale is not None:
                    value = value * scale
                new[index + (planes[0] + noff), b, first + shift : first + shift + size, :] = value

    if s_planes is None:
        each(planes[1] - planes[0], body, unroll)
        return
    inner = []
    for plane in range(*planes):
        has = tuple(s_planes[0] <= plane + p < s_planes[1] for p in (-1, 0, 1))
        if all(has):
            inner.append(plane)
        else:
            body(plane - planes[0], has)
    if inner:
        first = inner[0] - planes[0]
        each(len(inner), lambda index: body(index + first), unroll)


def restrict(source, soff, v, voff, pairs, rows, summed, store, chunk=8, v_planes=None, s_planes=None, unroll=1):
    count = v.shape[1]
    width = min(2, count)
    half = rows // 2

    def body(index, has_v=(True,) * 4, has_s=(True,) * 2):
        low_v, low_s = 2 * index + (2 * pairs[0] + voff), 2 * index + (2 * pairs[0] + soff)
        for first in range(0, half, chunk):
            size = min(chunk, half - first)

            def at(field, plane, b, offset):
                return field[plane, b, pl.ds(8 + 2 * first + offset, size, stride=2), :]

            def both(field, plane, b):
                return at(field, plane, b, 0) + at(field, plane, b, 1)

            def total_of(terms):
                total = terms[0]
                for term in terms[1:]:
                    total = total + term
                return total

            inside = [p for p in (1, 2) if has_v[p]]
            sums = []
            if inside:
                whole = [total_of([both(v, low_v + p - 1, b) for p in inside]) for b in range(count)]
                near = beside_lanes(whole)
            for b in range(count):
                terms = []
                if inside:
                    terms.append(near[b] - 4.0 * whole[b])
                    terms += [at(v, low_v + p - 1, b, -1) + at(v, low_v + p - 1, b, 2) for p in inside]
                terms += [both(source, low_s + p, b) for p in (0, 1) if has_s[p]]
                terms += [both(v, low_v + p - 1, b) for p in (0, 3) if has_v[p]]
                sums.append(total_of(terms))
            for b in range(count):
                cut = slice(LANES * (b % width), LANES * (b % width + 1))
                summed[index, b // width, first : first + size, cut] = sums[b]

    def finish():
        matrix = pair_matrix(width * LANES)
        for index in range(pairs[1] - pairs[0]):
            for group in range(count // width):
                store(index, group, 0.5 * select_dot(summed[index, group], matrix))

    if v_planes is None:
        each(pairs[1] - pairs[0], body, unroll)
        finish()
        return
    inner = []
    for coarse in range(*pairs):
        has_v = tuple(v_planes[0] <= 2 * coarse + p - 1 < v_planes[1] for p in range(4))
        has_s = tuple(s_planes[0] <= 2 * coarse + p < s_planes[1] for p in range(2))
        if all(has_v + has_s):
            inner.append(coarse)
        else:
            body(coarse - pairs[0], has_v, has_s)
    if inner:
        first = inner[0] - pairs[0]
        each(len(inner), lambda index: body(index + first), unroll)
    finish()


def zero(ref, planes):
    for plane in planes:
        ref[plane] = jnp.zeros(ref.shape[1:], F32)


def zero_rims(ref, planes=None):
    rows = ref.shape[2]
    for plane in range(ref.shape[0]) if planes is None else planes:
        for b in range(ref.shape[1]):
            ref[plane, b, 0:8, :] = jnp.zeros((8, LANES), F32)
            ref[plane, b, rows - 8 : rows, :] = jnp.zeros((8, LANES), F32)


def block_copies(wide, tiled, planes, first, rows, sem, back=False):
    copies = []
    for b in range(tiled.shape[1]):
        pair = (
            wide.at[:, :, pl.ds(LANES * b, LANES)],
            tiled.at[pl.ds(planes[0], planes[1]), b, pl.ds(first, rows), :],
        )
        copies.append(pltpu.make_async_copy(*(pair[::-1] if back else pair), sem))
    return copies


def pack_kernel(
    mask_in, fine, flux, coarse, out, x_first, x_last, z_first, z_last, mask, fine_s, flux_s, sem, edge_sem
):
    patches, fine_z = fine.shape[0], fine.shape[1]
    n0 = fine_z // 2
    blocks = fine_s.shape[0]
    copies = [
        pltpu.make_async_copy(fine.at[:, :, pl.ds(LANES * b, LANES)], fine_s.at[b], sem.at[b])
        for b in range(blocks)
    ]
    copies.append(pltpu.make_async_copy(flux, flux_s, sem.at[blocks]))
    copies.append(pltpu.make_async_copy(mask_in, mask, sem.at[blocks + 1]))
    n, x = coarse.shape[0], coarse.shape[1]
    cuts = [
        pltpu.make_async_copy(coarse.at[pl.ds(n - 2, 2)], z_last, edge_sem.at[0]),
        pltpu.make_async_copy(coarse.at[pl.ds(0, 2)], z_first, edge_sem.at[1]),
        pltpu.make_async_copy(coarse.at[:, pl.ds(x - HX, HX), :], x_last, edge_sem.at[2]),
        pltpu.make_async_copy(coarse.at[:, pl.ds(0, HX), :], x_first, edge_sem.at[3]),
    ]
    for copy in copies + cuts:
        copy.start()
    base = lax.axis_index("box") * patches
    side = (iota((n0, LANES), 1) >> 4) & 3
    source, target = iota((LANES, LANES), 0), iota((LANES, LANES), 1)
    s, i = (source >> 4) & 3, (source & 15) >> 1
    goal = jnp.where(
        s == 0, i + 91, jnp.where(s == 1, i + 1, jnp.where(s == 2, 80 - 10 * i, 89 - 10 * i))
    )
    matrices = [as_matrix(goal == target)]
    for b in range(blocks):
        place = source + LANES * b
        goal = 10 * (8 - (place >> 5)) + ((place & 15) >> 1) + 1
        matrices.append(as_matrix(goal == target))
    for copy in copies:
        copy.wait()
    masked, fine_rows = [], [[] for _ in range(blocks)]
    for patch in range(patches):
        m = [mask[s, base + patch].astype(F32) for s in range(4)]
        factor = jnp.where(side == 0, m[0], jnp.where(side == 1, m[1], jnp.where(side == 2, m[2], m[3])))
        masked.append(
            (flux_s[patch, pl.ds(0, n0, stride=2), :] + flux_s[patch, pl.ds(1, n0, stride=2), :]) * factor
        )
        for b in range(blocks):
            fine_rows[b].append(
                fine_s[b, patch, pl.ds(0, n0, stride=2), :] + fine_s[b, patch, pl.ds(1, n0, stride=2), :]
            )
    total = select_dot(jnp.concatenate(masked, axis=0), matrices[0])
    for b in range(blocks):
        total = total + select_dot(jnp.concatenate(fine_rows[b], axis=0), matrices[b + 1])
    out[...] = 0.125 * total
    for cut in cuts:
        cut.wait()


class Tiles:
    def __init__(self):
        self.lane = iota((16, LANES), 1)
        row = iota((16, LANES), 0)
        self.ring_row = (row >= 3) & (row < 13)
        self.core_row = (row >= 4) & (row < 12)

    def put(self, field, row, column, pairs):
        row = pl.multiple_of(row, 8)
        block, offset = column >> 7, column & (LANES - 1)
        across = self.lane - offset
        ring = self.ring_row & (across >= 3) & (across < 13)
        core = self.core_row & (across >= 4) & (across < 12)
        for plane, line in pairs:
            values = jnp.broadcast_to(line, (8, LANES))
            values = pltpu.roll(values, 0, 1, stride=10, stride_axis=0)
            tile = jnp.concatenate(
                [
                    pltpu.roll(values, (offset + 11) & (LANES - 1), 1),
                    pltpu.roll(values, (offset + 91) & (LANES - 1), 1),
                ],
                axis=0,
            )
            now = field[plane, block, pl.ds(row, 16), :]
            field[plane, block, pl.ds(row, 16), :] = jnp.where(core, 0.0, now) + jnp.where(ring, tile, 0.0)


def listed(table, keeps, found):
    def step(patch, counts):
        owner, x = table[0, patch], table[1, patch]
        for row, count in enumerate(counts):
            found[row, count] = patch
        return tuple(count + jnp.where(keep(owner, x), 1, 0) for keep, count in zip(keeps, counts))

    zeros = (jnp.zeros((), I32),) * len(keeps)
    return lax.fori_loop(0, table.shape[1], step, zeros, unroll=8)


def down_kernel(
    boxes, slabs, n0, x0,
    box_list, coarse, x_low, x_high, packed,
    f_own, v_own, c1, c2, up, down, late_up, late_down,
    fb, vb, g1, v1, summed0, summed1, patches, found, sem, out_sem,
):
    edges = Edges(boxes, slabs)
    rows0, rows1, rows2 = x0 + 2 * HX, x0 // 2 + HX, x0 // 4 + HX // 2
    n1, n2 = n0 // 2, n0 // 4
    copies = (
        block_copies(x_low, fb, (2, n0), 8, HX, sem.at[0])
        + block_copies(coarse, fb, (2, n0), 8 + HX, x0, sem.at[1])
        + block_copies(x_high, fb, (2, n0), 8 + HX + x0, HX, sem.at[2])
    )
    fetch = pltpu.make_async_copy(box_list, patches, sem.at[3])
    fetch.start()
    for copy in copies:
        copy.start()
    fetch.wait()

    def row_of(owner, x):
        return (owner - edges.box) * x0 + x - 4 + HX

    def is_near(owner, x):
        row = row_of(owner, x)
        return (row >= 0) & (row < rows0)

    near_count, own_count = listed(patches, (is_near, lambda owner, x: owner == edges.box), found)
    for copy in copies:
        copy.wait()
    tiles = Tiles()

    def place(index):
        patch = found[0, index]
        lines = [(2 + z, packed[pl.ds(patch * n0 + z, 1), :]) for z in range(n0)]
        tiles.put(fb, row_of(patches[0, patch], patches[1, patch]) + 8, patches[2, patch] - 4, lines)

    lax.fori_loop(0, near_count, lambda index, carry: place(index) or carry, 0)

    inner = pl.ds(8 + HX - HU, x0 + 2 * HU)
    f_copy = pltpu.make_async_copy(fb.at[pl.ds(2, n0), :, inner, :], f_own, out_sem.at[0])
    f_copy.start()

    relax(vb, 3, (-1, n0 + 1), fb, 2, rows0, HX, edges, n0, s_planes=(0, n0), unroll=3)
    v_copy = pltpu.make_async_copy(vb.at[pl.ds(4, n0 - 2), :, inner, :], v_own, out_sem.at[1])
    v_copy.start()

    h1 = HX // 2

    def store1(index, group, value):
        value = value * edges.planes(index - 1, n1)
        g1[index + 3, group, 8 : 8 + h1, :] = value[:h1] * edges.low()
        g1[index + 3, group, 8 + h1 : 8 + rows1 - h1, :] = value[h1 : rows1 - h1]
        g1[index + 3, group, 8 + rows1 - h1 : 8 + rows1, :] = value[rows1 - h1 :] * edges.high()

    restrict(fb, 2, vb, 3, (-1, n1 + 1), rows0, summed0, store1, v_planes=(-1, n0 + 1), s_planes=(0, n0))
    for plane in range(n1 + 2):
        for b in range(g1.shape[1]):
            c1[plane, b] = g1[plane + 3, b, 8 + h1 - HU : 8 + rows1 - h1 + HU, :]

    relax(v1, 5, (-2, n1 + 2), g1, 4, rows1, h1, edges, n1, s_planes=(-1, n1 + 1), unroll=2)

    h2 = HX // 4

    def store2(index, group, value):
        c2[index, group, 0:h2, :] = value[:h2] * edges.low()
        c2[index, group, h2 : rows2 - h2, :] = value[h2 : rows2 - h2]
        c2[index, group, rows2 - h2 : rows2, :] = value[rows2 - h2 :] * edges.high()

    restrict(g1, 4, v1, 5, (-2, n2 + 2), rows1, summed1, store2, v_planes=(-2, n1 + 2), s_planes=(-1, n1 + 1))

    near = c1.shape[2] - HU
    for target, fine_plane, coarse_first in ((up, n1 + 1, n2 + 2), (down, 0, 0)):
        target[0:rows2] = c2[coarse_first, 0]
        target[rows2 : 2 * rows2] = c2[coarse_first + 1, 0]
        for b in range(c1.shape[1]):
            first = target.shape[0] - near * (c1.shape[1] - b)
            target[first : first + near] = c1[fine_plane, b, HU // 2 : HU // 2 + near, :]
    rim = 2 * rows2
    slots = (up.shape[0] - rim - near * c1.shape[1]) // 2 - 8 * fb.shape[1]
    wide = late_up.shape[0] // fb.shape[1]
    for b in range(fb.shape[1]):
        at = slice(4 + HX, 4 + HX + wide)
        late_up[wide * b : wide * (b + 1)] = fb[n0 - 1, b, at, :]
        late_down[wide * b : wide * (b + 1)] = fb[4, b, at, :]
        for z in range(2):
            first = rim + 8 * (fb.shape[1] * z + b)
            for target, plane in ((up, n0 + z), (down, 2 + z)):
                target[first : first + 3, :] = fb[plane, b, 8 + HX - 3 : 8 + HX, :]
                target[first + 3 : first + 6, :] = fb[plane, b, 8 + HX + x0 : 8 + HX + x0 + 3, :]
                target[first + 6 : first + 8, :] = jnp.zeros((2, LANES), F32)
    rim = rim + 16 * fb.shape[1]
    up[rim : rim + 2 * slots, :] = jnp.zeros((2 * slots, LANES), F32)
    down[rim : rim + 2 * slots, :] = jnp.zeros((2 * slots, LANES), F32)

    def keep(slot):
        patch = found[1, slot]
        for z in range(2):
            up[pl.ds(rim + z * slots + slot, 1), :] = packed[pl.ds(patch * n0 + n0 - 2 + z, 1), :]
            down[pl.ds(rim + z * slots + slot, 1), :] = packed[pl.ds(patch * n0 + z, 1), :]

    lax.fori_loop(0, own_count, lambda index, carry: keep(index) or carry, 0)
    f_copy.wait()
    v_copy.wait()


def total_kernel(c2, below, above, copies):
    n2, rows2 = c2.shape[0] - 4, c2.shape[2]
    for plane in range(n2):
        value = c2[2 + plane, 0]
        if plane < 2:
            value = value + below[plane * rows2 : (plane + 1) * rows2]
        if plane >= n2 - 2:
            first = (plane - (n2 - 2)) * rows2
            value = value + above[first : first + rows2]
        for slab in range(copies.shape[0]):
            copies[slab, plane * rows2 : (plane + 1) * rows2] = value


def join_kernel(c1, below, above, s1, up, down):
    n1, r1 = s1.shape[0], c1.shape[2]
    for plane in range(n1):
        s1[plane] = c1[1 + plane]
    near = r1 - HU
    cells = slice(HU // 2, HU // 2 + near)
    for b in range(s1.shape[1]):
        first = below.shape[0] - near * (s1.shape[1] - b)
        s1[0, b, cells, :] = s1[0, b, cells, :] + below[first : first + near]
        s1[n1 - 1, b, cells, :] = s1[n1 - 1, b, cells, :] + above[first : first + near]
    for p in range(4):
        for b in range(s1.shape[1]):
            first = near * (p * s1.shape[1] + b)
            up[first : first + near] = s1[n1 - 4 + p, b, HU // 2 : HU // 2 + near, :]
            down[first : first + near] = s1[p, b, HU // 2 : HU // 2 + near, :]


def third_kernel(boxes, slabs, s2, s3, fb, vb, summed):
    edges = Edges(boxes, slabs)
    planes, rows = s2.shape[0], s2.shape[1]
    zero(fb, (0, planes + 1))
    zero(vb, (0, planes + 1))
    for plane in range(planes):
        fb[plane + 1, 0, 8 : 8 + rows, :] = s2[plane]
    relax(vb, 1, (0, planes), fb, 1, rows, HX // 4, edges, None, chunk=32, unroll=4)
    quarter = planes // 4
    h3 = HX // 8
    own = rows // 2 - 2 * h3
    lanes = LANES // 2

    for part in range(2):

        def store(index, group, value, part=part):
            s3[index, :, lanes * part : lanes * (part + 1)] = value[h3 : h3 + own]

        restrict(fb, 1, vb, 1, (quarter * part, quarter * (part + 1)), rows, summed, store, unroll=quarter)


def middle_kernel(
    boxes, slabs,
    s3, s2,
    e2p,
    sc, va3, vb3, e3p, f2, v2a, v2b,
):
    edges = Edges(boxes, slabs)
    slab = edges.slab
    half, rows3 = sc.shape[0], sc.shape[2] - 16
    own3 = s3.shape[2]
    zero_rims(va3)
    zero_rims(vb3)
    for box in range(boxes):
        for plane in range(half):
            value = s3[box, plane]
            sc[plane, 0, 8 + box * own3 : 8 + (box + 1) * own3, :] = value
            va3[plane, 0, 8 + box * own3 : 8 + (box + 1) * own3, :] = C * value

    def coarsest(old, new):
        chunk = 16
        lane = iota((chunk, LANES), 1)
        for row in range(0, rows3, chunk):
            inner = slice(row + 8, row + 8 + chunk)
            for plane in range(half):
                middle = old[plane, 0, inner, :]
                before = jnp.where((lane & 63) == 0, 0.0, pltpu.roll(middle, 1, 1))
                after = jnp.where((lane & 63) == 63, 0.0, pltpu.roll(middle, LANES - 1, 1))
                if plane > 0:
                    lower = old[plane - 1, 0, inner, :]
                else:
                    lower = jnp.where(lane < 64, 0.0, pltpu.roll(old[half - 1, 0, inner, :], 64, 1))
                if plane < half - 1:
                    upper = old[plane + 1, 0, inner, :]
                else:
                    upper = jnp.where(lane < 64, pltpu.roll(old[0, 0, inner, :], 64, 1), 0.0)
                beside = old[plane, 0, row + 7 : row + 7 + chunk, :] + old[plane, 0, row + 9 : row + 9 + chunk, :]
                near = beside + ((before + after) + (lower + upper))
                new[plane, 0, inner, :] = (1.0 - OMEGA) * middle + C * (sc[plane, 0, inner, :] + near)

    def double(index):
        coarsest(va3, vb3)
        coarsest(vb3, va3)

    each((CSWEEPS - 1) // 2, double)
    coarsest(va3, vb3)

    n2, rows2 = s2.shape[0] // slabs, s2.shape[1]
    n3 = n2 // 2
    shape = (LANES, LANES)
    copy_low = (iota(shape, 0) == (iota(shape, 1) >> 1)).astype(F32)
    copy_high = (iota(shape, 0) == (iota(shape, 1) >> 1) + 64).astype(F32)
    total3 = 2 * half
    h3 = HX // 8
    window = pl.multiple_of(edges.box * own3, 8)
    for k in range(-2, n3 + 2):
        plane = slab * n3 + k
        inside = (plane >= 0) & (plane < total3)
        safe = jnp.clip(plane, 0, total3 - 1)
        upper = safe >= half
        matrix = jnp.where(upper, copy_high, copy_low) * jnp.where(inside, 1.0, 0.0)
        value = vb3[jnp.where(upper, safe - half, safe), 0, pl.ds(window, own3 + 16), :]
        value = select_dot(value, matrix.astype(BF16))[8 - h3 : 8 + own3 + h3]
        e3p[k + 2, pl.ds(0, own3 + 2 * h3, stride=2), :] = value
        e3p[k + 2, pl.ds(1, own3 + 2 * h3, stride=2), :] = value

    planes2 = s2.shape[0]
    for p in range(-5, n2 + 5):
        plane = slab * n2 + p
        inside = jnp.where((plane >= 0) & (plane < planes2), 1.0, 0.0)
        f2[p + 5, 0, 8 : 8 + rows2, :] = s2[jnp.clip(plane, 0, planes2 - 1)] * inside

    def extra2(index, b, first, size):
        return e3p[index >> 1, first : first + size, :]

    h2 = HX // 4
    relax(v2a, 5, (-4, n2 + 4), f2, 5, rows2, h2, edges, n2, extra=extra2, chunk=32, unroll=2)
    relax(v2b, 5, (-3, n2 + 3), f2, 5, rows2, h2, edges, n2, old=v2a, ooff=5, chunk=32, unroll=2)
    relax(v2a, 5, (-2, n2 + 2), f2, 5, rows2, h2, edges, n2, old=v2b, ooff=5, chunk=32, unroll=2)

    cut = h2 - HU // 2
    matrix2 = copy_matrix(LANES)
    for k in range(-2, n2 + 2):
        value = select_dot(v2a[k + 5, 0, 8 + cut : 8 + rows2 - cut, :], matrix2)
        for b in range(2):
            part = value[:, LANES * b : LANES * (b + 1)]
            e2p[k + 2, b, pl.ds(0, rows2 - 2 * cut, stride=2), :] = part
            e2p[k + 2, b, pl.ds(1, rows2 - 2 * cut, stride=2), :] = part


def first_level(edges, s1, below, above, e2p, e1, f1, v1a, v1b):
    n1, rows1 = s1.shape[0], s1.shape[2]
    near = rows1 - HU
    inner = slice(8 + HU // 2, 8 + HU // 2 + near)
    for b in range(f1.shape[1]):
        for p in range(4):
            first = near * (p * f1.shape[1] + b)
            for plane, message in ((p, below), (4 + n1 + p, above)):
                f1[plane, b, inner, :] = message[first : first + near]
        for p in range(n1):
            f1[4 + p, b, 8 : 8 + rows1, :] = s1[p, b]

    def extra1(index, b, first, size):
        return e2p[(index + 1) >> 1, b, first : first + size, :]

    relax(v1a, 4, (-3, n1 + 3), f1, 4, rows1, HU, edges, n1, extra=extra1, unroll=2)
    relax(v1b, 4, (-2, n1 + 2), f1, 4, rows1, HU, edges, n1, old=v1a, ooff=4, unroll=2)
    relax(e1, 1, (-1, n1 + 1), f1, 4, rows1, HU, edges, n1, old=v1b, ooff=4, shift=0, unroll=2)


def early_kernel(
    boxes, slabs, n0, x0, rim,
    box_list, f_own, z_below, z_above, below, above,
    f_rim, v_rim,
    fb, va, patches, found, sem, out_sem,
):
    edges = Edges(boxes, slabs)
    rows = x0 + 2 * HU
    fetch = pltpu.make_async_copy(box_list, patches, sem.at[4])
    copies = (
        [
            pltpu.make_async_copy(f_own.at[pl.ds(0, 2)], fb.at[pl.ds(2, 2), :, pl.ds(8, rows), :], sem.at[0]),
            pltpu.make_async_copy(f_own.at[pl.ds(n0 - 2, 2)], fb.at[pl.ds(4, 2), :, pl.ds(8, rows), :], sem.at[3]),
        ]
        + block_copies(z_below, fb, (0, 2), 8 + HU, x0, sem.at[1])
        + block_copies(z_above, fb, (6, 2), 8 + HU, x0, sem.at[2])
    )
    fetch.start()
    for copy in copies:
        copy.start()
    fetch.wait()

    (count,) = listed(patches, (lambda owner, x: owner == edges.box,), found)
    packed = rim + 16 * fb.shape[1]
    slots = boxes * max(2, patches.shape[1] // boxes // 4)
    for copy in copies:
        copy.wait()
    for z in range(2):
        for b in range(fb.shape[1]):
            at = rim + 8 * (fb.shape[1] * z + b)
            for plane, message in ((z, below), (6 + z, above)):
                fb[plane, b, 5 + HU : 8 + HU, :] = message[at : at + 3]
                fb[plane, b, 8 + HU + x0 : 11 + HU + x0, :] = message[at + 3 : at + 6]
    tiles = Tiles()

    def place(slot):
        lines = [(z, below, z) for z in range(2)] + [(6 + z, above, z) for z in range(2)]
        lines = [(plane, message[pl.ds(packed + z * slots + slot, 1), :]) for plane, message, z in lines]
        patch = found[0, slot]
        tiles.put(fb, patches[1, patch] - 4 + HU + 8, patches[2, patch] - 4, lines)

    lax.fori_loop(0, count, lambda index, carry: place(index) or carry, 0)
    outs = [
        pltpu.make_async_copy(fb.at[pl.ds(1, 1)], f_rim.at[pl.ds(0, 1)], out_sem.at[0]),
        pltpu.make_async_copy(fb.at[pl.ds(6, 1)], f_rim.at[pl.ds(1, 1)], out_sem.at[1]),
        pltpu.make_async_copy(va.at[pl.ds(0, 3)], v_rim.at[pl.ds(0, 3)], out_sem.at[2]),
        pltpu.make_async_copy(va.at[pl.ds(3, 3)], v_rim.at[pl.ds(3, 3)], out_sem.at[3]),
    ]
    outs[0].start()
    outs[1].start()
    relax(va, 2, (-2, 1), fb, 2, rows, HU, edges, n0, s_planes=(-2, n0), unroll=2)
    outs[2].start()
    relax(va, 4 - n0, (n0 - 1, n0 + 2), fb, 6 - n0, rows, HU, edges, n0, s_planes=(0, n0 + 2), unroll=2)
    outs[3].start()
    for out in outs:
        out.wait()


def tail_kernel(
    boxes, slabs, n0, x0,
    e2p, s1, below, above, late_below, late_above, f_own, f_rim, v_own, v_rim,
    out,
    f1, v1a, v1b, e1,
    fb, va, vb, ob, sem, out_sem,
):
    inner = pl.ds(8, x0 + 2 * HU)
    copies = [
        pltpu.make_async_copy(v_own, va.at[pl.ds(4, n0 - 2), :, inner, :], sem.at[0]),
        pltpu.make_async_copy(v_rim.at[pl.ds(0, 3)], va.at[pl.ds(1, 3)], sem.at[1]),
        pltpu.make_async_copy(v_rim.at[pl.ds(3, 3)], va.at[pl.ds(n0 + 2, 3)], sem.at[2]),
        pltpu.make_async_copy(f_own, fb.at[pl.ds(1, n0), :, inner, :], sem.at[3]),
        pltpu.make_async_copy(f_rim.at[pl.ds(0, 1)], fb.at[pl.ds(0, 1)], sem.at[4]),
        pltpu.make_async_copy(f_rim.at[pl.ds(1, 1)], fb.at[pl.ds(n0 + 1, 1)], sem.at[5]),
    ]
    for copy in copies:
        copy.start()
    edges = Edges(boxes, slabs)
    first_level(edges, s1, below, above, e2p, e1, f1, v1a, v1b)
    for copy in copies:
        copy.wait()
    rows = x0 + 2 * HU
    matrix = copy_matrix(LANES)
    cut = HU // 2
    r1 = e1.shape[2]
    size1 = r1 - 2 * cut
    wide = late_below.shape[0] // fb.shape[1]
    for b in range(fb.shape[1]):
        at = slice(4 + HU, 4 + HU + wide)
        for plane, message in ((1, late_below), (4 + n0, late_above)):
            first = wide * b
            va[plane, b, at, :] = va[plane, b, at, :] + (C * C) * message[first : first + wide]

    def prolong(k):
        for group in range(e1.shape[1]):
            value = select_dot(e1[k, group, cut : r1 - cut, :], matrix)
            for b in range(2):
                part = value[:, LANES * b : LANES * (b + 1)]
                for plane in (2 * k + 1, 2 * k + 2):
                    for start in (8, 9):
                        at = pl.ds(start, size1, stride=2)
                        va[plane, 2 * group + b, at, :] = va[plane, 2 * group + b, at, :] + part

    each(e1.shape[0], prolong, unroll=3)
    relax(vb, 3, (-1, n0 + 1), fb, 1, rows, HU, edges, n0, old=va, ooff=3, unroll=5)

    def last(z):
        view = ob.at[pl.ds(z, 1)]
        relax(view, 0, (0, 1), fb.at[pl.ds(z + 1, 1)], 0, rows, HU, edges, None, old=vb.at[pl.ds(z + 2, 3)], ooff=1, shift=-HU, cut=1)
        for copy in block_copies(out.at[pl.ds(z, 1)], ob, (z, 1), 0, x0, out_sem, back=True):
            copy.start()

    each(n0, last, unroll=4)
    for copy in block_copies(out, ob, (0, n0), 0, x0, out_sem, back=True):
        copy.wait()


def shape_of(*dims):
    return jax.ShapeDtypeStruct(dims, F32)


def scratch(*dims):
    return pltpu.VMEM(dims, F32)


def in_hbm(array):
    return pltpu.with_memory_space_constraint(array, pltpu.MemorySpace.HBM)


def limit(mebibytes):
    return pltpu.CompilerParams(vmem_limit_bytes=mebibytes << 20)


def cost(flops, moved):
    return pl.CostEstimate(flops=flops, bytes_accessed=moved, transcendentals=0)


def shift_by(array, axis, step):
    size = lax.axis_size(axis)
    pairs = [(i, i + step) for i in range(size) if 0 <= i + step < size]
    return lax.ppermute(array, axis, pairs)


def per_device(coarse, fine_div, reflux, box_list, cf_mask):
    boxes, slabs = lax.axis_size("box"), lax.axis_size("gz")
    n0, x0, y0 = coarse.shape
    n1, n2 = n0 // 2, n0 // 4
    b0, b1 = y0 // LANES, y0 // LANES // 2
    patches, fine_z, fine_lanes = fine_div.shape
    rows0, rows1, rows2 = x0 + 2 * HX, x0 // 2 + HX, x0 // 4 + HX // 2
    up_rows0, up_rows1 = x0 + 2 * HU, x0 // 2 + 2 * HU
    dma = pltpu.SemaphoreType.DMA
    hbm = pltpu.MemorySpace.HBM
    table = pltpu.SMEM((3, box_list.shape[0]), I32)

    fine_blocks = fine_lanes // LANES
    packed, x_first, x_last, z_first, z_last = pl.pallas_call(
        pack_kernel,
        name="pack",
        out_shape=(
            shape_of(patches * n0, LANES),
            shape_of(n0, HX, y0),
            shape_of(n0, HX, y0),
            shape_of(2, x0, y0),
            shape_of(2, x0, y0),
        ),
        in_specs=[HBM] * 4,
        out_specs=(VM,) * 5,
        scratch_shapes=[
            pltpu.SMEM(cf_mask.shape[::-1], I32),
            scratch(fine_blocks, patches, fine_z, LANES),
            scratch(patches, fine_z, LANES),
            dma((fine_blocks + 2,)),
            dma((4,)),
        ],
        compiler_params=limit(4),
        cost_estimate=cost(10**7, 10**6),
    )(in_hbm(cf_mask.T), in_hbm(fine_div), in_hbm(reflux), in_hbm(coarse))
    z_below = shift_by(z_last, "gz", 1)
    z_above = shift_by(z_first, "gz", -1)
    x_low = shift_by(x_last, "box", 1)
    x_high = shift_by(x_first, "box", -1)
    packed = lax.all_gather(packed, "box", axis=0, tiled=True)

    slots = boxes * max(2, patches // 4)
    rim = 2 * rows2
    message = rim + 2 * (8 * b0 + slots) + b1 * (up_rows1 - HU)
    f_own, v_own, c1, c2, up, down, late_up, late_down = pl.pallas_call(
        functools.partial(down_kernel, boxes, slabs, n0, x0),
        name="down",
        out_shape=(
            hbm((n0, b0, up_rows0, LANES), F32),
            hbm((n0 - 2, b0, up_rows0, LANES), F32),
            shape_of(n1 + 2, b1, up_rows1, LANES),
            shape_of(n2 + 4, 1, rows2, LANES),
            shape_of(message, LANES),
            shape_of(message, LANES),
            shape_of(b0 * (x0 + HU), LANES),
            shape_of(b0 * (x0 + HU), LANES),
        ),
        in_specs=[HBM] * 4 + [VM],
        out_specs=(HBM,) * 2 + (VM,) * 6,
        scratch_shapes=[
            scratch(n0 + 4, b0, rows0 + 16, LANES),
            scratch(n0 + 6, b0, rows0 + 16, LANES),
            scratch(n1 + 8, b1, rows1 + 16, LANES),
            scratch(n1 + 10, b1, rows1 + 16, LANES),
            scratch(n1 + 2, b0 // 2, rows1, 2 * LANES),
            scratch(n2 + 4, max(1, b1 // 2), rows2, min(2, b1) * LANES),
            table,
            table,
            dma((4,)),
            dma((2,)),
        ],
        compiler_params=limit(20),
        cost_estimate=cost(3 * 10**7, 10**7),
    )(in_hbm(box_list.T), in_hbm(coarse), x_low, x_high, packed)

    from_below = shift_by(up, "gz", 1)
    from_above = shift_by(down, "gz", -1)
    late_below = shift_by(late_up, "gz", 1)
    late_above = shift_by(late_down, "gz", -1)
    copies = pl.pallas_call(
        total_kernel,
        name="total",
        out_shape=shape_of(slabs, n2 * rows2, LANES),
        in_specs=[VM] * 3,
        out_specs=VM,
        compiler_params=limit(3),
        cost_estimate=cost(10**6, 10**6),
    )(c2, from_below, from_above)
    s2 = lax.all_to_all(copies, "gz", split_axis=0, concat_axis=0, tiled=True)
    s2 = s2.reshape(slabs * n2, rows2, LANES)
    last = 4 * b1 * (up_rows1 - HU)
    s1, up, down = pl.pallas_call(
        join_kernel,
        name="join",
        out_shape=(shape_of(n1, b1, up_rows1, LANES), shape_of(last, LANES), shape_of(last, LANES)),
        in_specs=[VM] * 3,
        out_specs=(VM,) * 3,
        compiler_params=limit(5),
        cost_estimate=cost(10**6, 10**6),
    )(c1, from_below, from_above)
    below = shift_by(up, "gz", 1)
    above = shift_by(down, "gz", -1)

    up_wide = up_rows0 + 16
    f_rim, v_rim = pl.pallas_call(
        functools.partial(early_kernel, boxes, slabs, n0, x0, rim),
        name="early",
        out_shape=(hbm((2, b0, up_wide, LANES), F32), hbm((6, b0, up_wide, LANES), F32)),
        in_specs=[HBM, HBM, HBM, HBM, VM, VM],
        out_specs=(HBM, HBM),
        scratch_shapes=[
            scratch(8, b0, up_wide, LANES),
            scratch(6, b0, up_wide, LANES),
            table,
            table,
            dma((5,)),
            dma((4,)),
        ],
        compiler_params=limit(10),
        cost_estimate=cost(2 * 10**7, 10**7),
    )(in_hbm(box_list.T), in_hbm(f_own), in_hbm(z_below), in_hbm(z_above), from_below, from_above)

    planes2, half = slabs * n2, slabs * n2 // 4
    own3 = x0 // 8
    s3 = pl.pallas_call(
        functools.partial(third_kernel, boxes, slabs),
        name="third",
        out_shape=shape_of(half, own3, LANES),
        in_specs=[VM],
        out_specs=VM,
        scratch_shapes=[scratch(planes2 + 2, 1, rows2 + 16, LANES)] * 2 + [scratch(half, 1, rows2 // 2, LANES)],
        compiler_params=limit(4),
        cost_estimate=cost(10**6, 10**6),
    )(s2)
    s3 = lax.all_gather(s3, "box", axis=0)
    rows3 = boxes * own3
    e2p = pl.pallas_call(
        functools.partial(middle_kernel, boxes, slabs),
        name="middle",
        out_shape=shape_of(n2 + 4, 2, up_rows1, LANES),
        in_specs=[VM] * 2,
        out_specs=VM,
        scratch_shapes=[scratch(half, 1, rows3 + 16, LANES)] * 3
        + [scratch(n2 // 2 + 4, rows2, LANES)]
        + [scratch(n2 + 10, 1, rows2 + 16, LANES)] * 3,
        compiler_params=limit(8),
        cost_estimate=cost(10**7, 2 * 10**6),
    )(s3, s2)
    return pl.pallas_call(
        functools.partial(tail_kernel, boxes, slabs, n0, x0),
        name="tail",
        out_shape=shape_of(n0, x0, y0),
        in_specs=[VM] * 6 + [HBM] * 4,
        out_specs=HBM,
        scratch_shapes=[scratch(n1 + 8, b1, up_rows1 + 16, LANES)] * 3
        + [scratch(n1 + 2, b1, up_rows1, LANES)]
        + [scratch(n0 + 2, b0, up_rows0 + 16, LANES)]
        + [scratch(n0 + 6, b0, up_rows0 + 16, LANES)] * 2
        + [scratch(n0, b0, x0, LANES), dma((6,)), dma(())],
        compiler_params=limit(24),
        cost_estimate=cost(4 * 10**7, 10**7),
    )(e2p, s1, below, above, late_below, late_above, in_hbm(f_own), in_hbm(f_rim), in_hbm(v_own), in_hbm(v_rim))


def solution(mesh):
    return jax.shard_map(
        per_device,
        mesh=mesh,
        in_specs=(P("gz", "box", None), P("box", "gz", None), P("box", "gz", None), P(), P()),
        out_specs=P("gz", "box", None),
        check_vma=False,
    )
```

```python
import functools

import jax
import jax.numpy as jnp
from jax import lax
from jax.experimental import pallas as pl
from jax.experimental.pallas import tpu as pltpu
from jax.sharding import PartitionSpec as P


CSWEEPS = 16
OMEGA = 0.8
C = OMEGA / 6.0
HX = 32
HU = 8
LANES = 128
F32 = jnp.float32
BF16 = jnp.bfloat16
I32 = jnp.int32

VM = pl.BlockSpec(memory_space=pltpu.VMEM)
SM = pl.BlockSpec(memory_space=pltpu.SMEM)
HBM = pl.BlockSpec(memory_space=pltpu.MemorySpace.HBM)


def iota(shape, dim):
    return lax.broadcasted_iota(I32, shape, dim)


def as_matrix(condition):
    return condition.astype(F32).astype(BF16)


def pair_matrix(length):
    shape = (length, length // 2)
    return as_matrix((iota(shape, 0) >> 1) == iota(shape, 1))


def copy_matrix(length):
    shape = (length, 2 * length)
    return as_matrix(iota(shape, 0) == (iota(shape, 1) >> 1))


def select_dot(values, matrix):
    high = values.astype(BF16)
    low = (values - high.astype(F32)).astype(BF16)
    return jnp.dot(high, matrix, preferred_element_type=F32) + jnp.dot(
        low, matrix, preferred_element_type=F32
    )


def each(count, body, unroll=1):
    def step(index, carry):
        body(index)
        return carry

    lax.fori_loop(0, count, step, 0, unroll=unroll)


def beside_lanes(blocks):
    lane = iota(blocks[0].shape, 1)
    right = [pltpu.roll(block, 1, 1) for block in blocks]
    left = [pltpu.roll(block, LANES - 1, 1) for block in blocks]
    sums = []
    for b in range(len(blocks)):
        before = right[b - 1] if b > 0 else 0.0
        after = left[b + 1] if b + 1 < len(blocks) else 0.0
        sums.append(
            jnp.where(lane == 0, before, right[b]) + jnp.where(lane == LANES - 1, after, left[b])
        )
    return sums


def around(field, plane, row, rows, has=(True, True, True)):
    count = field.shape[1]

    def at(p, first):
        return [field[p, b, first : first + rows, :] for b in range(count)]

    sides = [at(plane + p, row + 8) for p in (-1, 1) if has[p + 1]]
    if not has[1]:
        return None, sides[0]
    middle = at(plane, row + 8)
    beside = zip(at(plane, row + 7), at(plane, row + 9), beside_lanes(middle))
    near = [(a + b) + c for a, b, c in beside]
    for side in sides:
        near = [a + b for a, b in zip(near, side)]
    return middle, near


class Edges:
    def __init__(self, boxes, slabs):
        self.box, self.slab = lax.axis_index("box"), lax.axis_index("gz")
        self.boxes, self.slabs = boxes, slabs

    def planes(self, plane, count):
        outside = ((plane < 0) & (self.slab == 0)) | ((plane >= count) & (self.slab == self.slabs - 1))
        return jnp.where(outside, 0.0, 1.0).astype(F32)

    def low(self):
        return jnp.where(self.box == 0, 0.0, 1.0).astype(F32)

    def high(self):
        return jnp.where(self.box == self.boxes - 1, 0.0, 1.0).astype(F32)


def chunks_of(rows, halo, chunk, cut=0):
    out = [] if cut else [(0, halo, -1)]
    inner = (halo, rows - halo)
    for first in range(inner[0], inner[1], chunk):
        out.append((first, min(chunk, inner[1] - first), 0))
    return out if cut else out + [(rows - halo, halo, 1)]


def scale_of(side, edges, plane_scale):
    if side == 0:
        return plane_scale
    row_scale = edges.low() if side < 0 else edges.high()
    return row_scale if plane_scale is None else row_scale * plane_scale


def relax(new, noff, planes, source, soff, rows, halo, edges, count, old=None, ooff=0, extra=None, chunk=16, shift=8, cut=0, s_planes=None, unroll=1):
    def body(index, has=(True, True, True)):
        plane_scale = None if count is None else edges.planes(index + planes[0], count)
        for first, size, side in chunks_of(rows, halo, chunk, cut):
            scale = scale_of(side, edges, plane_scale)
            if old is None:
                middle, near = around(source, index + (planes[0] + soff), first, size, has)
                values = [(C * C) * n for n in near]
                if middle is not None:
                    values = [(1.2 * C) * m + v for m, v in zip(middle, values)]
                if extra is not None:
                    values = [v + extra(index, b, first, size) for b, v in enumerate(values)]
            else:
                middle, near = around(old, index + (planes[0] + ooff), first, size)
                at = index + (planes[0] + soff)
                values = [
                    (1.0 - OMEGA) * m + C * (source[at, b, first + 8 : first + 8 + size, :] + n)
                    for b, (m, n) in enumerate(zip(middle, near))
                ]
            for b, value in enumerate(values):
                if scale is not None:
                    value = value * scale
                new[index + (planes[0] + noff), b, first + shift : first + shift + size, :] = value

    if s_planes is None:
        each(planes[1] - planes[0], body, unroll)
        return
    inner = []
    for plane in range(*planes):
        has = tuple(s_planes[0] <= plane + p < s_planes[1] for p in (-1, 0, 1))
        if all(has):
            inner.append(plane)
        else:
            body(plane - planes[0], has)
    if inner:
        first = inner[0] - planes[0]
        each(len(inner), lambda index: body(index + first), unroll)


def restrict(source, soff, v, voff, pairs, rows, summed, store, chunk=8, v_planes=None, s_planes=None, unroll=1):
    count = v.shape[1]
    width = min(2, count)
    half = rows // 2

    def body(index, has_v=(True,) * 4, has_s=(True,) * 2):
        low_v, low_s = 2 * index + (2 * pairs[0] + voff), 2 * index + (2 * pairs[0] + soff)
        for first in range(0, half, chunk):
            size = min(chunk, half - first)

            def at(field, plane, b, offset):
                return field[plane, b, pl.ds(8 + 2 * first + offset, size, stride=2), :]

            def both(field, plane, b):
                return at(field, plane, b, 0) + at(field, plane, b, 1)

            def total_of(terms):
                total = terms[0]
                for term in terms[1:]:
                    total = total + term
                return total

            inside = [p for p in (1, 2) if has_v[p]]
            sums = []
            if inside:
                whole = [total_of([both(v, low_v + p - 1, b) for p in inside]) for b in range(count)]
                near = beside_lanes(whole)
            for b in range(count):
                terms = []
                if inside:
                    terms.append(near[b] - 4.0 * whole[b])
                    terms += [at(v, low_v + p - 1, b, -1) + at(v, low_v + p - 1, b, 2) for p in inside]
                terms += [both(source, low_s + p, b) for p in (0, 1) if has_s[p]]
                terms += [both(v, low_v + p - 1, b) for p in (0, 3) if has_v[p]]
                sums.append(total_of(terms))
            for b in range(count):
                cut = slice(LANES * (b % width), LANES * (b % width + 1))
                summed[index, b // width, first : first + size, cut] = sums[b]

    def finish():
        matrix = pair_matrix(width * LANES)
        for index in range(pairs[1] - pairs[0]):
            for group in range(count // width):
                store(index, group, 0.5 * select_dot(summed[index, group], matrix))

    if v_planes is None:
        each(pairs[1] - pairs[0], body, unroll)
        finish()
        return
    inner = []
    for coarse in range(*pairs):
        has_v = tuple(v_planes[0] <= 2 * coarse + p - 1 < v_planes[1] for p in range(4))
        has_s = tuple(s_planes[0] <= 2 * coarse + p < s_planes[1] for p in range(2))
        if all(has_v + has_s):
            inner.append(coarse)
        else:
            body(coarse - pairs[0], has_v, has_s)
    if inner:
        first = inner[0] - pairs[0]
        each(len(inner), lambda index: body(index + first), unroll)
    finish()


def zero(ref, planes):
    for plane in planes:
        ref[plane] = jnp.zeros(ref.shape[1:], F32)


def zero_rims(ref, planes=None):
    rows = ref.shape[2]
    for plane in range(ref.shape[0]) if planes is None else planes:
        for b in range(ref.shape[1]):
            ref[plane, b, 0:8, :] = jnp.zeros((8, LANES), F32)
            ref[plane, b, rows - 8 : rows, :] = jnp.zeros((8, LANES), F32)


def block_copies(wide, tiled, planes, first, rows, sem, back=False):
    copies = []
    for b in range(tiled.shape[1]):
        pair = (
            wide.at[:, :, pl.ds(LANES * b, LANES)],
            tiled.at[pl.ds(planes[0], planes[1]), b, pl.ds(first, rows), :],
        )
        copies.append(pltpu.make_async_copy(*(pair[::-1] if back else pair), sem))
    return copies


def pack_kernel(
    mask_in, fine, flux, coarse, out, x_first, x_last, z_first, z_last, mask, fine_s, flux_s, sem, edge_sem
):
    patches, fine_z = fine.shape[0], fine.shape[1]
    n0 = fine_z // 2
    blocks = fine_s.shape[0]
    copies = [
        pltpu.make_async_copy(fine.at[:, :, pl.ds(LANES * b, LANES)], fine_s.at[b], sem.at[b])
        for b in range(blocks)
    ]
    copies.append(pltpu.make_async_copy(flux, flux_s, sem.at[blocks]))
    copies.append(pltpu.make_async_copy(mask_in, mask, sem.at[blocks + 1]))
    n, x = coarse.shape[0], coarse.shape[1]
    cuts = [
        pltpu.make_async_copy(coarse.at[pl.ds(n - 2, 2)], z_last, edge_sem.at[0]),
        pltpu.make_async_copy(coarse.at[pl.ds(0, 2)], z_first, edge_sem.at[1]),
        pltpu.make_async_copy(coarse.at[:, pl.ds(x - HX, HX), :], x_last, edge_sem.at[2]),
        pltpu.make_async_copy(coarse.at[:, pl.ds(0, HX), :], x_first, edge_sem.at[3]),
    ]
    for copy in copies + cuts:
        copy.start()
    base = lax.axis_index("box") * patches
    side = (iota((n0, LANES), 1) >> 4) & 3
    source, target = iota((LANES, LANES), 0), iota((LANES, LANES), 1)
    s, i = (source >> 4) & 3, (source & 15) >> 1
    goal = jnp.where(
        s == 0, i + 91, jnp.where(s == 1, i + 1, jnp.where(s == 2, 80 - 10 * i, 89 - 10 * i))
    )
    matrices = [as_matrix(goal == target)]
    for b in range(blocks):
        place = source + LANES * b
        goal = 10 * (8 - (place >> 5)) + ((place & 15) >> 1) + 1
        matrices.append(as_matrix(goal == target))
    for copy in copies:
        copy.wait()
    masked, fine_rows = [], [[] for _ in range(blocks)]
    for patch in range(patches):
        m = [mask[s, base + patch].astype(F32) for s in range(4)]
        factor = jnp.where(side == 0, m[0], jnp.where(side == 1, m[1], jnp.where(side == 2, m[2], m[3])))
        masked.append(
            (flux_s[patch, pl.ds(0, n0, stride=2), :] + flux_s[patch, pl.ds(1, n0, stride=2), :]) * factor
        )
        for b in range(blocks):
            fine_rows[b].append(
                fine_s[b, patch, pl.ds(0, n0, stride=2), :] + fine_s[b, patch, pl.ds(1, n0, stride=2), :]
            )
    total = select_dot(jnp.concatenate(masked, axis=0), matrices[0])
    for b in range(blocks):
        total = total + select_dot(jnp.concatenate(fine_rows[b], axis=0), matrices[b + 1])
    out[...] = 0.125 * total
    for cut in cuts:
        cut.wait()


class Tiles:
    def __init__(self):
        self.lane = iota((16, LANES), 1)
        row = iota((16, LANES), 0)
        self.ring_row = (row >= 3) & (row < 13)
        self.core_row = (row >= 4) & (row < 12)

    def put(self, field, row, column, pairs):
        row = pl.multiple_of(row, 8)
        block, offset = column >> 7, column & (LANES - 1)
        across = self.lane - offset
        ring = self.ring_row & (across >= 3) & (across < 13)
        core = self.core_row & (across >= 4) & (across < 12)
        for plane, line in pairs:
            values = jnp.broadcast_to(line, (8, LANES))
            values = pltpu.roll(values, 0, 1, stride=10, stride_axis=0)
            tile = jnp.concatenate(
                [
                    pltpu.roll(values, (offset + 11) & (LANES - 1), 1),
                    pltpu.roll(values, (offset + 91) & (LANES - 1), 1),
                ],
                axis=0,
            )
            now = field[plane, block, pl.ds(row, 16), :]
            field[plane, block, pl.ds(row, 16), :] = jnp.where(core, 0.0, now) + jnp.where(ring, tile, 0.0)


def listed(table, keeps, found):
    def step(patch, counts):
        owner, x = table[0, patch], table[1, patch]
        for row, count in enumerate(counts):
            found[row, count] = patch
        return tuple(count + jnp.where(keep(owner, x), 1, 0) for keep, count in zip(keeps, counts))

    zeros = (jnp.zeros((), I32),) * len(keeps)
    return lax.fori_loop(0, table.shape[1], step, zeros, unroll=8)


def down_kernel(
    boxes, slabs, n0, x0,
    box_list, coarse, x_low, x_high, packed,
    f_own, v_own, c1, c2, up, down, late_up, late_down,
    fb, vb, g1, v1, summed0, summed1, patches, found, sem, out_sem,
):
    edges = Edges(boxes, slabs)
    rows0, rows1, rows2 = x0 + 2 * HX, x0 // 2 + HX, x0 // 4 + HX // 2
    n1, n2 = n0 // 2, n0 // 4
    copies = (
        block_copies(x_low, fb, (2, n0), 8, HX, sem.at[0])
        + block_copies(coarse, fb, (2, n0), 8 + HX, x0, sem.at[1])
        + block_copies(x_high, fb, (2, n0), 8 + HX + x0, HX, sem.at[2])
    )
    fetch = pltpu.make_async_copy(box_list, patches, sem.at[3])
    fetch.start()
    for copy in copies:
        copy.start()
    fetch.wait()

    def row_of(owner, x):
        return (owner - edges.box) * x0 + x - 4 + HX

    def is_near(owner, x):
        row = row_of(owner, x)
        return (row >= 0) & (row < rows0)

    near_count, own_count = listed(patches, (is_near, lambda owner, x: owner == edges.box), found)
    for copy in copies:
        copy.wait()
    tiles = Tiles()

    def place(index):
        patch = found[0, index]
        lines = [(2 + z, packed[pl.ds(patch * n0 + z, 1), :]) for z in range(n0)]
        tiles.put(fb, row_of(patches[0, patch], patches[1, patch]) + 8, patches[2, patch] - 4, lines)

    lax.fori_loop(0, near_count, lambda index, carry: place(index) or carry, 0)

    inner = pl.ds(8 + HX - HU, x0 + 2 * HU)
    f_copy = pltpu.make_async_copy(fb.at[pl.ds(2, n0), :, inner, :], f_own, out_sem.at[0])
    f_copy.start()

    relax(vb, 3, (-1, n0 + 1), fb, 2, rows0, HX, edges, n0, s_planes=(0, n0), unroll=3)
    v_copy = pltpu.make_async_copy(vb.at[pl.ds(4, n0 - 2), :, inner, :], v_own, out_sem.at[1])
    v_copy.start()

    h1 = HX // 2

    def store1(index, group, value):
        value = value * edges.planes(index - 1, n1)
        g1[index + 3, group, 8 : 8 + h1, :] = value[:h1] * edges.low()
        g1[index + 3, group, 8 + h1 : 8 + rows1 - h1, :] = value[h1 : rows1 - h1]
        g1[index + 3, group, 8 + rows1 - h1 : 8 + rows1, :] = value[rows1 - h1 :] * edges.high()

    restrict(fb, 2, vb, 3, (-1, n1 + 1), rows0, summed0, store1, v_planes=(-1, n0 + 1), s_planes=(0, n0))
    for plane in range(n1 + 2):
        for b in range(g1.shape[1]):
            c1[plane, b] = g1[plane + 3, b, 8 + h1 - HU : 8 + rows1 - h1 + HU, :]

    relax(v1, 5, (-2, n1 + 2), g1, 4, rows1, h1, edges, n1, s_planes=(-1, n1 + 1), unroll=2)

    h2 = HX // 4

    def store2(index, group, value):
        c2[index, group, 0:h2, :] = value[:h2] * edges.low()
        c2[index, group, h2 : rows2 - h2, :] = value[h2 : rows2 - h2]
        c2[index, group, rows2 - h2 : rows2, :] = value[rows2 - h2 :] * edges.high()

    restrict(g1, 4, v1, 5, (-2, n2 + 2), rows1, summed1, store2, v_planes=(-2, n1 + 2), s_planes=(-1, n1 + 1))

    near = c1.shape[2] - HU
    for target, fine_plane, coarse_first in ((up, n1 + 1, n2 + 2), (down, 0, 0)):
        target[0:rows2] = c2[coarse_first, 0]
        target[rows2 : 2 * rows2] = c2[coarse_first + 1, 0]
        for b in range(c1.shape[1]):
            first = target.shape[0] - near * (c1.shape[1] - b)
            target[first : first + near] = c1[fine_plane, b, HU // 2 : HU // 2 + near, :]
    rim = 2 * rows2
    slots = (up.shape[0] - rim - near * c1.shape[1]) // 2 - 8 * fb.shape[1]
    wide = late_up.shape[0] // fb.shape[1]
    for b in range(fb.shape[1]):
        at = slice(4 + HX, 4 + HX + wide)
        late_up[wide * b : wide * (b + 1)] = fb[n0 - 1, b, at, :]
        late_down[wide * b : wide * (b + 1)] = fb[4, b, at, :]
        for z in range(2):
            first = rim + 8 * (fb.shape[1] * z + b)
            for target, plane in ((up, n0 + z), (down, 2 + z)):
                target[first : first + 3, :] = fb[plane, b, 8 + HX - 3 : 8 + HX, :]
                target[first + 3 : first + 6, :] = fb[plane, b, 8 + HX + x0 : 8 + HX + x0 + 3, :]
                target[first + 6 : first + 8, :] = jnp.zeros((2, LANES), F32)
    rim = rim + 16 * fb.shape[1]
    up[rim : rim + 2 * slots, :] = jnp.zeros((2 * slots, LANES), F32)
    down[rim : rim + 2 * slots, :] = jnp.zeros((2 * slots, LANES), F32)

    def keep(slot):
        patch = found[1, slot]
        for z in range(2):
            up[pl.ds(rim + z * slots + slot, 1), :] = packed[pl.ds(patch * n0 + n0 - 2 + z, 1), :]
            down[pl.ds(rim + z * slots + slot, 1), :] = packed[pl.ds(patch * n0 + z, 1), :]

    lax.fori_loop(0, own_count, lambda index, carry: keep(index) or carry, 0)
    f_copy.wait()
    v_copy.wait()


def total_kernel(c2, below, above, copies):
    n2, rows2 = c2.shape[0] - 4, c2.shape[2]
    for plane in range(n2):
        value = c2[2 + plane, 0]
        if plane < 2:
            value = value + below[plane * rows2 : (plane + 1) * rows2]
        if plane >= n2 - 2:
            first = (plane - (n2 - 2)) * rows2
            value = value + above[first : first + rows2]
        for slab in range(copies.shape[0]):
            copies[slab, plane * rows2 : (plane + 1) * rows2] = value


def join_kernel(c1, below, above, s1, up, down):
    n1, r1 = s1.shape[0], c1.shape[2]
    for plane in range(n1):
        s1[plane] = c1[1 + plane]
    near = r1 - HU
    cells = slice(HU // 2, HU // 2 + near)
    for b in range(s1.shape[1]):
        first = below.shape[0] - near * (s1.shape[1] - b)
        s1[0, b, cells, :] = s1[0, b, cells, :] + below[first : first + near]
        s1[n1 - 1, b, cells, :] = s1[n1 - 1, b, cells, :] + above[first : first + near]
    for p in range(4):
        for b in range(s1.shape[1]):
            first = near * (p * s1.shape[1] + b)
            up[first : first + near] = s1[n1 - 4 + p, b, HU // 2 : HU // 2 + near, :]
            down[first : first + near] = s1[p, b, HU // 2 : HU // 2 + near, :]


def third_kernel(boxes, slabs, s2, s3, fb, vb, summed):
    edges = Edges(boxes, slabs)
    planes, rows = s2.shape[0], s2.shape[1]
    zero(fb, (0, planes + 1))
    zero(vb, (0, planes + 1))
    for plane in range(planes):
        fb[plane + 1, 0, 8 : 8 + rows, :] = s2[plane]
    relax(vb, 1, (0, planes), fb, 1, rows, HX // 4, edges, None, chunk=32, unroll=4)
    quarter = planes // 4
    h3 = HX // 8
    own = rows // 2 - 2 * h3
    lanes = LANES // 2

    for part in range(2):

        def store(index, group, value, part=part):
            s3[index, :, lanes * part : lanes * (part + 1)] = value[h3 : h3 + own]

        restrict(fb, 1, vb, 1, (quarter * part, quarter * (part + 1)), rows, summed, store, unroll=quarter)


def middle_kernel(
    boxes, slabs,
    s3, s2,
    e2p,
    sc, va3, vb3, e3p, f2, v2a, v2b,
):
    edges = Edges(boxes, slabs)
    slab = edges.slab
    half, rows3 = sc.shape[0], sc.shape[2] - 16
    own3 = s3.shape[2]
    zero_rims(va3)
    zero_rims(vb3)
    for box in range(boxes):
        for plane in range(half):
            value = s3[box, plane]
            sc[plane, 0, 8 + box * own3 : 8 + (box + 1) * own3, :] = value
            va3[plane, 0, 8 + box * own3 : 8 + (box + 1) * own3, :] = C * value

    def coarsest(old, new):
        chunk = 16
        lane = iota((chunk, LANES), 1)
        for row in range(0, rows3, chunk):
            inner = slice(row + 8, row + 8 + chunk)
            for plane in range(half):
                middle = old[plane, 0, inner, :]
                before = jnp.where((lane & 63) == 0, 0.0, pltpu.roll(middle, 1, 1))
                after = jnp.where((lane & 63) == 63, 0.0, pltpu.roll(middle, LANES - 1, 1))
                if plane > 0:
                    lower = old[plane - 1, 0, inner, :]
                else:
                    lower = jnp.where(lane < 64, 0.0, pltpu.roll(old[half - 1, 0, inner, :], 64, 1))
                if plane < half - 1:
                    upper = old[plane + 1, 0, inner, :]
                else:
                    upper = jnp.where(lane < 64, pltpu.roll(old[0, 0, inner, :], 64, 1), 0.0)
                beside = old[plane, 0, row + 7 : row + 7 + chunk, :] + old[plane, 0, row + 9 : row + 9 + chunk, :]
                near = beside + ((before + after) + (lower + upper))
                new[plane, 0, inner, :] = (1.0 - OMEGA) * middle + C * (sc[plane, 0, inner, :] + near)

    def double(index):
        coarsest(va3, vb3)
        coarsest(vb3, va3)

    each((CSWEEPS - 1) // 2, double)
    coarsest(va3, vb3)

    n2, rows2 = s2.shape[0] // slabs, s2.shape[1]
    n3 = n2 // 2
    shape = (LANES, LANES)
    copy_low = (iota(shape, 0) == (iota(shape, 1) >> 1)).astype(F32)
    copy_high = (iota(shape, 0) == (iota(shape, 1) >> 1) + 64).astype(F32)
    total3 = 2 * half
    h3 = HX // 8
    window = pl.multiple_of(edges.box * own3, 8)
    for k in range(-2, n3 + 2):
        plane = slab * n3 + k
        inside = (plane >= 0) & (plane < total3)
        safe = jnp.clip(plane, 0, total3 - 1)
        upper = safe >= half
        matrix = jnp.where(upper, copy_high, copy_low) * jnp.where(inside, 1.0, 0.0)
        value = vb3[jnp.where(upper, safe - half, safe), 0, pl.ds(window, own3 + 16), :]
        value = select_dot(value, matrix.astype(BF16))[8 - h3 : 8 + own3 + h3]
        e3p[k + 2, pl.ds(0, own3 + 2 * h3, stride=2), :] = value
        e3p[k + 2, pl.ds(1, own3 + 2 * h3, stride=2), :] = value

    planes2 = s2.shape[0]
    for p in range(-5, n2 + 5):
        plane = slab * n2 + p
        inside = jnp.where((plane >= 0) & (plane < planes2), 1.0, 0.0)
        f2[p + 5, 0, 8 : 8 + rows2, :] = s2[jnp.clip(plane, 0, planes2 - 1)] * inside

    def extra2(index, b, first, size):
        return e3p[index >> 1, first : first + size, :]

    h2 = HX // 4
    relax(v2a, 5, (-4, n2 + 4), f2, 5, rows2, h2, edges, n2, extra=extra2, chunk=32, unroll=5)
    relax(v2b, 5, (-3, n2 + 3), f2, 5, rows2, h2, edges, n2, old=v2a, ooff=5, chunk=32, unroll=4)
    relax(v2a, 5, (-2, n2 + 2), f2, 5, rows2, h2, edges, n2, old=v2b, ooff=5, chunk=32, unroll=3)

    cut = h2 - HU // 2
    matrix2 = copy_matrix(LANES)
    for k in range(-2, n2 + 2):
        value = select_dot(v2a[k + 5, 0, 8 + cut : 8 + rows2 - cut, :], matrix2)
        for b in range(2):
            part = value[:, LANES * b : LANES * (b + 1)]
            e2p[k + 2, b, pl.ds(0, rows2 - 2 * cut, stride=2), :] = part
            e2p[k + 2, b, pl.ds(1, rows2 - 2 * cut, stride=2), :] = part


def first_level(edges, s1, below, above, e2p, e1, f1, v1a, v1b):
    n1, rows1 = s1.shape[0], s1.shape[2]
    near = rows1 - HU
    inner = slice(8 + HU // 2, 8 + HU // 2 + near)
    for b in range(f1.shape[1]):
        for p in range(4):
            first = near * (p * f1.shape[1] + b)
            for plane, message in ((p, below), (4 + n1 + p, above)):
                f1[plane, b, inner, :] = message[first : first + near]
        for p in range(n1):
            f1[4 + p, b, 8 : 8 + rows1, :] = s1[p, b]

    def extra1(index, b, first, size):
        return e2p[(index + 1) >> 1, b, first : first + size, :]

    relax(v1a, 4, (-3, n1 + 3), f1, 4, rows1, HU, edges, n1, extra=extra1, unroll=5)
    relax(v1b, 4, (-2, n1 + 2), f1, 4, rows1, HU, edges, n1, old=v1a, ooff=4, unroll=4)
    relax(e1, 1, (-1, n1 + 1), f1, 4, rows1, HU, edges, n1, old=v1b, ooff=4, shift=0, unroll=3)


def early_kernel(
    boxes, slabs, n0, x0, rim,
    box_list, f_own, z_below, z_above, below, above,
    f_rim, v_rim,
    fb, va, patches, found, sem, out_sem,
):
    edges = Edges(boxes, slabs)
    rows = x0 + 2 * HU
    fetch = pltpu.make_async_copy(box_list, patches, sem.at[4])
    copies = (
        [
            pltpu.make_async_copy(f_own.at[pl.ds(0, 2)], fb.at[pl.ds(2, 2), :, pl.ds(8, rows), :], sem.at[0]),
            pltpu.make_async_copy(f_own.at[pl.ds(n0 - 2, 2)], fb.at[pl.ds(4, 2), :, pl.ds(8, rows), :], sem.at[3]),
        ]
        + block_copies(z_below, fb, (0, 2), 8 + HU, x0, sem.at[1])
        + block_copies(z_above, fb, (6, 2), 8 + HU, x0, sem.at[2])
    )
    fetch.start()
    for copy in copies:
        copy.start()
    fetch.wait()

    (count,) = listed(patches, (lambda owner, x: owner == edges.box,), found)
    packed = rim + 16 * fb.shape[1]
    slots = boxes * max(2, patches.shape[1] // boxes // 4)
    for copy in copies:
        copy.wait()
    for z in range(2):
        for b in range(fb.shape[1]):
            at = rim + 8 * (fb.shape[1] * z + b)
            for plane, message in ((z, below), (6 + z, above)):
                fb[plane, b, 5 + HU : 8 + HU, :] = message[at : at + 3]
                fb[plane, b, 8 + HU + x0 : 11 + HU + x0, :] = message[at + 3 : at + 6]
    tiles = Tiles()

    def place(slot):
        lines = [(z, below, z) for z in range(2)] + [(6 + z, above, z) for z in range(2)]
        lines = [(plane, message[pl.ds(packed + z * slots + slot, 1), :]) for plane, message, z in lines]
        patch = found[0, slot]
        tiles.put(fb, patches[1, patch] - 4 + HU + 8, patches[2, patch] - 4, lines)

    lax.fori_loop(0, count, lambda index, carry: place(index) or carry, 0)
    outs = [
        pltpu.make_async_copy(fb.at[pl.ds(1, 1)], f_rim.at[pl.ds(0, 1)], out_sem.at[0]),
        pltpu.make_async_copy(fb.at[pl.ds(6, 1)], f_rim.at[pl.ds(1, 1)], out_sem.at[1]),
        pltpu.make_async_copy(va.at[pl.ds(0, 3)], v_rim.at[pl.ds(0, 3)], out_sem.at[2]),
        pltpu.make_async_copy(va.at[pl.ds(3, 3)], v_rim.at[pl.ds(3, 3)], out_sem.at[3]),
    ]
    outs[0].start()
    outs[1].start()
    relax(va, 2, (-2, 1), fb, 2, rows, HU, edges, n0, s_planes=(-2, n0), unroll=2)
    outs[2].start()
    relax(va, 4 - n0, (n0 - 1, n0 + 2), fb, 6 - n0, rows, HU, edges, n0, s_planes=(0, n0 + 2), unroll=2)
    outs[3].start()
    for out in outs:
        out.wait()


def tail_kernel(
    boxes, slabs, n0, x0,
    e2p, s1, below, above, late_below, late_above, f_own, f_rim, v_own, v_rim,
    out,
    f1, v1a, v1b, e1,
    fb, va, vb, ob, sem, out_sem,
):
    inner = pl.ds(8, x0 + 2 * HU)
    copies = [
        pltpu.make_async_copy(v_own, va.at[pl.ds(4, n0 - 2), :, inner, :], sem.at[0]),
        pltpu.make_async_copy(v_rim.at[pl.ds(0, 3)], va.at[pl.ds(1, 3)], sem.at[1]),
        pltpu.make_async_copy(v_rim.at[pl.ds(3, 3)], va.at[pl.ds(n0 + 2, 3)], sem.at[2]),
        pltpu.make_async_copy(f_own, fb.at[pl.ds(1, n0), :, inner, :], sem.at[3]),
        pltpu.make_async_copy(f_rim.at[pl.ds(0, 1)], fb.at[pl.ds(0, 1)], sem.at[4]),
        pltpu.make_async_copy(f_rim.at[pl.ds(1, 1)], fb.at[pl.ds(n0 + 1, 1)], sem.at[5]),
    ]
    for copy in copies:
        copy.start()
    edges = Edges(boxes, slabs)
    first_level(edges, s1, below, above, e2p, e1, f1, v1a, v1b)
    for copy in copies:
        copy.wait()
    rows = x0 + 2 * HU
    matrix = copy_matrix(LANES)
    cut = HU // 2
    r1 = e1.shape[2]
    size1 = r1 - 2 * cut
    wide = late_below.shape[0] // fb.shape[1]
    for b in range(fb.shape[1]):
        at = slice(4 + HU, 4 + HU + wide)
        for plane, message in ((1, late_below), (4 + n0, late_above)):
            first = wide * b
            va[plane, b, at, :] = va[plane, b, at, :] + (C * C) * message[first : first + wide]

    def prolong(k):
        for group in range(e1.shape[1]):
            value = select_dot(e1[k, group, cut : r1 - cut, :], matrix)
            for b in range(2):
                part = value[:, LANES * b : LANES * (b + 1)]
                for plane in (2 * k + 1, 2 * k + 2):
                    for start in (8, 9):
                        at = pl.ds(start, size1, stride=2)
                        va[plane, 2 * group + b, at, :] = va[plane, 2 * group + b, at, :] + part

    each(e1.shape[0], prolong, unroll=3)
    relax(vb, 3, (-1, n0 + 1), fb, 1, rows, HU, edges, n0, old=va, ooff=3, unroll=5)

    def last(z):
        view = ob.at[pl.ds(z, 1)]
        relax(view, 0, (0, 1), fb.at[pl.ds(z + 1, 1)], 0, rows, HU, edges, None, old=vb.at[pl.ds(z + 2, 3)], ooff=1, shift=-HU, cut=1)
        for copy in block_copies(out.at[pl.ds(z, 1)], ob, (z, 1), 0, x0, out_sem, back=True):
            copy.start()

    each(n0, last, unroll=4)
    for copy in block_copies(out, ob, (0, n0), 0, x0, out_sem, back=True):
        copy.wait()


def shape_of(*dims):
    return jax.ShapeDtypeStruct(dims, F32)


def scratch(*dims):
    return pltpu.VMEM(dims, F32)


def in_hbm(array):
    return pltpu.with_memory_space_constraint(array, pltpu.MemorySpace.HBM)


def limit(mebibytes):
    return pltpu.CompilerParams(vmem_limit_bytes=mebibytes << 20)


def cost(flops, moved):
    return pl.CostEstimate(flops=flops, bytes_accessed=moved, transcendentals=0)


def shift_by(array, axis, step):
    size = lax.axis_size(axis)
    pairs = [(i, i + step) for i in range(size) if 0 <= i + step < size]
    return lax.ppermute(array, axis, pairs)


def per_device(coarse, fine_div, reflux, box_list, cf_mask):
    boxes, slabs = lax.axis_size("box"), lax.axis_size("gz")
    n0, x0, y0 = coarse.shape
    n1, n2 = n0 // 2, n0 // 4
    b0, b1 = y0 // LANES, y0 // LANES // 2
    patches, fine_z, fine_lanes = fine_div.shape
    rows0, rows1, rows2 = x0 + 2 * HX, x0 // 2 + HX, x0 // 4 + HX // 2
    up_rows0, up_rows1 = x0 + 2 * HU, x0 // 2 + 2 * HU
    dma = pltpu.SemaphoreType.DMA
    hbm = pltpu.MemorySpace.HBM
    table = pltpu.SMEM((3, box_list.shape[0]), I32)

    fine_blocks = fine_lanes // LANES
    packed, x_first, x_last, z_first, z_last = pl.pallas_call(
        pack_kernel,
        name="pack",
        out_shape=(
            shape_of(patches * n0, LANES),
            shape_of(n0, HX, y0),
            shape_of(n0, HX, y0),
            shape_of(2, x0, y0),
            shape_of(2, x0, y0),
        ),
        in_specs=[HBM] * 4,
        out_specs=(VM,) * 5,
        scratch_shapes=[
            pltpu.SMEM(cf_mask.shape[::-1], I32),
            scratch(fine_blocks, patches, fine_z, LANES),
            scratch(patches, fine_z, LANES),
            dma((fine_blocks + 2,)),
            dma((4,)),
        ],
        compiler_params=limit(4),
        cost_estimate=cost(10**7, 10**6),
    )(in_hbm(cf_mask.T), in_hbm(fine_div), in_hbm(reflux), in_hbm(coarse))
    z_below = shift_by(z_last, "gz", 1)
    z_above = shift_by(z_first, "gz", -1)
    x_low = shift_by(x_last, "box", 1)
    x_high = shift_by(x_first, "box", -1)
    packed = lax.all_gather(packed, "box", axis=0, tiled=True)

    slots = boxes * max(2, patches // 4)
    rim = 2 * rows2
    message = rim + 2 * (8 * b0 + slots) + b1 * (up_rows1 - HU)
    f_own, v_own, c1, c2, up, down, late_up, late_down = pl.pallas_call(
        functools.partial(down_kernel, boxes, slabs, n0, x0),
        name="down",
        out_shape=(
            hbm((n0, b0, up_rows0, LANES), F32),
            hbm((n0 - 2, b0, up_rows0, LANES), F32),
            shape_of(n1 + 2, b1, up_rows1, LANES),
            shape_of(n2 + 4, 1, rows2, LANES),
            shape_of(message, LANES),
            shape_of(message, LANES),
            shape_of(b0 * (x0 + HU), LANES),
            shape_of(b0 * (x0 + HU), LANES),
        ),
        in_specs=[HBM] * 4 + [VM],
        out_specs=(HBM,) * 2 + (VM,) * 6,
        scratch_shapes=[
            scratch(n0 + 4, b0, rows0 + 16, LANES),
            scratch(n0 + 6, b0, rows0 + 16, LANES),
            scratch(n1 + 8, b1, rows1 + 16, LANES),
            scratch(n1 + 10, b1, rows1 + 16, LANES),
            scratch(n1 + 2, b0 // 2, rows1, 2 * LANES),
            scratch(n2 + 4, max(1, b1 // 2), rows2, min(2, b1) * LANES),
            table,
            table,
            dma((4,)),
            dma((2,)),
        ],
        compiler_params=limit(20),
        cost_estimate=cost(3 * 10**7, 10**7),
    )(in_hbm(box_list.T), in_hbm(coarse), x_low, x_high, packed)

    from_below = shift_by(up, "gz", 1)
    from_above = shift_by(down, "gz", -1)
    late_below = shift_by(late_up, "gz", 1)
    late_above = shift_by(late_down, "gz", -1)
    copies = pl.pallas_call(
        total_kernel,
        name="total",
        out_shape=shape_of(slabs, n2 * rows2, LANES),
        in_specs=[VM] * 3,
        out_specs=VM,
        compiler_params=limit(3),
        cost_estimate=cost(10**6, 10**6),
    )(c2, from_below, from_above)
    s2 = lax.all_to_all(copies, "gz", split_axis=0, concat_axis=0, tiled=True)
    s2 = s2.reshape(slabs * n2, rows2, LANES)
    last = 4 * b1 * (up_rows1 - HU)
    s1, up, down = pl.pallas_call(
        join_kernel,
        name="join",
        out_shape=(shape_of(n1, b1, up_rows1, LANES), shape_of(last, LANES), shape_of(last, LANES)),
        in_specs=[VM] * 3,
        out_specs=(VM,) * 3,
        compiler_params=limit(5),
        cost_estimate=cost(10**6, 10**6),
    )(c1, from_below, from_above)
    below = shift_by(up, "gz", 1)
    above = shift_by(down, "gz", -1)

    up_wide = up_rows0 + 16
    f_rim, v_rim = pl.pallas_call(
        functools.partial(early_kernel, boxes, slabs, n0, x0, rim),
        name="early",
        out_shape=(hbm((2, b0, up_wide, LANES), F32), hbm((6, b0, up_wide, LANES), F32)),
        in_specs=[HBM, HBM, HBM, HBM, VM, VM],
        out_specs=(HBM, HBM),
        scratch_shapes=[
            scratch(8, b0, up_wide, LANES),
            scratch(6, b0, up_wide, LANES),
            table,
            table,
            dma((5,)),
            dma((4,)),
        ],
        compiler_params=limit(10),
        cost_estimate=cost(2 * 10**7, 10**7),
    )(in_hbm(box_list.T), in_hbm(f_own), in_hbm(z_below), in_hbm(z_above), from_below, from_above)

    planes2, half = slabs * n2, slabs * n2 // 4
    own3 = x0 // 8
    s3 = pl.pallas_call(
        functools.partial(third_kernel, boxes, slabs),
        name="third",
        out_shape=shape_of(half, own3, LANES),
        in_specs=[VM],
        out_specs=VM,
        scratch_shapes=[scratch(planes2 + 2, 1, rows2 + 16, LANES)] * 2 + [scratch(half, 1, rows2 // 2, LANES)],
        compiler_params=limit(4),
        cost_estimate=cost(10**6, 10**6),
    )(s2)
    s3 = lax.all_gather(s3, "box", axis=0)
    rows3 = boxes * own3
    e2p = pl.pallas_call(
        functools.partial(middle_kernel, boxes, slabs),
        name="middle",
        out_shape=shape_of(n2 + 4, 2, up_rows1, LANES),
        in_specs=[VM] * 2,
        out_specs=VM,
        scratch_shapes=[scratch(half, 1, rows3 + 16, LANES)] * 3
        + [scratch(n2 // 2 + 4, rows2, LANES)]
        + [scratch(n2 + 10, 1, rows2 + 16, LANES)] * 3,
        compiler_params=limit(8),
        cost_estimate=cost(10**7, 2 * 10**6),
    )(s3, s2)
    return pl.pallas_call(
        functools.partial(tail_kernel, boxes, slabs, n0, x0),
        name="tail",
        out_shape=shape_of(n0, x0, y0),
        in_specs=[VM] * 6 + [HBM] * 4,
        out_specs=HBM,
        scratch_shapes=[scratch(n1 + 8, b1, up_rows1 + 16, LANES)] * 3
        + [scratch(n1 + 2, b1, up_rows1, LANES)]
        + [scratch(n0 + 2, b0, up_rows0 + 16, LANES)]
        + [scratch(n0 + 6, b0, up_rows0 + 16, LANES)] * 2
        + [scratch(n0, b0, x0, LANES), dma((6,)), dma(())],
        compiler_params=limit(24),
        cost_estimate=cost(4 * 10**7, 10**7),
    )(e2p, s1, below, above, late_below, late_above, in_hbm(f_own), in_hbm(f_rim), in_hbm(v_own), in_hbm(v_rim))


def solution(mesh):
    return jax.shard_map(
        per_device,
        mesh=mesh,
        in_specs=(P("gz", "box", None), P("box", "gz", None), P("box", "gz", None), P(), P()),
        out_specs=P("gz", "box", None),
        check_vma=False,
    )
```
